256 devices in a mesh: req: 32 (over y, x, core), head: 8 (over z).
Axes of the slice: x: 4, y: 4, z: 8, core: 2. Of those that a mesh axis runs over, the one named last changes fastest.
Arguments:
- queries: bfloat16 [1024, 16384], P(('req', 'head')), may hold values from -15 to 15
- cache_keys: bfloat16 [8, 32768, 1024], P(None, 'req', 'head'), may hold values from -6 to 6
- cache_values: bfloat16 [8, 32768, 1024], P(None, 'req', 'head'), may hold values from -6 to 6
- tree_keys: bfloat16 [1024, 1024], P('req', 'head'), may hold values from -10 to 10
- tree_values: bfloat16 [1024, 1024], P('req', 'head'), may hold values from -6 to 6
- parents: int32 [8, 128], replicated, may hold values from -1 to 126, as said below
- tree_sizes: int32 [8], replicated, may hold values from 16 to 128
- cache_lens: int32 [8], replicated, may hold values from 2 to 32768
Outputs:
- attended: bfloat16 [1024, 16384], P('req', 'head')
The draws below stay inside these ranges and needn't reach their ends.
Inputs may be any that keep to these rules, and one draw needn't show every extreme that they name: parents[a, 0] = -1 (the root); for node i >= 1, parents[a, i] is a node of 0 to i - 1.
All inputs are finite; a program needn't handle non-finite values.
Results may differ from the reference program's by a relative error of at most 0.003.
Values may be sent and summed in bfloat16 or wider, within the bound.
A program may use at most 128 MiB of HBM per device.

```python
import math
import jax
import jax.numpy as jnp
from jax import lax

NH = 128
KVH = 8
HD = 128
TMAX = 128
REQS = 8
CTX = 32768
ROWS = 1024
N_REQ = 32


def draw_queries(key, part):
    shape = (REQS * TMAX, NH * HD)
    own_key = jax.random.fold_in(key, 11)
    values = 2.5 * jax.random.truncated_normal(own_key, -6.0, 6.0, shape, jnp.float32)
    return values.astype(jnp.bfloat16)


def draw_cache_keys(key, part):
    shape = (REQS, CTX, KVH * HD)
    own_key = jax.random.fold_in(key, 12)
    values = jax.random.truncated_normal(own_key, -6.0, 6.0, shape, jnp.float32)
    return values.astype(jnp.bfloat16)


def draw_parents(key, part):
    node_ids = jnp.arange(TMAX, dtype=jnp.int32)
    jumps = jax.random.randint(jax.random.fold_in(key, 13), (REQS, TMAX), 0, 4, dtype=jnp.int32)
    jumps = jnp.where(node_ids[None, :] == TMAX - 1, 0, jumps)
    reach_back = jnp.minimum(jumps, jnp.maximum(node_ids - 1, 0)[None, :])
    picked = node_ids[None, :] - 1 - reach_back
    return jnp.where(node_ids[None, :] == 0, -1, picked).astype(jnp.int32)


def place_ends(drawn, key, smallest, top_value):
    dims = drawn.shape
    index_at = [jax.random.randint(jax.random.fold_in(key, axis), (), 0, dims[axis]) for axis in range(len(dims))]
    drawn = drawn.at[tuple(index_at)].set(smallest)
    longest = dims.index(max(dims))
    index_at[longest] = (index_at[longest] + 1) % dims[longest]
    return drawn.at[tuple(index_at)].set(top_value)


def steps_of(rng, extent, shards, smallest, top_value):
    level = 1.0
    for axis_at, parts in shards:
        steps = jax.random.uniform(jax.random.fold_in(jax.random.fold_in(rng, 6), axis_at), (parts,), jnp.float32, smallest / len(shards), top_value / len(shards))
        level = level * jnp.repeat(jnp.exp(steps), extent[axis_at] // parts).reshape((-1,) + (1,) * (len(extent) - 1 - axis_at))
    return level


def normal_values(rng, extent, deviation, reach, pieces=(), kind=jnp.bfloat16):
    values = deviation * jax.random.normal(rng, extent, jnp.float32)
    if pieces:
        values = values * steps_of(rng, extent, pieces, -0.22, 0.18)
    return jnp.clip(values, -reach, reach).astype(kind)


def setup_inputs(seed: int = 0) -> dict:
    seeds = jax.random.split(jax.random.key(seed), 9)
    return {
        "queries": draw_queries(jax.random.fold_in(seeds[8], 71), 0),
        "cache_keys": draw_cache_keys(jax.random.fold_in(seeds[8], 71), 0),
        "cache_values": normal_values(seeds[2], (REQS, CTX, KVH * HD), 1.0, 6.0, ((1, 32), (2, 8))),
        "tree_keys": normal_values(seeds[3], (ROWS, KVH * HD), 1.7, 10.0, ((0, 32), (1, 8))),
        "tree_values": normal_values(seeds[4], (ROWS, KVH * HD), 1.0, 6.0, ((0, 32), (1, 8))),
        "parents": draw_parents(jax.random.fold_in(seeds[8], 71), 0),
        "tree_sizes": place_ends(jax.random.randint(seeds[6], (REQS,), 16, TMAX + 1), jax.random.fold_in(seeds[6], 1), 16, TMAX).astype(jnp.int32),
        "cache_lens": place_ends(jax.random.randint(seeds[7], (REQS,), 2, CTX + 1), jax.random.fold_in(seeds[7], 1), 2, CTX).astype(jnp.int32),
    }


negative_fill = -1e+30

def ancestry(parents):
    node_ids = jnp.arange(TMAX, dtype=jnp.int32)
    linked = jnp.logical_or(parents[:, :, None] == node_ids[None, None, :], node_ids[:, None] == node_ids[None, :])
    reached = linked.astype(jnp.float32)
    for doubling in range((TMAX - 1).bit_length()):
        squared = jnp.einsum('aij,ajk->aik', reached, reached, precision=lax.Precision.HIGHEST)
        reached = jnp.minimum(squared, 1.0)
    return reached

def reference(queries, cache_keys, cache_values, tree_keys, tree_values, parents, tree_sizes, cache_lens):
    group_size = NH // KVH
    softmax_scale = 1.0 / math.sqrt(HD)
    cache_block = CTX // N_REQ
    rows_owned = REQS * TMAX // N_REQ
    reached = ancestry(parents)
    owners = jnp.arange(N_REQ, dtype=jnp.int32)
    node_ids = jnp.arange(TMAX, dtype=jnp.int32)
    positions = jnp.arange(CTX, dtype=jnp.int32).reshape(N_REQ, cache_block)

    def one_request(request):
        start = request * TMAX
        query_block = lax.dynamic_slice_in_dim(queries, start, TMAX, 0).astype(jnp.float32)
        query_block = query_block.reshape(TMAX, KVH, group_size, HD).transpose(1, 0, 2, 3)
        block_keys = lax.dynamic_index_in_dim(cache_keys, request, 0, keepdims=False).astype(jnp.float32)
        block_keys = block_keys.reshape(N_REQ, cache_block, KVH, HD).transpose(2, 0, 1, 3)
        block_values = lax.dynamic_index_in_dim(cache_values, request, 0, keepdims=False).astype(jnp.float32)
        block_values = block_values.reshape(N_REQ, cache_block, KVH, HD).transpose(2, 0, 1, 3)
        node_keys = lax.dynamic_slice_in_dim(tree_keys, start, TMAX, 0).astype(jnp.float32)
        node_keys = node_keys.reshape(TMAX, KVH, HD).transpose(1, 0, 2)
        node_values = lax.dynamic_slice_in_dim(tree_values, start, TMAX, 0).astype(jnp.float32)
        node_values = node_values.reshape(TMAX, KVH, HD).transpose(1, 0, 2)
        length = lax.dynamic_index_in_dim(cache_lens, request, 0, keepdims=False)
        live_cache = positions < length
        live_tree = lax.dynamic_index_in_dim(reached, request, 0, keepdims=False) > 0.5
        member = ((start + node_ids) // rows_owned)[:, None] == owners[None, :]

        def one_head(operands):
            head_queries, head_keys, head_values, head_nodes, head_node_values = operands
            cache_scores = jnp.einsum('iqd,jpd->iqjp', head_queries, head_keys, precision=lax.Precision.HIGHEST) * softmax_scale
            cache_scores = jnp.where(live_cache[None, None], cache_scores, negative_fill)
            tree_scores = jnp.einsum('iqd,kd->iqk', head_queries, head_nodes, precision=lax.Precision.HIGHEST) * softmax_scale
            tree_scores = jnp.where(live_tree[:, None, :], tree_scores, negative_fill)
            grouped = jnp.where(member[None, None], tree_scores[..., None], negative_fill)
            peaks = jnp.maximum(lax.optimization_barrier(jnp.max(cache_scores, axis=3)), lax.optimization_barrier(jnp.max(grouped, axis=2)))
            cache_weights = jnp.where(live_cache[None, None], jnp.exp(cache_scores - peaks[..., None]), 0.0)
            tree_live = jnp.logical_and(live_tree[:, None, :, None], member[None, None])
            tree_weights = jnp.where(tree_live, jnp.exp(grouped - peaks[:, :, None, :]), 0.0)
            totals = lax.optimization_barrier(jnp.sum(cache_weights, axis=3)) + lax.optimization_barrier(jnp.sum(tree_weights, axis=2))
            cache_rounded = lax.optimization_barrier(cache_weights.astype(jnp.bfloat16)).astype(jnp.float32)
            tree_rounded = lax.optimization_barrier(tree_weights.astype(jnp.bfloat16)).astype(jnp.float32)
            group_sums = jnp.einsum('iqjp,jpd->iqjd', cache_rounded, head_values, precision=lax.Precision.HIGHEST)
            group_sums = group_sums + jnp.einsum('iqkj,kd->iqjd', tree_rounded, head_node_values, precision=lax.Precision.HIGHEST)
            floored = jnp.maximum(totals, 1.0)
            partials = group_sums / floored[..., None]
            log_totals = peaks + jnp.log(floored)
            highest = lax.optimization_barrier(jnp.max(log_totals, axis=2))
            weights = jnp.exp(log_totals - highest[..., None])
            return lax.optimization_barrier(jnp.sum(weights[..., None] * partials, axis=2)) / lax.optimization_barrier(jnp.sum(weights, axis=2))[..., None]
        merged = lax.map(one_head, (query_block, block_keys, block_values, node_keys, node_values))
        merged = merged.transpose(1, 0, 2, 3).reshape(TMAX, NH * HD)
        live_size = lax.dynamic_index_in_dim(tree_sizes, request, 0, keepdims=False)
        return jnp.where((node_ids < live_size)[:, None], merged, 0.0).astype(jnp.bfloat16)
    attended = lax.map(one_request, jnp.arange(REQS, dtype=jnp.int32))
    return attended.reshape(REQS * TMAX, NH * HD)
```

```python
import math

import jax
import jax.numpy as jnp
from jax import lax
from jax.sharding import Mesh
from jax.sharding import PartitionSpec as P

NH = 128
KVH = 8
HD = 128


negative_fill = -1e30


def ancestry(parents):
    node_count = parents.shape[1]
    node_ids = jnp.arange(node_count, dtype=jnp.int32)
    linked = jnp.logical_or(
        parents[:, :, None] == node_ids[None, None, :], node_ids[:, None] == node_ids[None, :]
    )
    reached = linked.astype(jnp.bfloat16)
    for doubling in range((node_count - 1).bit_length()):
        squared = jnp.einsum("aij,ajk->aik", reached, reached, preferred_element_type=jnp.float32)
        reached = jnp.minimum(squared, 1.0).astype(jnp.bfloat16)
    return reached


def body(
    queries, cache_keys, cache_values, tree_keys, tree_values, parents, tree_sizes, cache_lens
):
    group_size = NH // KVH
    softmax_scale = 1.0 / math.sqrt(HD)
    request = lax.axis_index("rh")
    quarter = lax.axis_index("rl")
    n_lo = lax.axis_size("rl")
    n_hi = lax.axis_size("rh")
    cache_block = cache_keys.shape[1]
    kv_local = cache_keys.shape[2] // HD
    heads_local = kv_local * group_size
    node_count = parents.shape[1]
    rows_owned = tree_keys.shape[0]

    by_head = lax.all_to_all(queries, "head", split_axis=1, concat_axis=0, tiled=True)
    query_block = lax.all_gather(by_head, "rl", axis=0, tiled=True)
    query_block = query_block.reshape(node_count, kv_local, group_size, HD)

    both = jnp.concatenate([cache_keys, cache_values], axis=2)
    mine = lax.all_to_all(both, "rh", split_axis=0, concat_axis=1, tiled=True)[0]
    mine = mine.reshape(n_hi, cache_block, 2, kv_local, HD)

    reached = ancestry(parents)
    ancestors = lax.dynamic_index_in_dim(reached, request, 0, keepdims=False)
    ancestors = lax.dynamic_slice_in_dim(ancestors, quarter * rows_owned, rows_owned, 1)
    live_tree_all = ancestors > 0.5
    length = lax.dynamic_index_in_dim(cache_lens, request, 0, keepdims=False)
    local_tree_keys = tree_keys.reshape(rows_owned, kv_local, HD)
    local_tree_values = tree_values.reshape(rows_owned, kv_local, HD)

    def one_group(s):
        block = s * n_lo + quarter
        positions = block * cache_block + jnp.arange(cache_block, dtype=jnp.int32)
        live_cache = positions < length
        live_tree = jnp.logical_and(live_tree_all, s == request)
        block_keys = mine[s, :, 0]
        block_values = mine[s, :, 1]
        cache_scores = (
            jnp.einsum(
                "igqd,pgd->igqp", query_block, block_keys, preferred_element_type=jnp.float32
            )
            * softmax_scale
        )
        cache_scores = jnp.where(live_cache[None, None, None, :], cache_scores, negative_fill)
        tree_scores = (
            jnp.einsum(
                "igqd,rgd->igqr", query_block, local_tree_keys, preferred_element_type=jnp.float32
            )
            * softmax_scale
        )
        tree_scores = jnp.where(live_tree[:, None, None, :], tree_scores, negative_fill)
        peaks = jnp.maximum(jnp.max(cache_scores, axis=3), jnp.max(tree_scores, axis=3))
        cache_weights = jnp.where(
            live_cache[None, None, None, :], jnp.exp(cache_scores - peaks[..., None]), 0.0
        )
        tree_weights = jnp.where(
            live_tree[:, None, None, :], jnp.exp(tree_scores - peaks[..., None]), 0.0
        )
        totals = jnp.sum(cache_weights, axis=3) + jnp.sum(tree_weights, axis=3)
        group_sums = jnp.einsum(
            "igqp,pgd->igqd",
            cache_weights.astype(jnp.bfloat16),
            block_values,
            preferred_element_type=jnp.float32,
        )
        group_sums = group_sums + jnp.einsum(
            "igqr,rgd->igqd",
            tree_weights.astype(jnp.bfloat16),
            local_tree_values,
            preferred_element_type=jnp.float32,
        )
        floored = jnp.maximum(totals, 1.0)
        partial_value = group_sums / floored[..., None]
        log_total = peaks + jnp.log(floored)
        return (
            partial_value.reshape(node_count, heads_local, HD),
            log_total.reshape(node_count, heads_local),
        )

    partials, log_totals = lax.map(one_group, jnp.arange(n_hi, dtype=jnp.int32))
    top = jnp.max(log_totals, axis=0)
    weights = jnp.exp(log_totals - top)
    den = jnp.sum(weights, axis=0)
    acc = jnp.sum(weights[..., None] * partials, axis=0)

    payload = jnp.concatenate(
        [acc.reshape(node_count, heads_local * HD), den, top], axis=1
    ).reshape(n_lo, rows_owned, heads_local * HD + 2 * heads_local)
    gathered = lax.all_to_all(payload, "rl", split_axis=0, concat_axis=0, tiled=True)
    got_acc = gathered[:, :, : heads_local * HD].reshape(n_lo, rows_owned, heads_local, HD)
    got_den = gathered[:, :, heads_local * HD : heads_local * HD + heads_local]
    got_top = gathered[:, :, heads_local * HD + heads_local :]
    highest = jnp.max(got_top, axis=0)
    scale = jnp.exp(got_top - highest)
    num = jnp.sum(scale[..., None] * got_acc, axis=0)
    total = jnp.sum(scale * got_den, axis=0)
    merged = (num / total[..., None]).reshape(rows_owned, heads_local * HD)

    row_nodes = quarter * rows_owned + jnp.arange(rows_owned, dtype=jnp.int32)
    live_size = lax.dynamic_index_in_dim(tree_sizes, request, 0, keepdims=False)
    live_rows = row_nodes < live_size
    return jnp.where(live_rows[:, None], merged, 0.0).astype(jnp.bfloat16)


def solution(mesh):
    def run(queries, cache_keys, cache_values, tree_keys, tree_values, parents, tree_sizes, cache_lens):
        n_hi = cache_keys.shape[0]
        n_lo = mesh.shape["req"] // n_hi
        split = Mesh(mesh.devices.reshape(n_hi, n_lo, mesh.shape["head"]), ("rh", "rl", "head"))
        rows = ("rh", "rl")
        placed = (
            P(("rh", "rl", "head"), None),
            P(None, rows, "head"),
            P(None, rows, "head"),
            P(rows, "head"),
            P(rows, "head"),
            P(),
            P(),
            P(),
        )
        return jax.shard_map(
            body, mesh=split, in_specs=placed, out_specs=P(rows, "head"), check_vma=False
        )(queries, cache_keys, cache_values, tree_keys, tree_values, parents, tree_sizes, cache_lens)

    return run
```

```python
import functools
import math

import jax
import jax.numpy as jnp
from jax import lax
from jax.experimental import pallas as pl
from jax.experimental.pallas import tpu as pltpu
from jax.sharding import Mesh
from jax.sharding import PartitionSpec as P

NH = 128
KVH = 8
HD = 128


negative_fill = -1e30


def ancestry(parents):
    node_count = parents.shape[1]
    node_ids = jnp.arange(node_count, dtype=jnp.int32)
    linked = jnp.logical_or(
        parents[:, :, None] == node_ids[None, None, :], node_ids[:, None] == node_ids[None, :]
    )
    reached = linked.astype(jnp.bfloat16)
    for doubling in range((node_count - 1).bit_length()):
        squared = jnp.einsum("aij,ajk->aik", reached, reached, preferred_element_type=jnp.float32)
        reached = jnp.minimum(squared, 1.0).astype(jnp.bfloat16)
    return reached


def attend_kernel(
    info_ref, q_ref, k_ref, v_ref, tk_ref, tv_ref, tmask_ref, acc_ref, top_ref, den_ref, *, scale
):
    s = pl.program_id(0)
    length = info_ref[0]
    request = info_ref[1]
    quarter = info_ref[2]
    n_lo = info_ref[3]
    rows = q_ref.shape[0]
    heads = q_ref.shape[1] // HD
    block_len = k_ref.shape[0]
    start = (s * n_lo + quarter) * block_len

    @pl.when(s == 0)
    def _():
        acc_ref[...] = jnp.zeros_like(acc_ref)
        top_ref[...] = jnp.full_like(top_ref, negative_fill)
        den_ref[...] = jnp.zeros_like(den_ref)

    def group(with_tree):
        def head(h, carry):
            col = pl.multiple_of(h * HD, HD)
            qh = q_ref[:, pl.ds(col, HD)]
            sc = (
                lax.dot_general(
                    qh, k_ref[...], (((1,), (1,)), ((), ())), preferred_element_type=jnp.float32
                )
                * scale
            )
            pos = start + lax.broadcasted_iota(jnp.int32, sc.shape, 1)
            live = pos < length
            sc = jnp.where(live, sc, negative_fill)
            peak = jnp.max(sc, axis=1, keepdims=True)
            if with_tree:
                st = (
                    lax.dot_general(
                        qh,
                        tk_ref[...],
                        (((1,), (1,)), ((), ())),
                        preferred_element_type=jnp.float32,
                    )
                    * scale
                )
                tlive = tmask_ref[...] > 0.5
                st = jnp.where(tlive, st, negative_fill)
                peak = jnp.maximum(peak, jnp.max(st, axis=1, keepdims=True))
            w = jnp.where(live, jnp.exp(sc - peak), 0.0)
            tot = jnp.sum(w, axis=1, keepdims=True)
            gs = jnp.dot(w.astype(jnp.bfloat16), v_ref[...], preferred_element_type=jnp.float32)
            if with_tree:
                wt = jnp.where(tlive, jnp.exp(st - peak), 0.0)
                tot = tot + jnp.sum(wt, axis=1, keepdims=True)
                gs = gs + jnp.dot(
                    wt.astype(jnp.bfloat16), tv_ref[...], preferred_element_type=jnp.float32
                )
            floored = jnp.maximum(tot, 1.0)
            part = gs / floored
            lt = peak + jnp.log(floored)
            old = top_ref[h][:, :1]
            new = jnp.maximum(old, lt)
            keep = jnp.exp(old - new)
            add = jnp.exp(lt - new)
            acc_ref[:, pl.ds(col, HD)] = keep * acc_ref[:, pl.ds(col, HD)] + add * part
            den_ref[h] = jnp.broadcast_to(keep * den_ref[h][:, :1] + add, (rows, HD))
            top_ref[h] = jnp.broadcast_to(new, (rows, HD))
            return carry

        lax.fori_loop(0, heads, head, 0)

    @pl.when(s == request)
    def _():
        group(True)

    @pl.when(jnp.logical_and(s != request, start < length))
    def _():
        group(False)


def attend(info, query_block, kv, tree_keys, tree_values, tree_mask, n_groups):
    rows, width = query_block.shape
    heads = width // HD
    block_len = kv.shape[0] // n_groups
    tree_rows = tree_keys.shape[0]
    stats = jax.ShapeDtypeStruct((heads, rows, HD), jnp.float32)
    return pl.pallas_call(
        functools.partial(attend_kernel, scale=1.0 / math.sqrt(HD)),
        out_shape=(jax.ShapeDtypeStruct((rows, width), jnp.float32), stats, stats),
        grid_spec=pltpu.PrefetchScalarGridSpec(
            num_scalar_prefetch=1,
            grid=(n_groups,),
            in_specs=[
                pl.BlockSpec((rows, width), lambda s, info: (0, 0)),
                pl.BlockSpec((block_len, HD), lambda s, info: (s, 0)),
                pl.BlockSpec((block_len, HD), lambda s, info: (s, 1)),
                pl.BlockSpec((tree_rows, HD), lambda s, info: (0, 0)),
                pl.BlockSpec((tree_rows, HD), lambda s, info: (0, 0)),
                pl.BlockSpec((rows, tree_rows), lambda s, info: (0, 0)),
            ],
            out_specs=[
                pl.BlockSpec((rows, width), lambda s, info: (0, 0)),
                pl.BlockSpec((heads, rows, HD), lambda s, info: (0, 0, 0)),
                pl.BlockSpec((heads, rows, HD), lambda s, info: (0, 0, 0)),
            ],
        ),
        compiler_params=pltpu.CompilerParams(dimension_semantics=("arbitrary",)),
    )(info, query_block, kv, kv, tree_keys, tree_values, tree_mask)


def body(
    queries, cache_keys, cache_values, tree_keys, tree_values, parents, tree_sizes, cache_lens
):
    group_size = NH // KVH
    softmax_scale = 1.0 / math.sqrt(HD)
    request = lax.axis_index("rh")
    quarter = lax.axis_index("rl")
    n_lo = lax.axis_size("rl")
    n_hi = lax.axis_size("rh")
    cache_block = cache_keys.shape[1]
    kv_local = cache_keys.shape[2] // HD
    heads_local = kv_local * group_size
    node_count = parents.shape[1]
    rows_owned = tree_keys.shape[0]

    by_head = lax.all_to_all(queries, "head", split_axis=1, concat_axis=0, tiled=True)
    query_block = lax.all_gather(by_head, "rl", axis=0, tiled=True)

    both = jnp.concatenate([cache_keys, cache_values], axis=2)
    mine = lax.all_to_all(both, "rh", split_axis=0, concat_axis=1, tiled=True)[0]

    reached = ancestry(parents)
    ancestors = lax.dynamic_index_in_dim(reached, request, 0, keepdims=False)
    ancestors = lax.dynamic_slice_in_dim(ancestors, quarter * rows_owned, rows_owned, 1)
    tree_mask = ancestors.astype(jnp.float32)
    length = lax.dynamic_index_in_dim(cache_lens, request, 0, keepdims=False)
    info = jnp.stack([length, request, quarter, n_lo]).astype(jnp.int32)
    acc, top, den = attend(info, query_block, mine, tree_keys, tree_values, tree_mask, n_hi)
    top = top[:, :, 0].T
    den = den[:, :, 0].T

    payload = jnp.concatenate([acc, den, top], axis=1).reshape(n_lo, rows_owned, heads_local * HD + 2 * heads_local)
    gathered = lax.all_to_all(payload, "rl", split_axis=0, concat_axis=0, tiled=True)
    got_acc = gathered[:, :, : heads_local * HD].reshape(n_lo, rows_owned, heads_local, HD)
    got_den = gathered[:, :, heads_local * HD : heads_local * HD + heads_local]
    got_top = gathered[:, :, heads_local * HD + heads_local :]
    highest = jnp.max(got_top, axis=0)
    scale = jnp.exp(got_top - highest)
    num = jnp.sum(scale[..., None] * got_acc, axis=0)
    total = jnp.sum(scale * got_den, axis=0)
    merged = (num / total[..., None]).reshape(rows_owned, heads_local * HD)

    row_nodes = quarter * rows_owned + jnp.arange(rows_owned, dtype=jnp.int32)
    live_size = lax.dynamic_index_in_dim(tree_sizes, request, 0, keepdims=False)
    live_rows = row_nodes < live_size
    return jnp.where(live_rows[:, None], merged, 0.0).astype(jnp.bfloat16)


def solution(mesh):
    def run(queries, cache_keys, cache_values, tree_keys, tree_values, parents, tree_sizes, cache_lens):
        n_hi = cache_keys.shape[0]
        n_lo = mesh.shape["req"] // n_hi
        split = Mesh(mesh.devices.reshape(n_hi, n_lo, mesh.shape["head"]), ("rh", "rl", "head"))
        rows = ("rh", "rl")
        placed = (
            P(("rh", "rl", "head"), None),
            P(None, rows, "head"),
            P(None, rows, "head"),
            P(rows, "head"),
            P(rows, "head"),
            P(),
            P(),
            P(),
        )
        return jax.shard_map(
            body, mesh=split, in_specs=placed, out_specs=P(rows, "head"), check_vma=False
        )(queries, cache_keys, cache_values, tree_keys, tree_values, parents, tree_sizes, cache_lens)

    return run
```

```python
import functools
import math

import jax
import jax.numpy as jnp
from jax import lax
from jax.experimental import pallas as pl
from jax.experimental.pallas import tpu as pltpu
from jax.sharding import Mesh
from jax.sharding import PartitionSpec as P

NH = 128
KVH = 8
HD = 128


negative_fill = -1e30


def ancestry(parents):
    node_count = parents.shape[1]
    node_ids = jnp.arange(node_count, dtype=jnp.int32)
    linked = jnp.logical_or(
        parents[:, :, None] == node_ids[None, None, :], node_ids[:, None] == node_ids[None, :]
    )
    reached = linked.astype(jnp.bfloat16)
    for doubling in range((node_count - 1).bit_length()):
        squared = jnp.einsum("aij,ajk->aik", reached, reached, preferred_element_type=jnp.float32)
        reached = jnp.minimum(squared, 1.0).astype(jnp.bfloat16)
    return reached


def attend_kernel(
    info_ref, q_ref, k_ref, v_ref, tk_ref, tv_ref, tmask_ref, acc_ref, top_ref, den_ref, *, scale
):
    s = pl.program_id(0)
    length = info_ref[0]
    request = info_ref[1]
    quarter = info_ref[2]
    n_lo = info_ref[3]
    rows = q_ref.shape[0]
    heads = q_ref.shape[1] // HD
    block_len = k_ref.shape[0]
    start = (s * n_lo + quarter) * block_len

    @pl.when(s == 0)
    def _():
        acc_ref[...] = jnp.zeros_like(acc_ref)
        top_ref[...] = jnp.full_like(top_ref, negative_fill)
        den_ref[...] = jnp.zeros_like(den_ref)

    def group(with_tree):
        def head(h, carry):
            col = pl.multiple_of(h * HD, HD)
            qh = q_ref[:, pl.ds(col, HD)]
            sc = (
                lax.dot_general(
                    qh, k_ref[...], (((1,), (1,)), ((), ())), preferred_element_type=jnp.float32
                )
                * scale
            )
            pos = start + lax.broadcasted_iota(jnp.int32, sc.shape, 1)
            live = pos < length
            sc = jnp.where(live, sc, negative_fill)
            peak = jnp.max(sc, axis=1, keepdims=True)
            if with_tree:
                st = (
                    lax.dot_general(
                        qh,
                        tk_ref[...],
                        (((1,), (1,)), ((), ())),
                        preferred_element_type=jnp.float32,
                    )
                    * scale
                )
                tlive = tmask_ref[...] > 0.5
                st = jnp.where(tlive, st, negative_fill)
                peak = jnp.maximum(peak, jnp.max(st, axis=1, keepdims=True))
            w = jnp.where(live, jnp.exp(sc - peak), 0.0)
            tot = jnp.sum(w, axis=1, keepdims=True)
            gs = jnp.dot(w.astype(jnp.bfloat16), v_ref[...], preferred_element_type=jnp.float32)
            if with_tree:
                wt = jnp.where(tlive, jnp.exp(st - peak), 0.0)
                tot = tot + jnp.sum(wt, axis=1, keepdims=True)
                gs = gs + jnp.dot(
                    wt.astype(jnp.bfloat16), tv_ref[...], preferred_element_type=jnp.float32
                )
            floored = jnp.maximum(tot, 1.0)
            part = gs / floored
            lt = peak + jnp.log(floored)
            old = top_ref[h][:, :1]
            new = jnp.maximum(old, lt)
            keep = jnp.exp(old - new)
            add = jnp.exp(lt - new)
            acc_ref[:, pl.ds(col, HD)] = keep * acc_ref[:, pl.ds(col, HD)] + add * part
            den_ref[h] = jnp.broadcast_to(keep * den_ref[h][:, :1] + add, (rows, HD))
            top_ref[h] = jnp.broadcast_to(new, (rows, HD))
            return carry

        lax.fori_loop(0, heads, head, 0)

    @pl.when(s == request)
    def _():
        group(True)

    @pl.when(jnp.logical_and(s != request, start < length))
    def _():
        group(False)


def attend(info, query_block, kv, tree_keys, tree_values, tree_mask, n_groups):
    rows, width = query_block.shape
    heads = width // HD
    block_len = kv.shape[0] // n_groups
    tree_rows = tree_keys.shape[0]
    stats = jax.ShapeDtypeStruct((heads, rows, HD), jnp.float32)
    return pl.pallas_call(
        functools.partial(attend_kernel, scale=1.0 / math.sqrt(HD)),
        out_shape=(jax.ShapeDtypeStruct((rows, width), jnp.float32), stats, stats),
        grid_spec=pltpu.PrefetchScalarGridSpec(
            num_scalar_prefetch=1,
            grid=(n_groups,),
            in_specs=[
                pl.BlockSpec((rows, width), lambda s, info: (0, 0)),
                pl.BlockSpec((block_len, HD), lambda s, info: (s, 0)),
                pl.BlockSpec((block_len, HD), lambda s, info: (s, 1)),
                pl.BlockSpec((tree_rows, HD), lambda s, info: (0, 0)),
                pl.BlockSpec((tree_rows, HD), lambda s, info: (0, 0)),
                pl.BlockSpec((rows, tree_rows), lambda s, info: (0, 0)),
            ],
            out_specs=[
                pl.BlockSpec((rows, width), lambda s, info: (0, 0)),
                pl.BlockSpec((heads, rows, HD), lambda s, info: (0, 0, 0)),
                pl.BlockSpec((heads, rows, HD), lambda s, info: (0, 0, 0)),
            ],
        ),
        compiler_params=pltpu.CompilerParams(dimension_semantics=("arbitrary",)),
    )(info, query_block, kv, kv, tree_keys, tree_values, tree_mask)


def body(
    queries, cache_keys, cache_values, tree_keys, tree_values, parents, tree_sizes, cache_lens
):
    group_size = NH // KVH
    softmax_scale = 1.0 / math.sqrt(HD)
    request = lax.axis_index("rh")
    quarter = lax.axis_index("rl")
    n_lo = lax.axis_size("rl")
    n_hi = lax.axis_size("rh")
    cache_block = cache_keys.shape[1]
    kv_local = cache_keys.shape[2] // HD
    heads_local = kv_local * group_size
    node_count = parents.shape[1]
    rows_owned = tree_keys.shape[0]

    n_head = lax.axis_size("head")
    width = queries.shape[1] // n_head
    sliced = queries.reshape(queries.shape[0], n_head, width).transpose(1, 0, 2)
    sliced = jnp.broadcast_to(sliced[None], (n_lo,) + sliced.shape)
    sliced = sliced.reshape(n_lo * n_head, queries.shape[0], width)
    query_block = lax.all_to_all(sliced, ("rl", "head"), split_axis=0, concat_axis=0, tiled=True)
    query_block = query_block.reshape(node_count, width)

    both = jnp.concatenate([cache_keys, cache_values], axis=2)
    mine = lax.all_to_all(both, "rh", split_axis=0, concat_axis=1, tiled=True)[0]

    reached = ancestry(parents)
    ancestors = lax.dynamic_index_in_dim(reached, request, 0, keepdims=False)
    ancestors = lax.dynamic_slice_in_dim(ancestors, quarter * rows_owned, rows_owned, 1)
    tree_mask = ancestors.astype(jnp.float32)
    length = lax.dynamic_index_in_dim(cache_lens, request, 0, keepdims=False)
    info = jnp.stack([length, request, quarter, n_lo]).astype(jnp.int32)
    acc, top, den = attend(info, query_block, mine, tree_keys, tree_values, tree_mask, n_hi)
    top = top[:, :, 0].T
    den = den[:, :, 0].T

    payload = jnp.concatenate([acc, den, top], axis=1).reshape(n_lo, rows_owned, heads_local * HD + 2 * heads_local)
    gathered = lax.all_to_all(payload, "rl", split_axis=0, concat_axis=0, tiled=True)
    got_acc = gathered[:, :, : heads_local * HD].reshape(n_lo, rows_owned, heads_local, HD)
    got_den = gathered[:, :, heads_local * HD : heads_local * HD + heads_local]
    got_top = gathered[:, :, heads_local * HD + heads_local :]
    highest = jnp.max(got_top, axis=0)
    scale = jnp.exp(got_top - highest)
    num = jnp.sum(scale[..., None] * got_acc, axis=0)
    total = jnp.sum(scale * got_den, axis=0)
    merged = (num / total[..., None]).reshape(rows_owned, heads_local * HD)

    row_nodes = quarter * rows_owned + jnp.arange(rows_owned, dtype=jnp.int32)
    live_size = lax.dynamic_index_in_dim(tree_sizes, request, 0, keepdims=False)
    live_rows = row_nodes < live_size
    return jnp.where(live_rows[:, None], merged, 0.0).astype(jnp.bfloat16)


def solution(mesh):
    def run(queries, cache_keys, cache_values, tree_keys, tree_values, parents, tree_sizes, cache_lens):
        n_hi = cache_keys.shape[0]
        n_lo = mesh.shape["req"] // n_hi
        split = Mesh(mesh.devices.reshape(n_hi, n_lo, mesh.shape["head"]), ("rh", "rl", "head"))
        rows = ("rh", "rl")
        placed = (
            P(("rh", "rl", "head"), None),
            P(None, rows, "head"),
            P(None, rows, "head"),
            P(rows, "head"),
            P(rows, "head"),
            P(),
            P(),
            P(),
        )
        return jax.shard_map(
            body, mesh=split, in_specs=placed, out_specs=P(rows, "head"), check_vma=False
        )(queries, cache_keys, cache_values, tree_keys, tree_values, parents, tree_sizes, cache_lens)

    return run
```

```python
import functools
import math

import jax
import jax.numpy as jnp
from jax import lax
from jax.experimental import pallas as pl
from jax.experimental.pallas import tpu as pltpu
from jax.sharding import Mesh
from jax.sharding import PartitionSpec as P

NH = 128
KVH = 8
HD = 128


negative_fill = -1e30


def ancestry(parents):
    node_count = parents.shape[1]
    node_ids = jnp.arange(node_count, dtype=jnp.int32)
    linked = jnp.logical_or(
        parents[:, :, None] == node_ids[None, None, :], node_ids[:, None] == node_ids[None, :]
    )
    reached = linked.astype(jnp.bfloat16)
    for doubling in range((node_count - 1).bit_length()):
        squared = jnp.einsum("aij,ajk->aik", reached, reached, preferred_element_type=jnp.float32)
        reached = jnp.minimum(squared, 1.0).astype(jnp.bfloat16)
    return reached


def attend_kernel(
    info_ref, q_ref, kt_ref, v_ref, tkt_ref, tv_ref, tmask_ref, acc_ref, top_ref, den_ref, *, scale
):
    s = pl.program_id(0)
    length = info_ref[0]
    request = info_ref[1]
    quarter = info_ref[2]
    n_lo = info_ref[3]
    live_nodes = info_ref[4]
    rows = q_ref.shape[0]
    heads = q_ref.shape[1] // HD
    block_len = kt_ref.shape[1]
    start = (s * n_lo + quarter) * block_len
    full = start + block_len <= length

    @pl.when(s == 0)
    def _():
        acc_ref[...] = jnp.zeros_like(acc_ref)
        top_ref[...] = jnp.full_like(top_ref, negative_fill)
        den_ref[...] = jnp.zeros_like(den_ref)

    def group(with_tree, masked, count):
        def head(h, carry):
            col = pl.multiple_of(h * HD, HD)
            qh = q_ref[:count, pl.ds(col, HD)]
            sc = jnp.dot(qh, kt_ref[...], preferred_element_type=jnp.float32) * scale
            if masked:
                pos = start + lax.broadcasted_iota(jnp.int32, sc.shape, 1)
                live = pos < length
                sc = jnp.where(live, sc, negative_fill)
            peak = jnp.max(sc, axis=1, keepdims=True)
            if with_tree:
                st = jnp.dot(qh, tkt_ref[...], preferred_element_type=jnp.float32) * scale
                tlive = tmask_ref[:count, :] > 0.5
                st = jnp.where(tlive, st, negative_fill)
                peak = jnp.maximum(peak, jnp.max(st, axis=1, keepdims=True))
            w = jnp.exp(sc - peak)
            if masked:
                w = jnp.where(live, w, 0.0)
            tot = jnp.sum(w, axis=1, keepdims=True)
            gs = jnp.dot(w.astype(jnp.bfloat16), v_ref[...], preferred_element_type=jnp.float32)
            if with_tree:
                wt = jnp.where(tlive, jnp.exp(st - peak), 0.0)
                tot = tot + jnp.sum(wt, axis=1, keepdims=True)
                gs = gs + jnp.dot(
                    wt.astype(jnp.bfloat16), tv_ref[...], preferred_element_type=jnp.float32
                )
            floored = jnp.maximum(tot, 1.0)
            part = gs / floored
            lt = peak + jnp.log(floored)
            old = top_ref[h, :count, :][:, :1]
            new = jnp.maximum(old, lt)
            keep = jnp.exp(old - new)
            add = jnp.exp(lt - new)
            acc_ref[:count, pl.ds(col, HD)] = (
                keep * acc_ref[:count, pl.ds(col, HD)] + add * part
            )
            den_ref[h, :count, :] = jnp.broadcast_to(
                keep * den_ref[h, :count, :][:, :1] + add, (count, HD)
            )
            top_ref[h, :count, :] = jnp.broadcast_to(new, (count, HD))
            return carry

        lax.fori_loop(0, heads, head, 0)

    half = rows // 2
    for with_tree in (True, False):
        mine = s == request if with_tree else jnp.logical_and(s != request, start < length)
        for masked in (False, True):
            case = jnp.logical_and(mine, jnp.logical_not(full) if masked else full)
            for count in (half, rows):
                few = live_nodes <= half
                pick = jnp.logical_and(case, few if count == half else jnp.logical_not(few))
                pl.when(pick)(functools.partial(group, with_tree, masked, count))


def attend(info, query_block, keys_t, values, tree_keys_t, tree_values, tree_mask):
    rows, width = query_block.shape
    heads = width // HD
    n_groups, _, block_len = keys_t.shape
    tree_rows = tree_values.shape[0]
    stats = jax.ShapeDtypeStruct((heads, rows, HD), jnp.float32)
    return pl.pallas_call(
        functools.partial(attend_kernel, scale=1.0 / math.sqrt(HD)),
        out_shape=(jax.ShapeDtypeStruct((rows, width), jnp.float32), stats, stats),
        grid_spec=pltpu.PrefetchScalarGridSpec(
            num_scalar_prefetch=1,
            grid=(n_groups,),
            in_specs=[
                pl.BlockSpec((rows, width), lambda s, info: (0, 0)),
                pl.BlockSpec((None, HD, block_len), lambda s, info: (s, 0, 0)),
                pl.BlockSpec((None, block_len, HD), lambda s, info: (s, 0, 0)),
                pl.BlockSpec((HD, tree_rows), lambda s, info: (0, 0)),
                pl.BlockSpec((tree_rows, HD), lambda s, info: (0, 0)),
                pl.BlockSpec((rows, tree_rows), lambda s, info: (0, 0)),
            ],
            out_specs=[
                pl.BlockSpec((rows, width), lambda s, info: (0, 0)),
                pl.BlockSpec((heads, rows, HD), lambda s, info: (0, 0, 0)),
                pl.BlockSpec((heads, rows, HD), lambda s, info: (0, 0, 0)),
            ],
        ),
        compiler_params=pltpu.CompilerParams(dimension_semantics=("arbitrary",)),
    )(info, query_block, keys_t, values, tree_keys_t, tree_values, tree_mask)


def body(
    queries, cache_keys, cache_values, tree_keys, tree_values, parents, tree_sizes, cache_lens
):
    group_size = NH // KVH
    softmax_scale = 1.0 / math.sqrt(HD)
    request = lax.axis_index("rh")
    quarter = lax.axis_index("rl")
    n_lo = lax.axis_size("rl")
    n_hi = lax.axis_size("rh")
    cache_block = cache_keys.shape[1]
    kv_local = cache_keys.shape[2] // HD
    heads_local = kv_local * group_size
    node_count = parents.shape[1]
    rows_owned = tree_keys.shape[0]

    n_head = lax.axis_size("head")
    width = queries.shape[1] // n_head
    sliced = queries.reshape(queries.shape[0], n_head, width).transpose(1, 0, 2)
    sliced = jnp.broadcast_to(sliced[None], (n_lo,) + sliced.shape)
    sliced = sliced.reshape(n_lo * n_head, queries.shape[0], width)
    query_block = lax.all_to_all(sliced, ("rl", "head"), split_axis=0, concat_axis=0, tiled=True)
    query_block = query_block.reshape(node_count, width)

    both = jnp.concatenate([cache_keys, cache_values], axis=2)
    mine = lax.all_to_all(both, "rh", split_axis=0, concat_axis=1, tiled=True)[0]

    reached = ancestry(parents)
    ancestors = lax.dynamic_index_in_dim(reached, request, 0, keepdims=False)
    ancestors = lax.dynamic_slice_in_dim(ancestors, quarter * rows_owned, rows_owned, 1)
    tree_mask = ancestors.astype(jnp.float32)
    length = lax.dynamic_index_in_dim(cache_lens, request, 0, keepdims=False)
    live_size = lax.dynamic_index_in_dim(tree_sizes, request, 0, keepdims=False)
    info = jnp.stack([length, request, quarter, n_lo, live_size]).astype(jnp.int32)
    mine = mine.reshape(n_hi, cache_block, 2 * HD)
    keys_t = mine[:, :, :HD].transpose(0, 2, 1)
    values = mine[:, :, HD:]
    acc, top, den = attend(info, query_block, keys_t, values, tree_keys.T, tree_values, tree_mask)
    top = top[:, :, 0].T
    den = den[:, :, 0].T

    payload = jnp.concatenate([acc, den, top], axis=1).reshape(n_lo, rows_owned, heads_local * HD + 2 * heads_local)
    gathered = lax.all_to_all(payload, "rl", split_axis=0, concat_axis=0, tiled=True)
    got_acc = gathered[:, :, : heads_local * HD].reshape(n_lo, rows_owned, heads_local, HD)
    got_den = gathered[:, :, heads_local * HD : heads_local * HD + heads_local]
    got_top = gathered[:, :, heads_local * HD + heads_local :]
    highest = jnp.max(got_top, axis=0)
    scale = jnp.exp(got_top - highest)
    num = jnp.sum(scale[..., None] * got_acc, axis=0)
    total = jnp.sum(scale * got_den, axis=0)
    merged = (num / total[..., None]).reshape(rows_owned, heads_local * HD)

    row_nodes = quarter * rows_owned + jnp.arange(rows_owned, dtype=jnp.int32)
    live_rows = row_nodes < live_size
    return jnp.where(live_rows[:, None], merged, 0.0).astype(jnp.bfloat16)


def solution(mesh):
    def run(queries, cache_keys, cache_values, tree_keys, tree_values, parents, tree_sizes, cache_lens):
        n_hi = cache_keys.shape[0]
        n_lo = mesh.shape["req"] // n_hi
        split = Mesh(mesh.devices.reshape(n_hi, n_lo, mesh.shape["head"]), ("rh", "rl", "head"))
        rows = ("rh", "rl")
        placed = (
            P(("rh", "rl", "head"), None),
            P(None, rows, "head"),
            P(None, rows, "head"),
            P(rows, "head"),
            P(rows, "head"),
            P(),
            P(),
            P(),
        )
        return jax.shard_map(
            body, mesh=split, in_specs=placed, out_specs=P(rows, "head"), check_vma=False
        )(queries, cache_keys, cache_values, tree_keys, tree_values, parents, tree_sizes, cache_lens)

    return run
```

```python
import functools
import math

import jax
import jax.numpy as jnp
from jax import lax
from jax.experimental import pallas as pl
from jax.experimental.pallas import tpu as pltpu
from jax.sharding import Mesh
from jax.sharding import PartitionSpec as P

NH = 128
KVH = 8
HD = 128


negative_fill = -1e30


def ancestry(parents):
    node_count = parents.shape[1]
    node_ids = jnp.arange(node_count, dtype=jnp.int32)
    linked = jnp.logical_or(
        parents[:, :, None] == node_ids[None, None, :], node_ids[:, None] == node_ids[None, :]
    )
    reached = linked.astype(jnp.bfloat16)
    for doubling in range((node_count - 1).bit_length()):
        squared = jnp.einsum("aij,ajk->aik", reached, reached, preferred_element_type=jnp.float32)
        reached = jnp.minimum(squared, 1.0).astype(jnp.bfloat16)
    return reached


def group_kernel(
    info_ref, q_ref, kt_ref, v_ref, tkt_ref, tv_ref, tmask_ref, part_ref, lt_ref, *, scale, own
):
    length = info_ref[0]
    request = info_ref[1]
    quarter = info_ref[2]
    n_lo = info_ref[3]
    live_nodes = info_ref[4]
    s = info_ref[5]
    rows = q_ref.shape[0]
    heads = q_ref.shape[1] // HD
    block_len = kt_ref.shape[1]
    start = (s * n_lo + quarter) * block_len
    full = start + block_len <= length

    def compute(with_tree, masked, count):
        def head(h, carry):
            col = pl.multiple_of(h * HD, HD)
            qh = q_ref[:count, pl.ds(col, HD)]
            sc = jnp.dot(qh, kt_ref[...], preferred_element_type=jnp.float32) * scale
            if masked:
                pos = start + lax.broadcasted_iota(jnp.int32, sc.shape, 1)
                live = pos < length
                sc = jnp.where(live, sc, negative_fill)
            peak = jnp.max(sc, axis=1, keepdims=True)
            if with_tree:
                st = jnp.dot(qh, tkt_ref[...], preferred_element_type=jnp.float32) * scale
                tlive = tmask_ref[:count, :] > 0.5
                st = jnp.where(tlive, st, negative_fill)
                peak = jnp.maximum(peak, jnp.max(st, axis=1, keepdims=True))
            w = jnp.exp(sc - peak)
            if masked:
                w = jnp.where(live, w, 0.0)
            tot = jnp.sum(w, axis=1, keepdims=True)
            gs = jnp.dot(w.astype(jnp.bfloat16), v_ref[...], preferred_element_type=jnp.float32)
            if with_tree:
                wt = jnp.where(tlive, jnp.exp(st - peak), 0.0)
                tot = tot + jnp.sum(wt, axis=1, keepdims=True)
                gs = gs + jnp.dot(
                    wt.astype(jnp.bfloat16), tv_ref[...], preferred_element_type=jnp.float32
                )
            floored = jnp.maximum(tot, 1.0)
            part_ref[:count, pl.ds(col, HD)] = gs / floored
            lt_ref[h, :count, :] = jnp.broadcast_to(peak + jnp.log(floored), (count, HD))
            return carry

        lax.fori_loop(0, heads, head, 0)
        if count < rows:
            part_ref[count:, :] = jnp.zeros((rows - count, part_ref.shape[1]), jnp.float32)
            lt_ref[:, count:, :] = jnp.full((heads, rows - count, HD), negative_fill, jnp.float32)

    half = rows // 2
    mine = True if own else start < length
    for masked in (False, True):
        case = jnp.logical_and(mine, jnp.logical_not(full) if masked else full)
        for count in (half, rows):
            few = live_nodes <= half
            pick = jnp.logical_and(case, few if count == half else jnp.logical_not(few))
            pl.when(pick)(functools.partial(compute, own, masked, count))

    if not own:

        @pl.when(start >= length)
        def _():
            part_ref[...] = jnp.zeros_like(part_ref)
            lt_ref[...] = jnp.full_like(lt_ref, negative_fill)


def attend_group(info, query_block, keys_t, values, tree_keys_t, tree_values, tree_mask, own):
    rows, width = query_block.shape
    heads = width // HD
    vmem = pl.BlockSpec(memory_space=pltpu.VMEM)
    return pl.pallas_call(
        functools.partial(group_kernel, scale=1.0 / math.sqrt(HD), own=own),
        out_shape=(
            jax.ShapeDtypeStruct((rows, width), jnp.float32),
            jax.ShapeDtypeStruct((heads, rows, HD), jnp.float32),
        ),
        in_specs=[pl.BlockSpec(memory_space=pltpu.SMEM)] + [vmem] * 6,
        out_specs=(vmem, vmem),
    )(info, query_block, keys_t, values, tree_keys_t, tree_values, tree_mask)


def body(
    queries, cache_keys, cache_values, tree_keys, tree_values, parents, tree_sizes, cache_lens
):
    group_size = NH // KVH
    softmax_scale = 1.0 / math.sqrt(HD)
    request = lax.axis_index("rh")
    quarter = lax.axis_index("rl")
    n_lo = lax.axis_size("rl")
    n_hi = lax.axis_size("rh")
    cache_block = cache_keys.shape[1]
    kv_local = cache_keys.shape[2] // HD
    heads_local = kv_local * group_size
    node_count = parents.shape[1]
    rows_owned = tree_keys.shape[0]

    n_head = lax.axis_size("head")
    width = queries.shape[1] // n_head
    sliced = queries.reshape(queries.shape[0], n_head, width).transpose(1, 0, 2)
    sliced = jnp.broadcast_to(sliced[None], (n_lo,) + sliced.shape)
    sliced = sliced.reshape(n_lo * n_head, queries.shape[0], width)
    query_block = lax.all_to_all(sliced, ("rl", "head"), split_axis=0, concat_axis=0, tiled=True)
    query_block = query_block.reshape(node_count, width)

    reached = ancestry(parents)
    ancestors = lax.dynamic_index_in_dim(reached, request, 0, keepdims=False)
    ancestors = lax.dynamic_slice_in_dim(ancestors, quarter * rows_owned, rows_owned, 1)
    tree_mask = ancestors.astype(jnp.float32)
    length = lax.dynamic_index_in_dim(cache_lens, request, 0, keepdims=False)
    live_size = lax.dynamic_index_in_dim(tree_sizes, request, 0, keepdims=False)
    keys_t = cache_keys.transpose(0, 2, 1)
    tree_keys_t = tree_keys.T

    def run_group(s, block_keys_t, block_values, own):
        info = jnp.stack([length, request, quarter, n_lo, live_size, s]).astype(jnp.int32)
        part, lt = attend_group(
            info, query_block, block_keys_t, block_values, tree_keys_t, tree_values, tree_mask, own
        )
        return part, lt[:, :, 0].T

    results = [
        run_group(
            request,
            lax.dynamic_index_in_dim(keys_t, request, 0, keepdims=False),
            lax.dynamic_index_in_dim(cache_values, request, 0, keepdims=False),
            True,
        )
    ]
    for shift in range(1, n_hi):
        target = (request + shift) % n_hi
        pairs = [(i, (i + shift) % n_hi) for i in range(n_hi)]
        got_keys_t, got_values = lax.ppermute(
            (
                lax.dynamic_index_in_dim(keys_t, target, 0, keepdims=False),
                lax.dynamic_index_in_dim(cache_values, target, 0, keepdims=False),
            ),
            "rh",
            pairs,
        )
        results.append(run_group((request - shift) % n_hi, got_keys_t, got_values, False))

    parts = jnp.stack([r[0] for r in results])
    lts = jnp.stack([r[1] for r in results])
    top = jnp.max(lts, axis=0)
    weights = jnp.exp(lts - top)
    den = jnp.sum(weights, axis=0)
    acc = jnp.sum(
        jnp.repeat(weights, HD, axis=2) * parts, axis=0
    )

    payload = jnp.concatenate([acc, den, top], axis=1).reshape(n_lo, rows_owned, heads_local * HD + 2 * heads_local)
    gathered = lax.all_to_all(payload, "rl", split_axis=0, concat_axis=0, tiled=True)
    got_acc = gathered[:, :, : heads_local * HD].reshape(n_lo, rows_owned, heads_local, HD)
    got_den = gathered[:, :, heads_local * HD : heads_local * HD + heads_local]
    got_top = gathered[:, :, heads_local * HD + heads_local :]
    highest = jnp.max(got_top, axis=0)
    scale = jnp.exp(got_top - highest)
    num = jnp.sum(scale[..., None] * got_acc, axis=0)
    total = jnp.sum(scale * got_den, axis=0)
    merged = (num / total[..., None]).reshape(rows_owned, heads_local * HD)

    row_nodes = quarter * rows_owned + jnp.arange(rows_owned, dtype=jnp.int32)
    live_rows = row_nodes < live_size
    return jnp.where(live_rows[:, None], merged, 0.0).astype(jnp.bfloat16)


def solution(mesh):
    def run(queries, cache_keys, cache_values, tree_keys, tree_values, parents, tree_sizes, cache_lens):
        n_hi = cache_keys.shape[0]
        n_lo = mesh.shape["req"] // n_hi
        split = Mesh(mesh.devices.reshape(n_hi, n_lo, mesh.shape["head"]), ("rh", "rl", "head"))
        rows = ("rh", "rl")
        placed = (
            P(("rh", "rl", "head"), None),
            P(None, rows, "head"),
            P(None, rows, "head"),
            P(rows, "head"),
            P(rows, "head"),
            P(),
            P(),
            P(),
        )
        return jax.shard_map(
            body, mesh=split, in_specs=placed, out_specs=P(rows, "head"), check_vma=False
        )(queries, cache_keys, cache_values, tree_keys, tree_values, parents, tree_sizes, cache_lens)

    return run
```

```python
import functools
import math

import jax
import jax.numpy as jnp
from jax import lax
from jax.experimental import pallas as pl
from jax.experimental.pallas import tpu as pltpu
from jax.sharding import Mesh
from jax.sharding import PartitionSpec as P

NH = 128
KVH = 8
HD = 128


negative_fill = -1e30


def ancestry(parents):
    node_count = parents.shape[1]
    node_ids = jnp.arange(node_count, dtype=jnp.int32)
    linked = jnp.logical_or(
        parents[:, :, None] == node_ids[None, None, :], node_ids[:, None] == node_ids[None, :]
    )
    reached = linked.astype(jnp.bfloat16)
    for doubling in range((node_count - 1).bit_length()):
        squared = jnp.einsum("aij,ajk->aik", reached, reached, preferred_element_type=jnp.float32)
        reached = jnp.minimum(squared, 1.0).astype(jnp.bfloat16)
    return reached


def group_kernel(
    info_ref, q_ref, kt_ref, v_ref, tkt_ref, tv_ref, tmask_ref, part_ref, lt_ref, *, scale, shift
):
    own = shift == 0
    length = info_ref[0]
    request = info_ref[1]
    quarter = info_ref[2]
    n_lo = info_ref[3]
    live_nodes = info_ref[4]
    n_hi = info_ref[5]
    s = lax.rem(request - shift + n_hi, n_hi)
    rows = q_ref.shape[0]
    heads = q_ref.shape[1] // HD
    block_len = kt_ref.shape[1]
    start = (s * n_lo + quarter) * block_len
    full = start + block_len <= length

    def compute(with_tree, masked, count):
        def head(h, lts):
            col = pl.multiple_of(h * HD, HD)
            qh = q_ref[:count, pl.ds(col, HD)]
            sc = jnp.dot(qh, kt_ref[...], preferred_element_type=jnp.float32) * scale
            if masked:
                pos = start + lax.broadcasted_iota(jnp.int32, sc.shape, 1)
                live = pos < length
                sc = jnp.where(live, sc, negative_fill)
            peak = jnp.max(sc, axis=1, keepdims=True)
            if with_tree:
                st = jnp.dot(qh, tkt_ref[...], preferred_element_type=jnp.float32) * scale
                tlive = tmask_ref[:count, :] > 0.5
                st = jnp.where(tlive, st, negative_fill)
                peak = jnp.maximum(peak, jnp.max(st, axis=1, keepdims=True))
            w = jnp.exp(sc - peak)
            if masked:
                w = jnp.where(live, w, 0.0)
            tot = jnp.sum(w, axis=1, keepdims=True)
            gs = jnp.dot(w.astype(jnp.bfloat16), v_ref[...], preferred_element_type=jnp.float32)
            if with_tree:
                wt = jnp.where(tlive, jnp.exp(st - peak), 0.0)
                tot = tot + jnp.sum(wt, axis=1, keepdims=True)
                gs = gs + jnp.dot(
                    wt.astype(jnp.bfloat16), tv_ref[...], preferred_element_type=jnp.float32
                )
            floored = jnp.maximum(tot, 1.0)
            part_ref[:count, pl.ds(col, HD)] = gs / floored
            lane = lax.broadcasted_iota(jnp.int32, lts.shape, 1)
            return jnp.where(lane == h, peak + jnp.log(floored), lts)

        lts = lax.fori_loop(
            0, heads, head, jnp.full((count, HD), negative_fill, jnp.float32)
        )
        lt_ref[:count, :] = lts
        if count < rows:
            part_ref[count:, :] = jnp.zeros((rows - count, part_ref.shape[1]), jnp.float32)
            lt_ref[count:, :] = jnp.full((rows - count, HD), negative_fill, jnp.float32)

    half = rows // 2
    mine = True if own else start < length
    for masked in (False, True):
        case = jnp.logical_and(mine, jnp.logical_not(full) if masked else full)
        for count in (half, rows):
            few = live_nodes <= half
            pick = jnp.logical_and(case, few if count == half else jnp.logical_not(few))
            pl.when(pick)(functools.partial(compute, own, masked, count))

    if not own:

        @pl.when(start >= length)
        def _():
            part_ref[...] = jnp.zeros_like(part_ref)
            lt_ref[...] = jnp.full_like(lt_ref, negative_fill)


def attend_group(info, query_block, keys_t, values, tree_keys_t, tree_values, tree_mask, shift):
    rows, width = query_block.shape
    heads = width // HD
    vmem = pl.BlockSpec(memory_space=pltpu.VMEM)
    return pl.pallas_call(
        functools.partial(group_kernel, scale=1.0 / math.sqrt(HD), shift=shift),
        out_shape=(
            jax.ShapeDtypeStruct((rows, width), jnp.float32),
            jax.ShapeDtypeStruct((rows, HD), jnp.float32),
        ),
        in_specs=[pl.BlockSpec(memory_space=pltpu.SMEM)] + [vmem] * 6,
        out_specs=(vmem, vmem),
    )(info, query_block, keys_t, values, tree_keys_t, tree_values, tree_mask)


def body(
    queries, cache_keys, cache_values, tree_keys, tree_values, parents, tree_sizes, cache_lens
):
    group_size = NH // KVH
    softmax_scale = 1.0 / math.sqrt(HD)
    request = lax.axis_index("rh")
    quarter = lax.axis_index("rl")
    n_lo = lax.axis_size("rl")
    n_hi = lax.axis_size("rh")
    cache_block = cache_keys.shape[1]
    kv_local = cache_keys.shape[2] // HD
    heads_local = kv_local * group_size
    node_count = parents.shape[1]
    rows_owned = tree_keys.shape[0]

    n_head = lax.axis_size("head")
    width = queries.shape[1] // n_head
    sliced = queries.reshape(queries.shape[0], n_head, width).transpose(1, 0, 2)
    sliced = jnp.broadcast_to(sliced[None], (n_lo,) + sliced.shape)
    sliced = sliced.reshape(n_lo * n_head, queries.shape[0], width)
    query_block = lax.all_to_all(sliced, ("rl", "head"), split_axis=0, concat_axis=0, tiled=True)
    query_block = query_block.reshape(node_count, width)

    reached = ancestry(parents)
    ancestors = lax.dynamic_index_in_dim(reached, request, 0, keepdims=False)
    ancestors = lax.dynamic_slice_in_dim(ancestors, quarter * rows_owned, rows_owned, 1)
    tree_mask = ancestors.astype(jnp.float32)
    length = lax.dynamic_index_in_dim(cache_lens, request, 0, keepdims=False)
    live_size = lax.dynamic_index_in_dim(tree_sizes, request, 0, keepdims=False)
    keys_t = cache_keys.transpose(0, 2, 1)
    tree_keys_t = tree_keys.T

    info = jnp.stack([length, request, quarter, n_lo, live_size, n_hi]).astype(jnp.int32)

    def run_group(shift, block_keys_t, block_values):
        part, lt = attend_group(
            info, query_block, block_keys_t, block_values, tree_keys_t, tree_values, tree_mask, shift
        )
        return part, lt[:, :heads_local]

    query_block, keys_t, values_all = lax.optimization_barrier((query_block, keys_t, cache_values))
    results = [
        run_group(
            0,
            lax.dynamic_index_in_dim(keys_t, request, 0, keepdims=False),
            lax.dynamic_index_in_dim(values_all, request, 0, keepdims=False),
        )
    ]
    for shift in range(1, n_hi):
        target = (request + shift) % n_hi
        pairs = [(i, (i + shift) % n_hi) for i in range(n_hi)]
        got_keys_t, got_values = lax.ppermute(
            (
                lax.dynamic_index_in_dim(keys_t, target, 0, keepdims=False),
                lax.dynamic_index_in_dim(values_all, target, 0, keepdims=False),
            ),
            "rh",
            pairs,
        )
        results.append(run_group(shift, got_keys_t, got_values))

    parts = jnp.stack([r[0] for r in results])
    lts = jnp.stack([r[1] for r in results])
    top = jnp.max(lts, axis=0)
    weights = jnp.exp(lts - top)
    den = jnp.sum(weights, axis=0)
    acc = jnp.sum(
        jnp.repeat(weights, HD, axis=2) * parts, axis=0
    )

    payload = jnp.concatenate([acc, den, top], axis=1).reshape(n_lo, rows_owned, heads_local * HD + 2 * heads_local)
    gathered = lax.all_to_all(payload, "rl", split_axis=0, concat_axis=0, tiled=True)
    got_acc = gathered[:, :, : heads_local * HD].reshape(n_lo, rows_owned, heads_local, HD)
    got_den = gathered[:, :, heads_local * HD : heads_local * HD + heads_local]
    got_top = gathered[:, :, heads_local * HD + heads_local :]
    highest = jnp.max(got_top, axis=0)
    scale = jnp.exp(got_top - highest)
    num = jnp.sum(scale[..., None] * got_acc, axis=0)
    total = jnp.sum(scale * got_den, axis=0)
    merged = (num / total[..., None]).reshape(rows_owned, heads_local * HD)

    row_nodes = quarter * rows_owned + jnp.arange(rows_owned, dtype=jnp.int32)
    live_rows = row_nodes < live_size
    return jnp.where(live_rows[:, None], merged, 0.0).astype(jnp.bfloat16)


def solution(mesh):
    def run(queries, cache_keys, cache_values, tree_keys, tree_values, parents, tree_sizes, cache_lens):
        n_hi = cache_keys.shape[0]
        n_lo = mesh.shape["req"] // n_hi
        split = Mesh(mesh.devices.reshape(n_hi, n_lo, mesh.shape["head"]), ("rh", "rl", "head"))
        rows = ("rh", "rl")
        placed = (
            P(("rh", "rl", "head"), None),
            P(None, rows, "head"),
            P(None, rows, "head"),
            P(rows, "head"),
            P(rows, "head"),
            P(),
            P(),
            P(),
        )
        return jax.shard_map(
            body, mesh=split, in_specs=placed, out_specs=P(rows, "head"), check_vma=False
        )(queries, cache_keys, cache_values, tree_keys, tree_values, parents, tree_sizes, cache_lens)

    return run
```

```python
import functools
import math

import jax
import jax.numpy as jnp
from jax import lax
from jax.experimental import pallas as pl
from jax.experimental.pallas import tpu as pltpu
from jax.sharding import Mesh
from jax.sharding import PartitionSpec as P

NH = 128
KVH = 8
HD = 128


negative_fill = -1e30


def ancestry(parents):
    node_count = parents.shape[1]
    node_ids = jnp.arange(node_count, dtype=jnp.int32)
    linked = jnp.logical_or(
        parents[:, :, None] == node_ids[None, None, :], node_ids[:, None] == node_ids[None, :]
    )
    reached = linked.astype(jnp.bfloat16)
    for doubling in range((node_count - 1).bit_length()):
        squared = jnp.einsum("aij,ajk->aik", reached, reached, preferred_element_type=jnp.float32)
        reached = jnp.minimum(squared, 1.0).astype(jnp.bfloat16)
    return reached


def attend_kernel(
    info_ref, q_ref, kt_ref, v_ref, tkt_ref, tv_ref, tmask_ref, acc_ref, top_ref, den_ref, *, scale
):
    s = pl.program_id(0)
    length = info_ref[0]
    request = info_ref[1]
    quarter = info_ref[2]
    n_lo = info_ref[3]
    live_nodes = info_ref[4]
    rows = q_ref.shape[0]
    heads = q_ref.shape[1] // HD
    block_len = kt_ref.shape[1]
    start = (s * n_lo + quarter) * block_len
    full = start + block_len <= length

    @pl.when(s == 0)
    def _():
        acc_ref[...] = jnp.zeros_like(acc_ref)
        top_ref[...] = jnp.full_like(top_ref, negative_fill)
        den_ref[...] = jnp.zeros_like(den_ref)

    def group(with_tree, masked, count):
        def head(h, carry):
            col = pl.multiple_of(h * HD, HD)
            qh = q_ref[:count, pl.ds(col, HD)]
            sc = jnp.dot(qh, kt_ref[...], preferred_element_type=jnp.float32) * scale
            if masked:
                pos = start + lax.broadcasted_iota(jnp.int32, sc.shape, 1)
                live = pos < length
                sc = jnp.where(live, sc, negative_fill)
            peak = jnp.max(sc, axis=1, keepdims=True)
            if with_tree:
                st = jnp.dot(qh, tkt_ref[...], preferred_element_type=jnp.float32) * scale
                tlive = tmask_ref[:count, :] > 0.5
                st = jnp.where(tlive, st, negative_fill)
                peak = jnp.maximum(peak, jnp.max(st, axis=1, keepdims=True))
            w = jnp.exp(sc - peak)
            if masked:
                w = jnp.where(live, w, 0.0)
            tot = jnp.sum(w, axis=1, keepdims=True)
            gs = jnp.dot(w.astype(jnp.bfloat16), v_ref[...], preferred_element_type=jnp.float32)
            if with_tree:
                wt = jnp.where(tlive, jnp.exp(st - peak), 0.0)
                tot = tot + jnp.sum(wt, axis=1, keepdims=True)
                gs = gs + jnp.dot(
                    wt.astype(jnp.bfloat16), tv_ref[...], preferred_element_type=jnp.float32
                )
            floored = jnp.maximum(tot, 1.0)
            part = gs / floored
            lt = peak + jnp.log(floored)
            old = top_ref[h, :count, :][:, :1]
            new = jnp.maximum(old, lt)
            keep = jnp.exp(old - new)
            add = jnp.exp(lt - new)
            acc_ref[:count, pl.ds(col, HD)] = (
                keep * acc_ref[:count, pl.ds(col, HD)] + add * part
            )
            den_ref[h, :count, :] = jnp.broadcast_to(
                keep * den_ref[h, :count, :][:, :1] + add, (count, HD)
            )
            top_ref[h, :count, :] = jnp.broadcast_to(new, (count, HD))
            return carry

        lax.fori_loop(0, heads, head, 0)

    half = rows // 2
    for with_tree in (True, False):
        mine = s == request if with_tree else jnp.logical_and(s != request, start < length)
        for masked in (False, True):
            case = jnp.logical_and(mine, jnp.logical_not(full) if masked else full)
            for count in (half, rows):
                few = live_nodes <= half
                pick = jnp.logical_and(case, few if count == half else jnp.logical_not(few))
                pl.when(pick)(functools.partial(group, with_tree, masked, count))


def attend(info, query_block, keys_t, values, tree_keys_t, tree_values, tree_mask):
    rows, width = query_block.shape
    heads = width // HD
    n_groups, _, block_len = keys_t.shape
    tree_rows = tree_values.shape[0]
    stats = jax.ShapeDtypeStruct((heads, rows, HD), jnp.float32)
    return pl.pallas_call(
        functools.partial(attend_kernel, scale=1.0 / math.sqrt(HD)),
        out_shape=(jax.ShapeDtypeStruct((rows, width), jnp.float32), stats, stats),
        grid_spec=pltpu.PrefetchScalarGridSpec(
            num_scalar_prefetch=1,
            grid=(n_groups,),
            in_specs=[
                pl.BlockSpec((rows, width), lambda s, info: (0, 0)),
                pl.BlockSpec((None, HD, block_len), lambda s, info: (s, 0, 0)),
                pl.BlockSpec((None, block_len, HD), lambda s, info: (s, 0, 0)),
                pl.BlockSpec((HD, tree_rows), lambda s, info: (0, 0)),
                pl.BlockSpec((tree_rows, HD), lambda s, info: (0, 0)),
                pl.BlockSpec((rows, tree_rows), lambda s, info: (0, 0)),
            ],
            out_specs=[
                pl.BlockSpec((rows, width), lambda s, info: (0, 0)),
                pl.BlockSpec((heads, rows, HD), lambda s, info: (0, 0, 0)),
                pl.BlockSpec((heads, rows, HD), lambda s, info: (0, 0, 0)),
            ],
        ),
        compiler_params=pltpu.CompilerParams(dimension_semantics=("arbitrary",)),
    )(info, query_block, keys_t, values, tree_keys_t, tree_values, tree_mask)


def exchange_kernel(src_ref, out_ref, slots, send_sem, recv_sem, own_sem, *, n_lo, n_head):
    request = lax.axis_index("rh")
    quarter = lax.axis_index("rl")
    head = lax.axis_index("head")
    me = quarter * n_head + head
    peers = n_lo * n_head
    mesh = pl.DeviceIdType.MESH

    barrier = pltpu.get_barrier_semaphore()
    for d in range(peers):
        dest = (request, d // n_head, d % n_head)

        @pl.when(d != me)
        def _():
            pl.semaphore_signal(barrier, inc=1, device_id=dest, device_id_type=mesh)

    pl.semaphore_wait(barrier, peers - 1)

    def push(d):
        return pltpu.make_async_remote_copy(
            src_ref.at[d % n_head],
            slots.at[me],
            send_sem.at[d],
            recv_sem.at[me],
            device_id=(request, d // n_head, d % n_head),
            device_id_type=mesh,
        )

    for d in range(peers):
        pl.when(d != me)(push(d).start)
    own = pltpu.make_async_copy(src_ref.at[head], slots.at[me], own_sem)
    own.start()
    own.wait()
    for d in range(peers):
        pl.when(d != me)(push(d).wait_send)
    for s in range(peers):
        arrival = pltpu.make_async_remote_copy(
            src_ref.at[0],
            slots.at[s],
            send_sem.at[s],
            recv_sem.at[s],
            device_id=(request, s // n_head, s % n_head),
            device_id_type=mesh,
        )
        pl.when(s != me)(arrival.wait_recv)
    out_ref[...] = slots[...]


def exchange_queries(pieces, n_lo, n_head):
    peers = n_lo * n_head
    shape = (peers,) + pieces.shape[1:]
    vmem = pl.BlockSpec(memory_space=pltpu.VMEM)
    return pl.pallas_call(
        functools.partial(exchange_kernel, n_lo=n_lo, n_head=n_head),
        out_shape=jax.ShapeDtypeStruct(shape, pieces.dtype),
        in_specs=[vmem],
        out_specs=vmem,
        scratch_shapes=[
            pltpu.VMEM(shape, pieces.dtype),
            pltpu.SemaphoreType.DMA((peers,)),
            pltpu.SemaphoreType.DMA((peers,)),
            pltpu.SemaphoreType.DMA(()),
        ],
        compiler_params=pltpu.CompilerParams(collective_id=0, has_side_effects=True),
    )(pieces)


def body(
    queries, cache_keys, cache_values, tree_keys, tree_values, parents, tree_sizes, cache_lens
):
    group_size = NH // KVH
    softmax_scale = 1.0 / math.sqrt(HD)
    request = lax.axis_index("rh")
    quarter = lax.axis_index("rl")
    n_lo = lax.axis_size("rl")
    n_hi = lax.axis_size("rh")
    cache_block = cache_keys.shape[1]
    kv_local = cache_keys.shape[2] // HD
    heads_local = kv_local * group_size
    node_count = parents.shape[1]
    rows_owned = tree_keys.shape[0]

    n_head = lax.axis_size("head")
    width = queries.shape[1] // n_head
    pieces = queries.reshape(queries.shape[0], n_head, width // HD, HD).transpose(1, 0, 2, 3)
    pieces = pieces.reshape(n_head, queries.shape[0] * width // HD, HD)
    query_block = exchange_queries(pieces, n_lo, n_head)
    query_block = query_block.reshape(node_count, width)

    both = jnp.concatenate([cache_keys, cache_values], axis=2)
    mine = lax.all_to_all(both, "rh", split_axis=0, concat_axis=1, tiled=True)[0]

    reached = ancestry(parents)
    ancestors = lax.dynamic_index_in_dim(reached, request, 0, keepdims=False)
    ancestors = lax.dynamic_slice_in_dim(ancestors, quarter * rows_owned, rows_owned, 1)
    tree_mask = ancestors.astype(jnp.float32)
    length = lax.dynamic_index_in_dim(cache_lens, request, 0, keepdims=False)
    live_size = lax.dynamic_index_in_dim(tree_sizes, request, 0, keepdims=False)
    info = jnp.stack([length, request, quarter, n_lo, live_size]).astype(jnp.int32)
    mine = mine.reshape(n_hi, cache_block, 2 * HD)
    keys_t = mine[:, :, :HD].transpose(0, 2, 1)
    values = mine[:, :, HD:]
    acc, top, den = attend(info, query_block, keys_t, values, tree_keys.T, tree_values, tree_mask)
    top = top[:, :, 0].T
    den = den[:, :, 0].T

    payload = jnp.concatenate([acc, den, top], axis=1).reshape(n_lo, rows_owned, heads_local * HD + 2 * heads_local)
    gathered = lax.all_to_all(payload, "rl", split_axis=0, concat_axis=0, tiled=True)
    got_acc = gathered[:, :, : heads_local * HD].reshape(n_lo, rows_owned, heads_local, HD)
    got_den = gathered[:, :, heads_local * HD : heads_local * HD + heads_local]
    got_top = gathered[:, :, heads_local * HD + heads_local :]
    highest = jnp.max(got_top, axis=0)
    scale = jnp.exp(got_top - highest)
    num = jnp.sum(scale[..., None] * got_acc, axis=0)
    total = jnp.sum(scale * got_den, axis=0)
    merged = (num / total[..., None]).reshape(rows_owned, heads_local * HD)

    row_nodes = quarter * rows_owned + jnp.arange(rows_owned, dtype=jnp.int32)
    live_rows = row_nodes < live_size
    return jnp.where(live_rows[:, None], merged, 0.0).astype(jnp.bfloat16)


def solution(mesh):
    def run(queries, cache_keys, cache_values, tree_keys, tree_values, parents, tree_sizes, cache_lens):
        n_hi = cache_keys.shape[0]
        n_lo = mesh.shape["req"] // n_hi
        split = Mesh(mesh.devices.reshape(n_hi, n_lo, mesh.shape["head"]), ("rh", "rl", "head"))
        rows = ("rh", "rl")
        placed = (
            P(("rh", "rl", "head"), None),
            P(None, rows, "head"),
            P(None, rows, "head"),
            P(rows, "head"),
            P(rows, "head"),
            P(),
            P(),
            P(),
        )
        return jax.shard_map(
            body, mesh=split, in_specs=placed, out_specs=P(rows, "head"), check_vma=False
        )(queries, cache_keys, cache_values, tree_keys, tree_values, parents, tree_sizes, cache_lens)

    return run
```

```python
import functools
import math

import jax
import jax.numpy as jnp
from jax import lax
from jax.experimental import pallas as pl
from jax.experimental.pallas import tpu as pltpu
from jax.sharding import Mesh
from jax.sharding import PartitionSpec as P

NH = 128
KVH = 8
HD = 128


negative_fill = -1e30


def ancestry(parents):
    node_count = parents.shape[1]
    node_ids = jnp.arange(node_count, dtype=jnp.int32)
    linked = jnp.logical_or(
        parents[:, :, None] == node_ids[None, None, :], node_ids[:, None] == node_ids[None, :]
    )
    reached = linked.astype(jnp.bfloat16)
    for doubling in range((node_count - 1).bit_length()):
        squared = jnp.einsum("aij,ajk->aik", reached, reached, preferred_element_type=jnp.float32)
        reached = jnp.minimum(squared, 1.0).astype(jnp.bfloat16)
    return reached


def attend_kernel(
    info_ref, q_ref, kt_hbm, v_hbm, tkt_ref, tv_ref, tmask_ref, acc_ref, top_ref, den_ref,
    kslots, vslots, send_sem, recv_sem, own_sem, *, scale, n_hi,
):
    request = lax.axis_index("rh")
    quarter = lax.axis_index("rl")
    head_axis = lax.axis_index("head")
    mesh = pl.DeviceIdType.MESH
    length = info_ref[0]
    n_lo = info_ref[1]
    rows = q_ref.shape[0]
    heads = q_ref.shape[1] // HD
    block_len = kt_hbm.shape[2]

    barrier = pltpu.get_barrier_semaphore()
    for t in range(n_hi):

        @pl.when(t != request)
        def _():
            pl.semaphore_signal(
                barrier, inc=1, device_id=(t, quarter, head_axis), device_id_type=mesh
            )

    pl.semaphore_wait(barrier, n_hi - 1)

    def pushes(t):
        dest = (t, quarter, head_axis)
        return (
            pltpu.make_async_remote_copy(
                kt_hbm.at[t], kslots.at[request], send_sem.at[t, 0], recv_sem.at[request, 0],
                device_id=dest, device_id_type=mesh,
            ),
            pltpu.make_async_remote_copy(
                v_hbm.at[t], vslots.at[request], send_sem.at[t, 1], recv_sem.at[request, 1],
                device_id=dest, device_id_type=mesh,
            ),
        )

    for shift in range(1, n_hi):
        t = lax.rem(request + shift, n_hi)
        for copy in pushes(t):
            copy.start()
    own_k = pltpu.make_async_copy(kt_hbm.at[request], kslots.at[request], own_sem.at[0])
    own_v = pltpu.make_async_copy(v_hbm.at[request], vslots.at[request], own_sem.at[1])
    own_k.start()
    own_v.start()

    acc_ref[...] = jnp.zeros_like(acc_ref)
    top_ref[...] = jnp.full_like(top_ref, negative_fill)
    den_ref[...] = jnp.zeros_like(den_ref)

    def group(s, with_tree):
        start = (s * n_lo + quarter) * block_len
        kt_ref = kslots.at[s]
        v_ref = vslots.at[s]

        def head(h, carry):
            col = pl.multiple_of(h * HD, HD)
            qh = q_ref[:, pl.ds(col, HD)]
            sc = jnp.dot(qh, kt_ref[...], preferred_element_type=jnp.float32) * scale
            pos = start + lax.broadcasted_iota(jnp.int32, sc.shape, 1)
            live = pos < length
            sc = jnp.where(live, sc, negative_fill)
            peak = jnp.max(sc, axis=1, keepdims=True)
            if with_tree:
                st = jnp.dot(qh, tkt_ref[...], preferred_element_type=jnp.float32) * scale
                tlive = tmask_ref[...] > 0.5
                st = jnp.where(tlive, st, negative_fill)
                peak = jnp.maximum(peak, jnp.max(st, axis=1, keepdims=True))
            w = jnp.where(live, jnp.exp(sc - peak), 0.0)
            tot = jnp.sum(w, axis=1, keepdims=True)
            gs = jnp.dot(w.astype(jnp.bfloat16), v_ref[...], preferred_element_type=jnp.float32)
            if with_tree:
                wt = jnp.where(tlive, jnp.exp(st - peak), 0.0)
                tot = tot + jnp.sum(wt, axis=1, keepdims=True)
                gs = gs + jnp.dot(
                    wt.astype(jnp.bfloat16), tv_ref[...], preferred_element_type=jnp.float32
                )
            floored = jnp.maximum(tot, 1.0)
            part = gs / floored
            lt = peak + jnp.log(floored)
            old = top_ref[h][:, :1]
            new = jnp.maximum(old, lt)
            keep = jnp.exp(old - new)
            add = jnp.exp(lt - new)
            acc_ref[:, pl.ds(col, HD)] = keep * acc_ref[:, pl.ds(col, HD)] + add * part
            den_ref[h] = jnp.broadcast_to(keep * den_ref[h][:, :1] + add, (rows, HD))
            top_ref[h] = jnp.broadcast_to(new, (rows, HD))
            return carry

        lax.fori_loop(0, heads, head, 0)

    own_k.wait()
    own_v.wait()
    group(request, True)

    def landed(s):
        source = (s, quarter, head_axis)
        return (
            pltpu.make_async_remote_copy(
                kt_hbm.at[s], kslots.at[s], send_sem.at[s, 0], recv_sem.at[s, 0],
                device_id=source, device_id_type=mesh,
            ),
            pltpu.make_async_remote_copy(
                v_hbm.at[s], vslots.at[s], send_sem.at[s, 1], recv_sem.at[s, 1],
                device_id=source, device_id_type=mesh,
            ),
        )

    def arrival(step, carry):
        s = lax.rem(request - step - 1 + n_hi, n_hi)
        for copy in landed(s):
            copy.wait_recv()
        group(s, False)
        return carry

    lax.fori_loop(0, n_hi - 1, arrival, 0)
    for shift in range(1, n_hi):
        t = lax.rem(request + shift, n_hi)
        for copy in pushes(t):
            copy.wait_send()


def attend(info, query_block, keys_t, values, tree_keys_t, tree_values, tree_mask):
    rows, width = query_block.shape
    heads = width // HD
    n_hi = keys_t.shape[0]
    stats = jax.ShapeDtypeStruct((heads, rows, HD), jnp.float32)
    vmem = pl.BlockSpec(memory_space=pltpu.VMEM)
    hbm = pl.BlockSpec(memory_space=pl.ANY)
    return pl.pallas_call(
        functools.partial(attend_kernel, scale=1.0 / math.sqrt(HD), n_hi=n_hi),
        out_shape=(jax.ShapeDtypeStruct((rows, width), jnp.float32), stats, stats),
        in_specs=[pl.BlockSpec(memory_space=pltpu.SMEM), vmem, hbm, hbm, vmem, vmem, vmem],
        out_specs=(vmem, vmem, vmem),
        scratch_shapes=[
            pltpu.VMEM(keys_t.shape, keys_t.dtype),
            pltpu.VMEM(values.shape, values.dtype),
            pltpu.SemaphoreType.DMA((n_hi, 2)),
            pltpu.SemaphoreType.DMA((n_hi, 2)),
            pltpu.SemaphoreType.DMA((2,)),
        ],
        compiler_params=pltpu.CompilerParams(
            collective_id=1, has_side_effects=True, vmem_limit_bytes=48 * 1024 * 1024
        ),
    )(info, query_block, keys_t, values, tree_keys_t, tree_values, tree_mask)


def exchange_kernel(src_ref, out_ref, slots, send_sem, recv_sem, own_sem, *, n_lo, n_head):
    request = lax.axis_index("rh")
    quarter = lax.axis_index("rl")
    head = lax.axis_index("head")
    me = quarter * n_head + head
    peers = n_lo * n_head
    mesh = pl.DeviceIdType.MESH

    barrier = pltpu.get_barrier_semaphore()
    for d in range(peers):
        dest = (request, d // n_head, d % n_head)

        @pl.when(d != me)
        def _():
            pl.semaphore_signal(barrier, inc=1, device_id=dest, device_id_type=mesh)

    pl.semaphore_wait(barrier, peers - 1)

    def push(d):
        return pltpu.make_async_remote_copy(
            src_ref.at[d % n_head],
            slots.at[me],
            send_sem.at[d],
            recv_sem.at[me],
            device_id=(request, d // n_head, d % n_head),
            device_id_type=mesh,
        )

    for d in range(peers):
        pl.when(d != me)(push(d).start)
    own = pltpu.make_async_copy(src_ref.at[head], slots.at[me], own_sem)
    own.start()
    own.wait()
    for d in range(peers):
        pl.when(d != me)(push(d).wait_send)
    for s in range(peers):
        arrival = pltpu.make_async_remote_copy(
            src_ref.at[0],
            slots.at[s],
            send_sem.at[s],
            recv_sem.at[s],
            device_id=(request, s // n_head, s % n_head),
            device_id_type=mesh,
        )
        pl.when(s != me)(arrival.wait_recv)
    out_ref[...] = slots[...]


def exchange_queries(pieces, n_lo, n_head):
    peers = n_lo * n_head
    shape = (peers,) + pieces.shape[1:]
    vmem = pl.BlockSpec(memory_space=pltpu.VMEM)
    return pl.pallas_call(
        functools.partial(exchange_kernel, n_lo=n_lo, n_head=n_head),
        out_shape=jax.ShapeDtypeStruct(shape, pieces.dtype),
        in_specs=[vmem],
        out_specs=vmem,
        scratch_shapes=[
            pltpu.VMEM(shape, pieces.dtype),
            pltpu.SemaphoreType.DMA((peers,)),
            pltpu.SemaphoreType.DMA((peers,)),
            pltpu.SemaphoreType.DMA(()),
        ],
        compiler_params=pltpu.CompilerParams(collective_id=0, has_side_effects=True),
    )(pieces)


def body(
    queries, cache_keys, cache_values, tree_keys, tree_values, parents, tree_sizes, cache_lens
):
    group_size = NH // KVH
    softmax_scale = 1.0 / math.sqrt(HD)
    request = lax.axis_index("rh")
    quarter = lax.axis_index("rl")
    n_lo = lax.axis_size("rl")
    n_hi = lax.axis_size("rh")
    cache_block = cache_keys.shape[1]
    kv_local = cache_keys.shape[2] // HD
    heads_local = kv_local * group_size
    node_count = parents.shape[1]
    rows_owned = tree_keys.shape[0]

    n_head = lax.axis_size("head")
    width = queries.shape[1] // n_head
    pieces = queries.reshape(queries.shape[0], n_head, width // HD, HD).transpose(1, 0, 2, 3)
    pieces = pieces.reshape(n_head, queries.shape[0] * width // HD, HD)
    query_block = exchange_queries(pieces, n_lo, n_head)
    query_block = query_block.reshape(node_count, width)

    reached = ancestry(parents)
    ancestors = lax.dynamic_index_in_dim(reached, request, 0, keepdims=False)
    ancestors = lax.dynamic_slice_in_dim(ancestors, quarter * rows_owned, rows_owned, 1)
    tree_mask = ancestors.astype(jnp.float32)
    length = lax.dynamic_index_in_dim(cache_lens, request, 0, keepdims=False)
    live_size = lax.dynamic_index_in_dim(tree_sizes, request, 0, keepdims=False)
    info = jnp.stack([length, jnp.int32(n_lo)]).astype(jnp.int32)
    keys_t = cache_keys.transpose(0, 2, 1)
    acc, top, den = attend(info, query_block, keys_t, cache_values, tree_keys.T, tree_values, tree_mask)
    top = top[:, :, 0].T
    den = den[:, :, 0].T

    payload = jnp.concatenate([acc, den, top], axis=1).reshape(n_lo, rows_owned, heads_local * HD + 2 * heads_local)
    gathered = lax.all_to_all(payload, "rl", split_axis=0, concat_axis=0, tiled=True)
    got_acc = gathered[:, :, : heads_local * HD].reshape(n_lo, rows_owned, heads_local, HD)
    got_den = gathered[:, :, heads_local * HD : heads_local * HD + heads_local]
    got_top = gathered[:, :, heads_local * HD + heads_local :]
    highest = jnp.max(got_top, axis=0)
    scale = jnp.exp(got_top - highest)
    num = jnp.sum(scale[..., None] * got_acc, axis=0)
    total = jnp.sum(scale * got_den, axis=0)
    merged = (num / total[..., None]).reshape(rows_owned, heads_local * HD)

    row_nodes = quarter * rows_owned + jnp.arange(rows_owned, dtype=jnp.int32)
    live_rows = row_nodes < live_size
    return jnp.where(live_rows[:, None], merged, 0.0).astype(jnp.bfloat16)


def solution(mesh):
    def run(queries, cache_keys, cache_values, tree_keys, tree_values, parents, tree_sizes, cache_lens):
        n_hi = cache_keys.shape[0]
        n_lo = mesh.shape["req"] // n_hi
        split = Mesh(mesh.devices.reshape(n_hi, n_lo, mesh.shape["head"]), ("rh", "rl", "head"))
        rows = ("rh", "rl")
        placed = (
            P(("rh", "rl", "head"), None),
            P(None, rows, "head"),
            P(None, rows, "head"),
            P(rows, "head"),
            P(rows, "head"),
            P(),
            P(),
            P(),
        )
        return jax.shard_map(
            body, mesh=split, in_specs=placed, out_specs=P(rows, "head"), check_vma=False
        )(queries, cache_keys, cache_values, tree_keys, tree_values, parents, tree_sizes, cache_lens)

    return run
```

```python
import functools
import math

import jax
import jax.numpy as jnp
from jax import lax
from jax.experimental import pallas as pl
from jax.experimental.pallas import tpu as pltpu
from jax.sharding import Mesh
from jax.sharding import PartitionSpec as P

NH = 128
KVH = 8
HD = 128


negative_fill = -1e30


def ancestry(parents):
    node_count = parents.shape[1]
    node_ids = jnp.arange(node_count, dtype=jnp.int32)
    linked = jnp.logical_or(
        parents[:, :, None] == node_ids[None, None, :], node_ids[:, None] == node_ids[None, :]
    )
    reached = linked.astype(jnp.bfloat16)
    for doubling in range((node_count - 1).bit_length()):
        squared = jnp.einsum("aij,ajk->aik", reached, reached, preferred_element_type=jnp.float32)
        reached = jnp.minimum(squared, 1.0).astype(jnp.bfloat16)
    return reached


def attend_kernel(
    info_ref, q_ref, kt_hbm, v_hbm, tkt_ref, tv_ref, tmask_ref, acc_out, stat_out,
    kslots, vslots, send_sem, recv_sem, own_sem, acc_ref, top_ref, den_ref, stats,
    acc_slots, stat_slots, fsend, frecv, fown, *, scale, n_hi, n_quarters,
):
    request = lax.axis_index("rh")
    quarter = lax.axis_index("rl")
    head_axis = lax.axis_index("head")
    mesh = pl.DeviceIdType.MESH
    length = info_ref[0]
    n_lo = info_ref[1]
    rows = q_ref.shape[0]
    heads = q_ref.shape[1] // HD
    block_len = kt_hbm.shape[2]

    barrier = pltpu.get_barrier_semaphore()
    for t in range(n_hi):

        @pl.when(t != request)
        def _():
            pl.semaphore_signal(
                barrier, inc=1, device_id=(t, quarter, head_axis), device_id_type=mesh
            )

    for r in range(n_quarters):

        @pl.when(r != quarter)
        def _():
            pl.semaphore_signal(
                barrier, inc=1, device_id=(request, r, head_axis), device_id_type=mesh
            )

    pl.semaphore_wait(barrier, n_hi - 1 + n_quarters - 1)

    def pushes(t):
        dest = (t, quarter, head_axis)
        return (
            pltpu.make_async_remote_copy(
                kt_hbm.at[t], kslots.at[request], send_sem.at[t, 0], recv_sem.at[request, 0],
                device_id=dest, device_id_type=mesh,
            ),
            pltpu.make_async_remote_copy(
                v_hbm.at[t], vslots.at[request], send_sem.at[t, 1], recv_sem.at[request, 1],
                device_id=dest, device_id_type=mesh,
            ),
        )

    for shift in range(1, n_hi):
        t = lax.rem(request + shift, n_hi)
        for copy in pushes(t):
            copy.start()
    own_k = pltpu.make_async_copy(kt_hbm.at[request], kslots.at[request], own_sem.at[0])
    own_v = pltpu.make_async_copy(v_hbm.at[request], vslots.at[request], own_sem.at[1])
    own_k.start()
    own_v.start()

    acc_ref[...] = jnp.zeros_like(acc_ref)
    top_ref[...] = jnp.full_like(top_ref, negative_fill)
    den_ref[...] = jnp.zeros_like(den_ref)

    def group(s, with_tree):
        start = (s * n_lo + quarter) * block_len
        kt_ref = kslots.at[s]
        v_ref = vslots.at[s]

        def head(h, carry):
            col = pl.multiple_of(h * HD, HD)
            qh = q_ref[:, pl.ds(col, HD)]
            sc = jnp.dot(qh, kt_ref[...], preferred_element_type=jnp.float32) * scale
            pos = start + lax.broadcasted_iota(jnp.int32, sc.shape, 1)
            live = pos < length
            sc = jnp.where(live, sc, negative_fill)
            peak = jnp.max(sc, axis=1, keepdims=True)
            if with_tree:
                st = jnp.dot(qh, tkt_ref[...], preferred_element_type=jnp.float32) * scale
                tlive = tmask_ref[...] > 0.5
                st = jnp.where(tlive, st, negative_fill)
                peak = jnp.maximum(peak, jnp.max(st, axis=1, keepdims=True))
            w = jnp.where(live, jnp.exp(sc - peak), 0.0)
            tot = jnp.sum(w, axis=1, keepdims=True)
            gs = jnp.dot(w.astype(jnp.bfloat16), v_ref[...], preferred_element_type=jnp.float32)
            if with_tree:
                wt = jnp.where(tlive, jnp.exp(st - peak), 0.0)
                tot = tot + jnp.sum(wt, axis=1, keepdims=True)
                gs = gs + jnp.dot(
                    wt.astype(jnp.bfloat16), tv_ref[...], preferred_element_type=jnp.float32
                )
            floored = jnp.maximum(tot, 1.0)
            part = gs / floored
            lt = peak + jnp.log(floored)
            old = top_ref[h][:, :1]
            new = jnp.maximum(old, lt)
            keep = jnp.exp(old - new)
            add = jnp.exp(lt - new)
            acc_ref[:, pl.ds(col, HD)] = keep * acc_ref[:, pl.ds(col, HD)] + add * part
            den_ref[h] = jnp.broadcast_to(keep * den_ref[h][:, :1] + add, (rows, HD))
            top_ref[h] = jnp.broadcast_to(new, (rows, HD))
            return carry

        lax.fori_loop(0, heads, head, 0)

    own_k.wait()
    own_v.wait()
    group(request, True)

    def landed(s):
        source = (s, quarter, head_axis)
        return (
            pltpu.make_async_remote_copy(
                kt_hbm.at[s], kslots.at[s], send_sem.at[s, 0], recv_sem.at[s, 0],
                device_id=source, device_id_type=mesh,
            ),
            pltpu.make_async_remote_copy(
                v_hbm.at[s], vslots.at[s], send_sem.at[s, 1], recv_sem.at[s, 1],
                device_id=source, device_id_type=mesh,
            ),
        )

    def arrival(step, carry):
        s = lax.rem(request - step - 1 + n_hi, n_hi)
        for copy in landed(s):
            copy.wait_recv()
        group(s, False)
        return carry

    lax.fori_loop(0, n_hi - 1, arrival, 0)
    for shift in range(1, n_hi):
        t = lax.rem(request + shift, n_hi)
        for copy in pushes(t):
            copy.wait_send()

    lane = lax.broadcasted_iota(jnp.int32, (rows, HD), 1)
    tops = jnp.full((rows, HD), negative_fill, jnp.float32)
    dens = jnp.zeros((rows, HD), jnp.float32)
    for h in range(heads):
        tops = jnp.where(lane == h, top_ref[h], tops)
        dens = jnp.where(lane == h, den_ref[h], dens)
    stats[0] = tops
    stats[1] = dens

    quarter_rows = rows // n_quarters

    def quarter_copies(r, slot, device):
        piece = pl.ds(r * quarter_rows, quarter_rows)
        return (
            pltpu.make_async_remote_copy(
                acc_ref.at[piece, :], acc_slots.at[slot], fsend.at[r, 0], frecv.at[slot, 0],
                device_id=device, device_id_type=mesh,
            ),
            pltpu.make_async_remote_copy(
                stats.at[:, piece, :], stat_slots.at[slot], fsend.at[r, 1], frecv.at[slot, 1],
                device_id=device, device_id_type=mesh,
            ),
        )

    for r in range(n_quarters):
        for copy in quarter_copies(r, quarter, (request, r, head_axis)):
            pl.when(r != quarter)(copy.start)
    mine = pl.ds(pl.multiple_of(quarter * quarter_rows, quarter_rows), quarter_rows)
    keep_acc = pltpu.make_async_copy(acc_ref.at[mine, :], acc_slots.at[quarter], fown.at[0])
    keep_stat = pltpu.make_async_copy(stats.at[:, mine, :], stat_slots.at[quarter], fown.at[1])
    keep_acc.start()
    keep_stat.start()
    keep_acc.wait()
    keep_stat.wait()
    for r in range(n_quarters):
        for copy in quarter_copies(r, r, (request, r, head_axis)):
            pl.when(r != quarter)(copy.wait_recv)
    for r in range(n_quarters):
        for copy in quarter_copies(r, quarter, (request, r, head_axis)):
            pl.when(r != quarter)(copy.wait_send)
    acc_out[...] = acc_slots[...]
    stat_out[...] = stat_slots[...]


def attend(info, query_block, keys_t, values, tree_keys_t, tree_values, tree_mask, n_quarters):
    rows, width = query_block.shape
    heads = width // HD
    n_hi = keys_t.shape[0]
    quarter_rows = rows // n_quarters
    vmem = pl.BlockSpec(memory_space=pltpu.VMEM)
    hbm = pl.BlockSpec(memory_space=pl.ANY)
    acc_shape = (n_quarters, quarter_rows, width)
    stat_shape = (n_quarters, 2, quarter_rows, HD)
    return pl.pallas_call(
        functools.partial(
            attend_kernel, scale=1.0 / math.sqrt(HD), n_hi=n_hi, n_quarters=n_quarters
        ),
        out_shape=(
            jax.ShapeDtypeStruct(acc_shape, jnp.float32),
            jax.ShapeDtypeStruct(stat_shape, jnp.float32),
        ),
        in_specs=[pl.BlockSpec(memory_space=pltpu.SMEM), vmem, hbm, hbm, vmem, vmem, vmem],
        out_specs=(vmem, vmem),
        scratch_shapes=[
            pltpu.VMEM(keys_t.shape, keys_t.dtype),
            pltpu.VMEM(values.shape, values.dtype),
            pltpu.SemaphoreType.DMA((n_hi, 2)),
            pltpu.SemaphoreType.DMA((n_hi, 2)),
            pltpu.SemaphoreType.DMA((2,)),
            pltpu.VMEM((rows, width), jnp.float32),
            pltpu.VMEM((heads, rows, HD), jnp.float32),
            pltpu.VMEM((heads, rows, HD), jnp.float32),
            pltpu.VMEM((2, rows, HD), jnp.float32),
            pltpu.VMEM(acc_shape, jnp.float32),
            pltpu.VMEM(stat_shape, jnp.float32),
            pltpu.SemaphoreType.DMA((n_quarters, 2)),
            pltpu.SemaphoreType.DMA((n_quarters, 2)),
            pltpu.SemaphoreType.DMA((2,)),
        ],
        compiler_params=pltpu.CompilerParams(
            collective_id=1, has_side_effects=True, vmem_limit_bytes=48 * 1024 * 1024
        ),
    )(info, query_block, keys_t, values, tree_keys_t, tree_values, tree_mask)


def exchange_kernel(src_ref, out_ref, slots, send_sem, recv_sem, own_sem, *, n_lo, n_head):
    request = lax.axis_index("rh")
    quarter = lax.axis_index("rl")
    head = lax.axis_index("head")
    me = quarter * n_head + head
    peers = n_lo * n_head
    mesh = pl.DeviceIdType.MESH

    barrier = pltpu.get_barrier_semaphore()
    for d in range(peers):
        dest = (request, d // n_head, d % n_head)

        @pl.when(d != me)
        def _():
            pl.semaphore_signal(barrier, inc=1, device_id=dest, device_id_type=mesh)

    pl.semaphore_wait(barrier, peers - 1)

    def push(d):
        return pltpu.make_async_remote_copy(
            src_ref.at[d % n_head],
            slots.at[me],
            send_sem.at[d],
            recv_sem.at[me],
            device_id=(request, d // n_head, d % n_head),
            device_id_type=mesh,
        )

    for d in range(peers):
        pl.when(d != me)(push(d).start)
    own = pltpu.make_async_copy(src_ref.at[head], slots.at[me], own_sem)
    own.start()
    own.wait()
    for d in range(peers):
        pl.when(d != me)(push(d).wait_send)
    for s in range(peers):
        arrival = pltpu.make_async_remote_copy(
            src_ref.at[0],
            slots.at[s],
            send_sem.at[s],
            recv_sem.at[s],
            device_id=(request, s // n_head, s % n_head),
            device_id_type=mesh,
        )
        pl.when(s != me)(arrival.wait_recv)
    out_ref[...] = slots[...]


def exchange_queries(pieces, n_lo, n_head):
    peers = n_lo * n_head
    shape = (peers,) + pieces.shape[1:]
    vmem = pl.BlockSpec(memory_space=pltpu.VMEM)
    return pl.pallas_call(
        functools.partial(exchange_kernel, n_lo=n_lo, n_head=n_head),
        out_shape=jax.ShapeDtypeStruct(shape, pieces.dtype),
        in_specs=[vmem],
        out_specs=vmem,
        scratch_shapes=[
            pltpu.VMEM(shape, pieces.dtype),
            pltpu.SemaphoreType.DMA((peers,)),
            pltpu.SemaphoreType.DMA((peers,)),
            pltpu.SemaphoreType.DMA(()),
        ],
        compiler_params=pltpu.CompilerParams(collective_id=0, has_side_effects=True),
    )(pieces)


def body(
    queries, cache_keys, cache_values, tree_keys, tree_values, parents, tree_sizes, cache_lens
):
    group_size = NH // KVH
    softmax_scale = 1.0 / math.sqrt(HD)
    request = lax.axis_index("rh")
    quarter = lax.axis_index("rl")
    n_lo = lax.axis_size("rl")
    n_hi = lax.axis_size("rh")
    cache_block = cache_keys.shape[1]
    kv_local = cache_keys.shape[2] // HD
    heads_local = kv_local * group_size
    node_count = parents.shape[1]
    rows_owned = tree_keys.shape[0]

    n_head = lax.axis_size("head")
    width = queries.shape[1] // n_head
    pieces = queries.reshape(queries.shape[0], n_head, width // HD, HD).transpose(1, 0, 2, 3)
    pieces = pieces.reshape(n_head, queries.shape[0] * width // HD, HD)
    query_block = exchange_queries(pieces, n_lo, n_head)
    query_block = query_block.reshape(node_count, width)

    reached = ancestry(parents)
    ancestors = lax.dynamic_index_in_dim(reached, request, 0, keepdims=False)
    ancestors = lax.dynamic_slice_in_dim(ancestors, quarter * rows_owned, rows_owned, 1)
    tree_mask = ancestors.astype(jnp.float32)
    length = lax.dynamic_index_in_dim(cache_lens, request, 0, keepdims=False)
    live_size = lax.dynamic_index_in_dim(tree_sizes, request, 0, keepdims=False)
    info = jnp.stack([length, jnp.int32(n_lo)]).astype(jnp.int32)
    keys_t = cache_keys.transpose(0, 2, 1)
    got_acc, got_stats = attend(
        info, query_block, keys_t, cache_values, tree_keys.T, tree_values, tree_mask, n_lo
    )
    got_acc = got_acc.reshape(n_lo, rows_owned, heads_local, HD)
    got_top = got_stats[:, 0, :, :heads_local]
    got_den = got_stats[:, 1, :, :heads_local]
    highest = jnp.max(got_top, axis=0)
    scale = jnp.exp(got_top - highest)
    num = jnp.sum(scale[..., None] * got_acc, axis=0)
    total = jnp.sum(scale * got_den, axis=0)
    merged = (num / total[..., None]).reshape(rows_owned, heads_local * HD)

    row_nodes = quarter * rows_owned + jnp.arange(rows_owned, dtype=jnp.int32)
    live_rows = row_nodes < live_size
    return jnp.where(live_rows[:, None], merged, 0.0).astype(jnp.bfloat16)


def solution(mesh):
    def run(queries, cache_keys, cache_values, tree_keys, tree_values, parents, tree_sizes, cache_lens):
        n_hi = cache_keys.shape[0]
        n_lo = mesh.shape["req"] // n_hi
        split = Mesh(mesh.devices.reshape(n_hi, n_lo, mesh.shape["head"]), ("rh", "rl", "head"))
        rows = ("rh", "rl")
        placed = (
            P(("rh", "rl", "head"), None),
            P(None, rows, "head"),
            P(None, rows, "head"),
            P(rows, "head"),
            P(rows, "head"),
            P(),
            P(),
            P(),
        )
        return jax.shard_map(
            body, mesh=split, in_specs=placed, out_specs=P(rows, "head"), check_vma=False
        )(queries, cache_keys, cache_values, tree_keys, tree_values, parents, tree_sizes, cache_lens)

    return run
```

```python
import functools
import math

import jax
import jax.numpy as jnp
from jax import lax
from jax.experimental import pallas as pl
from jax.experimental.pallas import tpu as pltpu
from jax.sharding import Mesh
from jax.sharding import PartitionSpec as P

NH = 128
KVH = 8
HD = 128


negative_fill = -1e30


def ancestry(parents):
    node_count = parents.shape[1]
    node_ids = jnp.arange(node_count, dtype=jnp.int32)
    linked = jnp.logical_or(
        parents[:, :, None] == node_ids[None, None, :], node_ids[:, None] == node_ids[None, :]
    )
    reached = linked.astype(jnp.bfloat16)
    for doubling in range((node_count - 1).bit_length()):
        squared = jnp.einsum("aij,ajk->aik", reached, reached, preferred_element_type=jnp.float32)
        reached = jnp.minimum(squared, 1.0).astype(jnp.bfloat16)
    return reached


def attend_kernel(
    info_ref, q_ref, kt_hbm, v_hbm, tkt_ref, tv_ref, tmask_ref, acc_out, stat_out,
    kslots, vslots, send_sem, recv_sem, own_sem, acc_ref, top_ref, den_ref, stats,
    acc_slots, stat_slots, fsend, frecv, fown, *, scale, n_hi, n_quarters,
):
    request = lax.axis_index("rh")
    quarter = lax.axis_index("rl")
    head_axis = lax.axis_index("head")
    mesh = pl.DeviceIdType.MESH
    length = info_ref[0]
    n_lo = info_ref[1]
    rows = q_ref.shape[0]
    heads = q_ref.shape[1] // HD
    block_len = kt_hbm.shape[2]

    barrier = pltpu.get_barrier_semaphore()
    for t in range(n_hi):

        @pl.when(t != request)
        def _():
            pl.semaphore_signal(
                barrier, inc=1, device_id=(t, quarter, head_axis), device_id_type=mesh
            )

    for r in range(n_quarters):

        @pl.when(r != quarter)
        def _():
            pl.semaphore_signal(
                barrier, inc=1, device_id=(request, r, head_axis), device_id_type=mesh
            )

    pl.semaphore_wait(barrier, n_hi - 1 + n_quarters - 1)

    def pushes(t):
        dest = (t, quarter, head_axis)
        return (
            pltpu.make_async_remote_copy(
                kt_hbm.at[t], kslots.at[request], send_sem.at[t, 0], recv_sem.at[request, 0],
                device_id=dest, device_id_type=mesh,
            ),
            pltpu.make_async_remote_copy(
                v_hbm.at[t], vslots.at[request], send_sem.at[t, 1], recv_sem.at[request, 1],
                device_id=dest, device_id_type=mesh,
            ),
        )

    for shift in range(1, n_hi):
        t = lax.rem(request + shift, n_hi)
        for copy in pushes(t):
            copy.start()
    own_k = pltpu.make_async_copy(kt_hbm.at[request], kslots.at[request], own_sem.at[0])
    own_v = pltpu.make_async_copy(v_hbm.at[request], vslots.at[request], own_sem.at[1])
    own_k.start()
    own_v.start()

    acc_ref[...] = jnp.zeros_like(acc_ref)
    top_ref[...] = jnp.full_like(top_ref, negative_fill)
    den_ref[...] = jnp.zeros_like(den_ref)

    def group(s, with_tree):
        start = (s * n_lo + quarter) * block_len
        kt_ref = kslots.at[s]
        v_ref = vslots.at[s]
        pos = start + lax.broadcasted_iota(jnp.int32, (1, block_len), 1)
        bias = jnp.where(pos < length, 0.0, negative_fill)

        def head(h, carry):
            col = pl.multiple_of(h * HD, HD)
            qh = q_ref[:, pl.ds(col, HD)]
            sc = jnp.dot(qh, kt_ref[...], preferred_element_type=jnp.float32) * scale + bias
            peak = jnp.max(sc, axis=1, keepdims=True)
            if with_tree:
                st = jnp.dot(qh, tkt_ref[...], preferred_element_type=jnp.float32) * scale
                tlive = tmask_ref[...] > 0.5
                st = jnp.where(tlive, st, negative_fill)
                peak = jnp.maximum(peak, jnp.max(st, axis=1, keepdims=True))
            w = jnp.exp(sc - jnp.maximum(peak, 0.1 * negative_fill))
            tot = jnp.sum(w, axis=1, keepdims=True)
            gs = jnp.dot(w.astype(jnp.bfloat16), v_ref[...], preferred_element_type=jnp.float32)
            if with_tree:
                wt = jnp.where(tlive, jnp.exp(st - peak), 0.0)
                tot = tot + jnp.sum(wt, axis=1, keepdims=True)
                gs = gs + jnp.dot(
                    wt.astype(jnp.bfloat16), tv_ref[...], preferred_element_type=jnp.float32
                )
            floored = jnp.maximum(tot, 1.0)
            part = gs / floored
            lt = peak + jnp.log(floored)
            old = top_ref[h][:, :1]
            new = jnp.maximum(old, lt)
            keep = jnp.exp(old - new)
            add = jnp.exp(lt - new)
            acc_ref[:, pl.ds(col, HD)] = keep * acc_ref[:, pl.ds(col, HD)] + add * part
            den_ref[h] = jnp.broadcast_to(keep * den_ref[h][:, :1] + add, (rows, HD))
            top_ref[h] = jnp.broadcast_to(new, (rows, HD))
            return carry

        lax.fori_loop(0, heads, head, 0)

    own_k.wait()
    own_v.wait()
    group(request, True)

    def landed(s):
        source = (s, quarter, head_axis)
        return (
            pltpu.make_async_remote_copy(
                kt_hbm.at[s], kslots.at[s], send_sem.at[s, 0], recv_sem.at[s, 0],
                device_id=source, device_id_type=mesh,
            ),
            pltpu.make_async_remote_copy(
                v_hbm.at[s], vslots.at[s], send_sem.at[s, 1], recv_sem.at[s, 1],
                device_id=source, device_id_type=mesh,
            ),
        )

    def arrival(step, carry):
        s = lax.rem(request - step - 1 + n_hi, n_hi)
        for copy in landed(s):
            copy.wait_recv()
        group(s, False)
        return carry

    lax.fori_loop(0, n_hi - 1, arrival, 0)
    for shift in range(1, n_hi):
        t = lax.rem(request + shift, n_hi)
        for copy in pushes(t):
            copy.wait_send()

    lane = lax.broadcasted_iota(jnp.int32, (rows, HD), 1)
    tops = jnp.full((rows, HD), negative_fill, jnp.float32)
    dens = jnp.zeros((rows, HD), jnp.float32)
    for h in range(heads):
        tops = jnp.where(lane == h, top_ref[h], tops)
        dens = jnp.where(lane == h, den_ref[h], dens)
    stats[0] = tops
    stats[1] = dens

    quarter_rows = rows // n_quarters

    def quarter_copies(r, slot, device):
        piece = pl.ds(r * quarter_rows, quarter_rows)
        return (
            pltpu.make_async_remote_copy(
                acc_ref.at[piece, :], acc_slots.at[slot], fsend.at[r, 0], frecv.at[slot, 0],
                device_id=device, device_id_type=mesh,
            ),
            pltpu.make_async_remote_copy(
                stats.at[:, piece, :], stat_slots.at[slot], fsend.at[r, 1], frecv.at[slot, 1],
                device_id=device, device_id_type=mesh,
            ),
        )

    for r in range(n_quarters):
        for copy in quarter_copies(r, quarter, (request, r, head_axis)):
            pl.when(r != quarter)(copy.start)
    mine = pl.ds(pl.multiple_of(quarter * quarter_rows, quarter_rows), quarter_rows)
    keep_acc = pltpu.make_async_copy(acc_ref.at[mine, :], acc_slots.at[quarter], fown.at[0])
    keep_stat = pltpu.make_async_copy(stats.at[:, mine, :], stat_slots.at[quarter], fown.at[1])
    keep_acc.start()
    keep_stat.start()
    keep_acc.wait()
    keep_stat.wait()
    for r in range(n_quarters):
        for copy in quarter_copies(r, r, (request, r, head_axis)):
            pl.when(r != quarter)(copy.wait_recv)
    for r in range(n_quarters):
        for copy in quarter_copies(r, quarter, (request, r, head_axis)):
            pl.when(r != quarter)(copy.wait_send)
    acc_out[...] = acc_slots[...]
    stat_out[...] = stat_slots[...]


def attend(info, query_block, keys_t, values, tree_keys_t, tree_values, tree_mask, n_quarters):
    rows, width = query_block.shape
    heads = width // HD
    n_hi = keys_t.shape[0]
    quarter_rows = rows // n_quarters
    vmem = pl.BlockSpec(memory_space=pltpu.VMEM)
    hbm = pl.BlockSpec(memory_space=pl.ANY)
    acc_shape = (n_quarters, quarter_rows, width)
    stat_shape = (n_quarters, 2, quarter_rows, HD)
    return pl.pallas_call(
        functools.partial(
            attend_kernel, scale=1.0 / math.sqrt(HD), n_hi=n_hi, n_quarters=n_quarters
        ),
        out_shape=(
            jax.ShapeDtypeStruct(acc_shape, jnp.float32),
            jax.ShapeDtypeStruct(stat_shape, jnp.float32),
        ),
        in_specs=[pl.BlockSpec(memory_space=pltpu.SMEM), vmem, hbm, hbm, vmem, vmem, vmem],
        out_specs=(vmem, vmem),
        scratch_shapes=[
            pltpu.VMEM(keys_t.shape, keys_t.dtype),
            pltpu.VMEM(values.shape, values.dtype),
            pltpu.SemaphoreType.DMA((n_hi, 2)),
            pltpu.SemaphoreType.DMA((n_hi, 2)),
            pltpu.SemaphoreType.DMA((2,)),
            pltpu.VMEM((rows, width), jnp.float32),
            pltpu.VMEM((heads, rows, HD), jnp.float32),
            pltpu.VMEM((heads, rows, HD), jnp.float32),
            pltpu.VMEM((2, rows, HD), jnp.float32),
            pltpu.VMEM(acc_shape, jnp.float32),
            pltpu.VMEM(stat_shape, jnp.float32),
            pltpu.SemaphoreType.DMA((n_quarters, 2)),
            pltpu.SemaphoreType.DMA((n_quarters, 2)),
            pltpu.SemaphoreType.DMA((2,)),
        ],
        compiler_params=pltpu.CompilerParams(
            collective_id=1, has_side_effects=True, vmem_limit_bytes=48 * 1024 * 1024
        ),
    )(info, query_block, keys_t, values, tree_keys_t, tree_values, tree_mask)


def exchange_kernel(src_ref, out_ref, slots, send_sem, recv_sem, own_sem, *, n_lo, n_head):
    request = lax.axis_index("rh")
    quarter = lax.axis_index("rl")
    head = lax.axis_index("head")
    me = quarter * n_head + head
    peers = n_lo * n_head
    mesh = pl.DeviceIdType.MESH

    barrier = pltpu.get_barrier_semaphore()
    for d in range(peers):
        dest = (request, d // n_head, d % n_head)

        @pl.when(d != me)
        def _():
            pl.semaphore_signal(barrier, inc=1, device_id=dest, device_id_type=mesh)

    pl.semaphore_wait(barrier, peers - 1)

    def push(d):
        return pltpu.make_async_remote_copy(
            src_ref.at[d % n_head],
            slots.at[me],
            send_sem.at[d],
            recv_sem.at[me],
            device_id=(request, d // n_head, d % n_head),
            device_id_type=mesh,
        )

    for d in range(peers):
        pl.when(d != me)(push(d).start)
    own = pltpu.make_async_copy(src_ref.at[head], slots.at[me], own_sem)
    own.start()
    own.wait()
    for d in range(peers):
        pl.when(d != me)(push(d).wait_send)
    for s in range(peers):
        arrival = pltpu.make_async_remote_copy(
            src_ref.at[0],
            slots.at[s],
            send_sem.at[s],
            recv_sem.at[s],
            device_id=(request, s // n_head, s % n_head),
            device_id_type=mesh,
        )
        pl.when(s != me)(arrival.wait_recv)
    out_ref[...] = slots[...]


def exchange_queries(pieces, n_lo, n_head):
    peers = n_lo * n_head
    shape = (peers,) + pieces.shape[1:]
    vmem = pl.BlockSpec(memory_space=pltpu.VMEM)
    return pl.pallas_call(
        functools.partial(exchange_kernel, n_lo=n_lo, n_head=n_head),
        out_shape=jax.ShapeDtypeStruct(shape, pieces.dtype),
        in_specs=[vmem],
        out_specs=vmem,
        scratch_shapes=[
            pltpu.VMEM(shape, pieces.dtype),
            pltpu.SemaphoreType.DMA((peers,)),
            pltpu.SemaphoreType.DMA((peers,)),
            pltpu.SemaphoreType.DMA(()),
        ],
        compiler_params=pltpu.CompilerParams(collective_id=0, has_side_effects=True),
    )(pieces)


def body(
    queries, cache_keys, cache_values, tree_keys, tree_values, parents, tree_sizes, cache_lens
):
    group_size = NH // KVH
    softmax_scale = 1.0 / math.sqrt(HD)
    request = lax.axis_index("rh")
    quarter = lax.axis_index("rl")
    n_lo = lax.axis_size("rl")
    n_hi = lax.axis_size("rh")
    cache_block = cache_keys.shape[1]
    kv_local = cache_keys.shape[2] // HD
    heads_local = kv_local * group_size
    node_count = parents.shape[1]
    rows_owned = tree_keys.shape[0]

    n_head = lax.axis_size("head")
    width = queries.shape[1] // n_head
    pieces = queries.reshape(queries.shape[0], n_head, width // HD, HD).transpose(1, 0, 2, 3)
    pieces = pieces.reshape(n_head, queries.shape[0] * width // HD, HD)
    query_block = exchange_queries(pieces, n_lo, n_head)
    query_block = query_block.reshape(node_count, width)

    reached = ancestry(parents)
    ancestors = lax.dynamic_index_in_dim(reached, request, 0, keepdims=False)
    ancestors = lax.dynamic_slice_in_dim(ancestors, quarter * rows_owned, rows_owned, 1)
    tree_mask = ancestors.astype(jnp.float32)
    length = lax.dynamic_index_in_dim(cache_lens, request, 0, keepdims=False)
    live_size = lax.dynamic_index_in_dim(tree_sizes, request, 0, keepdims=False)
    info = jnp.stack([length, jnp.int32(n_lo)]).astype(jnp.int32)
    keys_t = cache_keys.transpose(0, 2, 1)
    got_acc, got_stats = attend(
        info, query_block, keys_t, cache_values, tree_keys.T, tree_values, tree_mask, n_lo
    )
    got_acc = got_acc.reshape(n_lo, rows_owned, heads_local, HD)
    got_top = got_stats[:, 0, :, :heads_local]
    got_den = got_stats[:, 1, :, :heads_local]
    highest = jnp.max(got_top, axis=0)
    scale = jnp.exp(got_top - highest)
    num = jnp.sum(scale[..., None] * got_acc, axis=0)
    total = jnp.sum(scale * got_den, axis=0)
    merged = (num / total[..., None]).reshape(rows_owned, heads_local * HD)

    row_nodes = quarter * rows_owned + jnp.arange(rows_owned, dtype=jnp.int32)
    live_rows = row_nodes < live_size
    return jnp.where(live_rows[:, None], merged, 0.0).astype(jnp.bfloat16)


def solution(mesh):
    def run(queries, cache_keys, cache_values, tree_keys, tree_values, parents, tree_sizes, cache_lens):
        n_hi = cache_keys.shape[0]
        n_lo = mesh.shape["req"] // n_hi
        split = Mesh(mesh.devices.reshape(n_hi, n_lo, mesh.shape["head"]), ("rh", "rl", "head"))
        rows = ("rh", "rl")
        placed = (
            P(("rh", "rl", "head"), None),
            P(None, rows, "head"),
            P(None, rows, "head"),
            P(rows, "head"),
            P(rows, "head"),
            P(),
            P(),
            P(),
        )
        return jax.shard_map(
            body, mesh=split, in_specs=placed, out_specs=P(rows, "head"), check_vma=False
        )(queries, cache_keys, cache_values, tree_keys, tree_values, parents, tree_sizes, cache_lens)

    return run
```

```python
import functools
import math

import jax
import jax.numpy as jnp
from jax import lax
from jax.experimental import pallas as pl
from jax.experimental.pallas import tpu as pltpu
from jax.sharding import Mesh
from jax.sharding import PartitionSpec as P

NH = 128
KVH = 8
HD = 128


negative_fill = -1e30


def ancestry(parents):
    node_count = parents.shape[1]
    node_ids = jnp.arange(node_count, dtype=jnp.int32)
    linked = jnp.logical_or(
        parents[:, :, None] == node_ids[None, None, :], node_ids[:, None] == node_ids[None, :]
    )
    reached = linked.astype(jnp.bfloat16)
    for doubling in range((node_count - 1).bit_length()):
        squared = jnp.einsum("aij,ajk->aik", reached, reached, preferred_element_type=jnp.float32)
        reached = jnp.minimum(squared, 1.0).astype(jnp.bfloat16)
    return reached


def attend_kernel(
    info_ref, q_ref, kt_hbm, v_hbm, tkt_ref, tv_ref, tmask_ref, acc_out, stat_out,
    kslots, vslots, send_sem, recv_sem, own_sem, acc_ref, top_ref, den_ref, stats,
    acc_slots, stat_slots, fsend, frecv, fown, *, scale, n_hi, n_quarters,
):
    request = lax.axis_index("rh")
    quarter = lax.axis_index("rl")
    head_axis = lax.axis_index("head")
    mesh = pl.DeviceIdType.MESH
    length = info_ref[0]
    n_lo = info_ref[1]
    rows = q_ref.shape[0]
    heads = q_ref.shape[1] // HD
    block_len = kt_hbm.shape[2]

    barrier = pltpu.get_barrier_semaphore()
    for t in range(n_hi):

        @pl.when(t != request)
        def _():
            pl.semaphore_signal(
                barrier, inc=1, device_id=(t, quarter, head_axis), device_id_type=mesh
            )

    for r in range(n_quarters):

        @pl.when(r != quarter)
        def _():
            pl.semaphore_signal(
                barrier, inc=1, device_id=(request, r, head_axis), device_id_type=mesh
            )

    pl.semaphore_wait(barrier, n_hi - 1 + n_quarters - 1)

    def pushes(t):
        dest = (t, quarter, head_axis)
        return (
            pltpu.make_async_remote_copy(
                kt_hbm.at[t], kslots.at[request], send_sem.at[t, 0], recv_sem.at[request, 0],
                device_id=dest, device_id_type=mesh,
            ),
            pltpu.make_async_remote_copy(
                v_hbm.at[t], vslots.at[request], send_sem.at[t, 1], recv_sem.at[request, 1],
                device_id=dest, device_id_type=mesh,
            ),
        )

    ahead = 2
    for shift in range(1, min(ahead, n_hi - 1) + 1):
        t = lax.rem(request + shift, n_hi)
        for copy in pushes(t):
            copy.start()
    own_k = pltpu.make_async_copy(kt_hbm.at[request], kslots.at[request], own_sem.at[0])
    own_v = pltpu.make_async_copy(v_hbm.at[request], vslots.at[request], own_sem.at[1])
    own_k.start()
    own_v.start()

    acc_ref[...] = jnp.zeros_like(acc_ref)
    top_ref[...] = jnp.full_like(top_ref, negative_fill)
    den_ref[...] = jnp.zeros_like(den_ref)

    def group(s, with_tree):
        start = (s * n_lo + quarter) * block_len
        kt_ref = kslots.at[s]
        v_ref = vslots.at[s]
        pos = start + lax.broadcasted_iota(jnp.int32, (1, block_len), 1)
        bias = jnp.where(pos < length, 0.0, negative_fill)

        def head(h, carry):
            col = pl.multiple_of(h * HD, HD)
            qh = q_ref[:, pl.ds(col, HD)]
            sc = jnp.dot(qh, kt_ref[...], preferred_element_type=jnp.float32) * scale + bias
            peak = jnp.max(sc, axis=1, keepdims=True)
            if with_tree:
                st = jnp.dot(qh, tkt_ref[...], preferred_element_type=jnp.float32) * scale
                tlive = tmask_ref[...] > 0.5
                st = jnp.where(tlive, st, negative_fill)
                peak = jnp.maximum(peak, jnp.max(st, axis=1, keepdims=True))
            w = jnp.exp(sc - jnp.maximum(peak, 0.1 * negative_fill))
            tot = jnp.sum(w, axis=1, keepdims=True)
            gs = jnp.dot(w.astype(jnp.bfloat16), v_ref[...], preferred_element_type=jnp.float32)
            if with_tree:
                wt = jnp.where(tlive, jnp.exp(st - peak), 0.0)
                tot = tot + jnp.sum(wt, axis=1, keepdims=True)
                gs = gs + jnp.dot(
                    wt.astype(jnp.bfloat16), tv_ref[...], preferred_element_type=jnp.float32
                )
            floored = jnp.maximum(tot, 1.0)
            part = gs / floored
            lt = peak + jnp.log(floored)
            old = top_ref[h][:, :1]
            new = jnp.maximum(old, lt)
            keep = jnp.exp(old - new)
            add = jnp.exp(lt - new)
            acc_ref[:, pl.ds(col, HD)] = keep * acc_ref[:, pl.ds(col, HD)] + add * part
            den_ref[h] = jnp.broadcast_to(keep * den_ref[h][:, :1] + add, (rows, HD))
            top_ref[h] = jnp.broadcast_to(new, (rows, HD))
            return carry

        lax.fori_loop(0, heads, head, 0)

    own_k.wait()
    own_v.wait()
    group(request, True)

    def landed(s):
        source = (s, quarter, head_axis)
        return (
            pltpu.make_async_remote_copy(
                kt_hbm.at[s], kslots.at[s], send_sem.at[s, 0], recv_sem.at[s, 0],
                device_id=source, device_id_type=mesh,
            ),
            pltpu.make_async_remote_copy(
                v_hbm.at[s], vslots.at[s], send_sem.at[s, 1], recv_sem.at[s, 1],
                device_id=source, device_id_type=mesh,
            ),
        )

    def arrival(step, carry):
        @pl.when(step + ahead + 1 < n_hi)
        def _():
            t = lax.rem(request + step + ahead + 1, n_hi)
            for copy in pushes(t):
                copy.start()

        s = lax.rem(request - step - 1 + n_hi, n_hi)
        for copy in landed(s):
            copy.wait_recv()
        group(s, False)
        return carry

    lax.fori_loop(0, n_hi - 1, arrival, 0)
    for shift in range(1, n_hi):
        t = lax.rem(request + shift, n_hi)
        for copy in pushes(t):
            copy.wait_send()

    lane = lax.broadcasted_iota(jnp.int32, (rows, HD), 1)
    tops = jnp.full((rows, HD), negative_fill, jnp.float32)
    dens = jnp.zeros((rows, HD), jnp.float32)
    for h in range(heads):
        tops = jnp.where(lane == h, top_ref[h], tops)
        dens = jnp.where(lane == h, den_ref[h], dens)
    stats[0] = tops
    stats[1] = dens

    quarter_rows = rows // n_quarters

    def quarter_copies(r, slot, device):
        piece = pl.ds(r * quarter_rows, quarter_rows)
        return (
            pltpu.make_async_remote_copy(
                acc_ref.at[piece, :], acc_slots.at[slot], fsend.at[r, 0], frecv.at[slot, 0],
                device_id=device, device_id_type=mesh,
            ),
            pltpu.make_async_remote_copy(
                stats.at[:, piece, :], stat_slots.at[slot], fsend.at[r, 1], frecv.at[slot, 1],
                device_id=device, device_id_type=mesh,
            ),
        )

    for r in range(n_quarters):
        for copy in quarter_copies(r, quarter, (request, r, head_axis)):
            pl.when(r != quarter)(copy.start)
    mine = pl.ds(pl.multiple_of(quarter * quarter_rows, quarter_rows), quarter_rows)
    keep_acc = pltpu.make_async_copy(acc_ref.at[mine, :], acc_slots.at[quarter], fown.at[0])
    keep_stat = pltpu.make_async_copy(stats.at[:, mine, :], stat_slots.at[quarter], fown.at[1])
    keep_acc.start()
    keep_stat.start()
    keep_acc.wait()
    keep_stat.wait()
    for r in range(n_quarters):
        for copy in quarter_copies(r, r, (request, r, head_axis)):
            pl.when(r != quarter)(copy.wait_recv)
    for r in range(n_quarters):
        for copy in quarter_copies(r, quarter, (request, r, head_axis)):
            pl.when(r != quarter)(copy.wait_send)
    acc_out[...] = acc_slots[...]
    stat_out[...] = stat_slots[...]


def attend(info, query_block, keys_t, values, tree_keys_t, tree_values, tree_mask, n_quarters):
    rows, width = query_block.shape
    heads = width // HD
    n_hi = keys_t.shape[0]
    quarter_rows = rows // n_quarters
    vmem = pl.BlockSpec(memory_space=pltpu.VMEM)
    hbm = pl.BlockSpec(memory_space=pl.ANY)
    acc_shape = (n_quarters, quarter_rows, width)
    stat_shape = (n_quarters, 2, quarter_rows, HD)
    return pl.pallas_call(
        functools.partial(
            attend_kernel, scale=1.0 / math.sqrt(HD), n_hi=n_hi, n_quarters=n_quarters
        ),
        out_shape=(
            jax.ShapeDtypeStruct(acc_shape, jnp.float32),
            jax.ShapeDtypeStruct(stat_shape, jnp.float32),
        ),
        in_specs=[pl.BlockSpec(memory_space=pltpu.SMEM), vmem, hbm, hbm, vmem, vmem, vmem],
        out_specs=(vmem, vmem),
        scratch_shapes=[
            pltpu.VMEM(keys_t.shape, keys_t.dtype),
            pltpu.VMEM(values.shape, values.dtype),
            pltpu.SemaphoreType.DMA((n_hi, 2)),
            pltpu.SemaphoreType.DMA((n_hi, 2)),
            pltpu.SemaphoreType.DMA((2,)),
            pltpu.VMEM((rows, width), jnp.float32),
            pltpu.VMEM((heads, rows, HD), jnp.float32),
            pltpu.VMEM((heads, rows, HD), jnp.float32),
            pltpu.VMEM((2, rows, HD), jnp.float32),
            pltpu.VMEM(acc_shape, jnp.float32),
            pltpu.VMEM(stat_shape, jnp.float32),
            pltpu.SemaphoreType.DMA((n_quarters, 2)),
            pltpu.SemaphoreType.DMA((n_quarters, 2)),
            pltpu.SemaphoreType.DMA((2,)),
        ],
        compiler_params=pltpu.CompilerParams(
            collective_id=1, has_side_effects=True, vmem_limit_bytes=48 * 1024 * 1024
        ),
    )(info, query_block, keys_t, values, tree_keys_t, tree_values, tree_mask)


def exchange_kernel(src_ref, out_ref, slots, send_sem, recv_sem, own_sem, *, n_lo, n_head):
    request = lax.axis_index("rh")
    quarter = lax.axis_index("rl")
    head = lax.axis_index("head")
    me = quarter * n_head + head
    peers = n_lo * n_head
    mesh = pl.DeviceIdType.MESH

    barrier = pltpu.get_barrier_semaphore()
    for d in range(peers):
        dest = (request, d // n_head, d % n_head)

        @pl.when(d != me)
        def _():
            pl.semaphore_signal(barrier, inc=1, device_id=dest, device_id_type=mesh)

    pl.semaphore_wait(barrier, peers - 1)

    def push(d):
        return pltpu.make_async_remote_copy(
            src_ref.at[d % n_head],
            slots.at[me],
            send_sem.at[d],
            recv_sem.at[me],
            device_id=(request, d // n_head, d % n_head),
            device_id_type=mesh,
        )

    for d in range(peers):
        pl.when(d != me)(push(d).start)
    own = pltpu.make_async_copy(src_ref.at[head], slots.at[me], own_sem)
    own.start()
    own.wait()
    for d in range(peers):
        pl.when(d != me)(push(d).wait_send)
    for s in range(peers):
        arrival = pltpu.make_async_remote_copy(
            src_ref.at[0],
            slots.at[s],
            send_sem.at[s],
            recv_sem.at[s],
            device_id=(request, s // n_head, s % n_head),
            device_id_type=mesh,
        )
        pl.when(s != me)(arrival.wait_recv)
    out_ref[...] = slots[...]


def exchange_queries(pieces, n_lo, n_head):
    peers = n_lo * n_head
    shape = (peers,) + pieces.shape[1:]
    vmem = pl.BlockSpec(memory_space=pltpu.VMEM)
    return pl.pallas_call(
        functools.partial(exchange_kernel, n_lo=n_lo, n_head=n_head),
        out_shape=jax.ShapeDtypeStruct(shape, pieces.dtype),
        in_specs=[vmem],
        out_specs=vmem,
        scratch_shapes=[
            pltpu.VMEM(shape, pieces.dtype),
            pltpu.SemaphoreType.DMA((peers,)),
            pltpu.SemaphoreType.DMA((peers,)),
            pltpu.SemaphoreType.DMA(()),
        ],
        compiler_params=pltpu.CompilerParams(collective_id=0, has_side_effects=True),
    )(pieces)


def body(
    queries, cache_keys, cache_values, tree_keys, tree_values, parents, tree_sizes, cache_lens
):
    group_size = NH // KVH
    softmax_scale = 1.0 / math.sqrt(HD)
    request = lax.axis_index("rh")
    quarter = lax.axis_index("rl")
    n_lo = lax.axis_size("rl")
    n_hi = lax.axis_size("rh")
    cache_block = cache_keys.shape[1]
    kv_local = cache_keys.shape[2] // HD
    heads_local = kv_local * group_size
    node_count = parents.shape[1]
    rows_owned = tree_keys.shape[0]

    n_head = lax.axis_size("head")
    width = queries.shape[1] // n_head
    pieces = queries.reshape(queries.shape[0], n_head, width // HD, HD).transpose(1, 0, 2, 3)
    pieces = pieces.reshape(n_head, queries.shape[0] * width // HD, HD)
    query_block = exchange_queries(pieces, n_lo, n_head)
    query_block = query_block.reshape(node_count, width)

    reached = ancestry(parents)
    ancestors = lax.dynamic_index_in_dim(reached, request, 0, keepdims=False)
    ancestors = lax.dynamic_slice_in_dim(ancestors, quarter * rows_owned, rows_owned, 1)
    tree_mask = ancestors.astype(jnp.float32)
    length = lax.dynamic_index_in_dim(cache_lens, request, 0, keepdims=False)
    live_size = lax.dynamic_index_in_dim(tree_sizes, request, 0, keepdims=False)
    info = jnp.stack([length, jnp.int32(n_lo)]).astype(jnp.int32)
    keys_t = cache_keys.transpose(0, 2, 1)
    got_acc, got_stats = attend(
        info, query_block, keys_t, cache_values, tree_keys.T, tree_values, tree_mask, n_lo
    )
    got_acc = got_acc.reshape(n_lo, rows_owned, heads_local, HD)
    got_top = got_stats[:, 0, :, :heads_local]
    got_den = got_stats[:, 1, :, :heads_local]
    highest = jnp.max(got_top, axis=0)
    scale = jnp.exp(got_top - highest)
    num = jnp.sum(scale[..., None] * got_acc, axis=0)
    total = jnp.sum(scale * got_den, axis=0)
    merged = (num / total[..., None]).reshape(rows_owned, heads_local * HD)

    row_nodes = quarter * rows_owned + jnp.arange(rows_owned, dtype=jnp.int32)
    live_rows = row_nodes < live_size
    return jnp.where(live_rows[:, None], merged, 0.0).astype(jnp.bfloat16)


def solution(mesh):
    def run(queries, cache_keys, cache_values, tree_keys, tree_values, parents, tree_sizes, cache_lens):
        n_hi = cache_keys.shape[0]
        n_lo = mesh.shape["req"] // n_hi
        split = Mesh(mesh.devices.reshape(n_hi, n_lo, mesh.shape["head"]), ("rh", "rl", "head"))
        rows = ("rh", "rl")
        placed = (
            P(("rh", "rl", "head"), None),
            P(None, rows, "head"),
            P(None, rows, "head"),
            P(rows, "head"),
            P(rows, "head"),
            P(),
            P(),
            P(),
        )
        return jax.shard_map(
            body, mesh=split, in_specs=placed, out_specs=P(rows, "head"), check_vma=False
        )(queries, cache_keys, cache_values, tree_keys, tree_values, parents, tree_sizes, cache_lens)

    return run
```

```python
import functools
import math

import jax
import jax.numpy as jnp
from jax import lax
from jax.experimental import pallas as pl
from jax.experimental.pallas import tpu as pltpu
from jax.sharding import Mesh
from jax.sharding import PartitionSpec as P

NH = 128
KVH = 8
HD = 128


negative_fill = -1e30


def ancestry(parents):
    node_count = parents.shape[1]
    node_ids = jnp.arange(node_count, dtype=jnp.int32)
    linked = jnp.logical_or(
        parents[:, :, None] == node_ids[None, None, :], node_ids[:, None] == node_ids[None, :]
    )
    reached = linked.astype(jnp.bfloat16)
    for doubling in range((node_count - 1).bit_length()):
        squared = jnp.einsum("aij,ajk->aik", reached, reached, preferred_element_type=jnp.float32)
        reached = jnp.minimum(squared, 1.0).astype(jnp.bfloat16)
    return reached


def attend_kernel(
    info_ref, q_ref, kt_hbm, v_hbm, tkt_ref, tv_ref, tmask_ref, acc_out, stat_out,
    kslots, vslots, send_sem, recv_sem, own_sem, acc_ref, top_ref, den_ref, stats,
    acc_slots, stat_slots, fsend, frecv, fown, *, scale, n_hi, n_quarters,
):
    request = lax.axis_index("rh")
    quarter = lax.axis_index("rl")
    head_axis = lax.axis_index("head")
    mesh = pl.DeviceIdType.MESH
    length = info_ref[0]
    n_lo = info_ref[1]
    rows = q_ref.shape[0]
    heads = q_ref.shape[1] // HD
    block_len = kt_hbm.shape[2]

    barrier = pltpu.get_barrier_semaphore()
    for t in range(n_hi):

        @pl.when(t != request)
        def _():
            pl.semaphore_signal(
                barrier, inc=1, device_id=(t, quarter, head_axis), device_id_type=mesh
            )

    for r in range(n_quarters):

        @pl.when(r != quarter)
        def _():
            pl.semaphore_signal(
                barrier, inc=1, device_id=(request, r, head_axis), device_id_type=mesh
            )

    pl.semaphore_wait(barrier, n_hi - 1 + n_quarters - 1)

    def pushes(t):
        dest = (t, quarter, head_axis)
        return (
            pltpu.make_async_remote_copy(
                kt_hbm.at[t], kslots.at[request], send_sem.at[t, 0], recv_sem.at[request, 0],
                device_id=dest, device_id_type=mesh,
            ),
            pltpu.make_async_remote_copy(
                v_hbm.at[t], vslots.at[request], send_sem.at[t, 1], recv_sem.at[request, 1],
                device_id=dest, device_id_type=mesh,
            ),
        )

    ahead = 2
    for shift in range(1, min(ahead, n_hi - 1) + 1):
        t = lax.rem(request + shift, n_hi)
        for copy in pushes(t):
            copy.start()
    own_k = pltpu.make_async_copy(kt_hbm.at[request], kslots.at[request], own_sem.at[0])
    own_v = pltpu.make_async_copy(v_hbm.at[request], vslots.at[request], own_sem.at[1])
    own_k.start()
    own_v.start()

    acc_ref[...] = jnp.zeros_like(acc_ref)
    top_ref[...] = jnp.full_like(top_ref, negative_fill)
    den_ref[...] = jnp.zeros_like(den_ref)

    def group(s, with_tree):
        start = (s * n_lo + quarter) * block_len
        kt_ref = kslots.at[s]
        v_ref = vslots.at[s]
        pos = start + lax.broadcasted_iota(jnp.int32, (1, block_len), 1)
        bias = jnp.where(pos < length, 0.0, negative_fill)

        def head(h, carry):
            col = pl.multiple_of(h * HD, HD)
            qh = q_ref[:, pl.ds(col, HD)]
            sc = jnp.dot(qh, kt_ref[...], preferred_element_type=jnp.float32) * scale + bias
            peak = jnp.max(sc, axis=1, keepdims=True)
            if with_tree:
                st = jnp.dot(qh, tkt_ref[...], preferred_element_type=jnp.float32) * scale
                tlive = tmask_ref[...] > 0.5
                st = jnp.where(tlive, st, negative_fill)
                peak = jnp.maximum(peak, jnp.max(st, axis=1, keepdims=True))
            w = jnp.exp(sc - jnp.maximum(peak, 0.1 * negative_fill))
            tot = jnp.sum(w, axis=1, keepdims=True)
            gs = jnp.dot(w.astype(jnp.bfloat16), v_ref[...], preferred_element_type=jnp.float32)
            if with_tree:
                wt = jnp.where(tlive, jnp.exp(st - peak), 0.0)
                tot = tot + jnp.sum(wt, axis=1, keepdims=True)
                gs = gs + jnp.dot(
                    wt.astype(jnp.bfloat16), tv_ref[...], preferred_element_type=jnp.float32
                )
            floored = jnp.maximum(tot, 1.0)
            part = gs / floored
            lt = peak + jnp.log(floored)
            old = top_ref[h][:, :1]
            new = jnp.maximum(old, lt)
            keep = jnp.exp(old - new)
            add = jnp.exp(lt - new)
            acc_ref[:, pl.ds(col, HD)] = keep * acc_ref[:, pl.ds(col, HD)] + add * part
            den_ref[h] = jnp.broadcast_to(keep * den_ref[h][:, :1] + add, (rows, HD))
            top_ref[h] = jnp.broadcast_to(new, (rows, HD))
            return carry

        lax.fori_loop(0, heads, head, 0, unroll=2)

    own_k.wait()
    own_v.wait()
    group(request, True)

    def landed(s):
        source = (s, quarter, head_axis)
        return (
            pltpu.make_async_remote_copy(
                kt_hbm.at[s], kslots.at[s], send_sem.at[s, 0], recv_sem.at[s, 0],
                device_id=source, device_id_type=mesh,
            ),
            pltpu.make_async_remote_copy(
                v_hbm.at[s], vslots.at[s], send_sem.at[s, 1], recv_sem.at[s, 1],
                device_id=source, device_id_type=mesh,
            ),
        )

    def arrival(step, carry):
        @pl.when(step + ahead + 1 < n_hi)
        def _():
            t = lax.rem(request + step + ahead + 1, n_hi)
            for copy in pushes(t):
                copy.start()

        s = lax.rem(request - step - 1 + n_hi, n_hi)
        for copy in landed(s):
            copy.wait_recv()
        group(s, False)
        return carry

    lax.fori_loop(0, n_hi - 1, arrival, 0)
    for shift in range(1, n_hi):
        t = lax.rem(request + shift, n_hi)
        for copy in pushes(t):
            copy.wait_send()

    lane = lax.broadcasted_iota(jnp.int32, (rows, HD), 1)
    tops = jnp.full((rows, HD), negative_fill, jnp.float32)
    dens = jnp.zeros((rows, HD), jnp.float32)
    for h in range(heads):
        tops = jnp.where(lane == h, top_ref[h], tops)
        dens = jnp.where(lane == h, den_ref[h], dens)
    stats[0] = tops
    stats[1] = dens

    quarter_rows = rows // n_quarters

    def quarter_copies(r, slot, device):
        piece = pl.ds(r * quarter_rows, quarter_rows)
        return (
            pltpu.make_async_remote_copy(
                acc_ref.at[piece, :], acc_slots.at[slot], fsend.at[r, 0], frecv.at[slot, 0],
                device_id=device, device_id_type=mesh,
            ),
            pltpu.make_async_remote_copy(
                stats.at[:, piece, :], stat_slots.at[slot], fsend.at[r, 1], frecv.at[slot, 1],
                device_id=device, device_id_type=mesh,
            ),
        )

    for r in range(n_quarters):
        for copy in quarter_copies(r, quarter, (request, r, head_axis)):
            pl.when(r != quarter)(copy.start)
    mine = pl.ds(pl.multiple_of(quarter * quarter_rows, quarter_rows), quarter_rows)
    keep_acc = pltpu.make_async_copy(acc_ref.at[mine, :], acc_slots.at[quarter], fown.at[0])
    keep_stat = pltpu.make_async_copy(stats.at[:, mine, :], stat_slots.at[quarter], fown.at[1])
    keep_acc.start()
    keep_stat.start()
    keep_acc.wait()
    keep_stat.wait()
    for r in range(n_quarters):
        for copy in quarter_copies(r, r, (request, r, head_axis)):
            pl.when(r != quarter)(copy.wait_recv)
    for r in range(n_quarters):
        for copy in quarter_copies(r, quarter, (request, r, head_axis)):
            pl.when(r != quarter)(copy.wait_send)
    acc_out[...] = acc_slots[...]
    stat_out[...] = stat_slots[...]


def attend(info, query_block, keys_t, values, tree_keys_t, tree_values, tree_mask, n_quarters):
    rows, width = query_block.shape
    heads = width // HD
    n_hi = keys_t.shape[0]
    quarter_rows = rows // n_quarters
    vmem = pl.BlockSpec(memory_space=pltpu.VMEM)
    hbm = pl.BlockSpec(memory_space=pl.ANY)
    acc_shape = (n_quarters, quarter_rows, width)
    stat_shape = (n_quarters, 2, quarter_rows, HD)
    return pl.pallas_call(
        functools.partial(
            attend_kernel, scale=1.0 / math.sqrt(HD), n_hi=n_hi, n_quarters=n_quarters
        ),
        out_shape=(
            jax.ShapeDtypeStruct(acc_shape, jnp.float32),
            jax.ShapeDtypeStruct(stat_shape, jnp.float32),
        ),
        in_specs=[pl.BlockSpec(memory_space=pltpu.SMEM), vmem, hbm, hbm, vmem, vmem, vmem],
        out_specs=(vmem, vmem),
        scratch_shapes=[
            pltpu.VMEM(keys_t.shape, keys_t.dtype),
            pltpu.VMEM(values.shape, values.dtype),
            pltpu.SemaphoreType.DMA((n_hi, 2)),
            pltpu.SemaphoreType.DMA((n_hi, 2)),
            pltpu.SemaphoreType.DMA((2,)),
            pltpu.VMEM((rows, width), jnp.float32),
            pltpu.VMEM((heads, rows, HD), jnp.float32),
            pltpu.VMEM((heads, rows, HD), jnp.float32),
            pltpu.VMEM((2, rows, HD), jnp.float32),
            pltpu.VMEM(acc_shape, jnp.float32),
            pltpu.VMEM(stat_shape, jnp.float32),
            pltpu.SemaphoreType.DMA((n_quarters, 2)),
            pltpu.SemaphoreType.DMA((n_quarters, 2)),
            pltpu.SemaphoreType.DMA((2,)),
        ],
        compiler_params=pltpu.CompilerParams(
            collective_id=1, has_side_effects=True, vmem_limit_bytes=48 * 1024 * 1024
        ),
    )(info, query_block, keys_t, values, tree_keys_t, tree_values, tree_mask)


def exchange_kernel(src_ref, out_ref, slots, send_sem, recv_sem, own_sem, *, n_lo, n_head):
    request = lax.axis_index("rh")
    quarter = lax.axis_index("rl")
    head = lax.axis_index("head")
    me = quarter * n_head + head
    peers = n_lo * n_head
    mesh = pl.DeviceIdType.MESH

    barrier = pltpu.get_barrier_semaphore()
    for d in range(peers):
        dest = (request, d // n_head, d % n_head)

        @pl.when(d != me)
        def _():
            pl.semaphore_signal(barrier, inc=1, device_id=dest, device_id_type=mesh)

    pl.semaphore_wait(barrier, peers - 1)

    def push(d):
        return pltpu.make_async_remote_copy(
            src_ref.at[d % n_head],
            slots.at[me],
            send_sem.at[d],
            recv_sem.at[me],
            device_id=(request, d // n_head, d % n_head),
            device_id_type=mesh,
        )

    for d in range(peers):
        pl.when(d != me)(push(d).start)
    own = pltpu.make_async_copy(src_ref.at[head], slots.at[me], own_sem)
    own.start()
    own.wait()
    for d in range(peers):
        pl.when(d != me)(push(d).wait_send)
    for s in range(peers):
        arrival = pltpu.make_async_remote_copy(
            src_ref.at[0],
            slots.at[s],
            send_sem.at[s],
            recv_sem.at[s],
            device_id=(request, s // n_head, s % n_head),
            device_id_type=mesh,
        )
        pl.when(s != me)(arrival.wait_recv)
    out_ref[...] = slots[...]


def exchange_queries(pieces, n_lo, n_head):
    peers = n_lo * n_head
    shape = (peers,) + pieces.shape[1:]
    vmem = pl.BlockSpec(memory_space=pltpu.VMEM)
    return pl.pallas_call(
        functools.partial(exchange_kernel, n_lo=n_lo, n_head=n_head),
        out_shape=jax.ShapeDtypeStruct(shape, pieces.dtype),
        in_specs=[vmem],
        out_specs=vmem,
        scratch_shapes=[
            pltpu.VMEM(shape, pieces.dtype),
            pltpu.SemaphoreType.DMA((peers,)),
            pltpu.SemaphoreType.DMA((peers,)),
            pltpu.SemaphoreType.DMA(()),
        ],
        compiler_params=pltpu.CompilerParams(collective_id=0, has_side_effects=True),
    )(pieces)


def body(
    queries, cache_keys, cache_values, tree_keys, tree_values, parents, tree_sizes, cache_lens
):
    group_size = NH // KVH
    softmax_scale = 1.0 / math.sqrt(HD)
    request = lax.axis_index("rh")
    quarter = lax.axis_index("rl")
    n_lo = lax.axis_size("rl")
    n_hi = lax.axis_size("rh")
    cache_block = cache_keys.shape[1]
    kv_local = cache_keys.shape[2] // HD
    heads_local = kv_local * group_size
    node_count = parents.shape[1]
    rows_owned = tree_keys.shape[0]

    n_head = lax.axis_size("head")
    width = queries.shape[1] // n_head
    pieces = queries.reshape(queries.shape[0], n_head, width // HD, HD).transpose(1, 0, 2, 3)
    pieces = pieces.reshape(n_head, queries.shape[0] * width // HD, HD)
    query_block = exchange_queries(pieces, n_lo, n_head)
    query_block = query_block.reshape(node_count, width)

    reached = ancestry(parents)
    ancestors = lax.dynamic_index_in_dim(reached, request, 0, keepdims=False)
    ancestors = lax.dynamic_slice_in_dim(ancestors, quarter * rows_owned, rows_owned, 1)
    tree_mask = ancestors.astype(jnp.float32)
    length = lax.dynamic_index_in_dim(cache_lens, request, 0, keepdims=False)
    live_size = lax.dynamic_index_in_dim(tree_sizes, request, 0, keepdims=False)
    info = jnp.stack([length, jnp.int32(n_lo)]).astype(jnp.int32)
    keys_t = cache_keys.transpose(0, 2, 1)
    got_acc, got_stats = attend(
        info, query_block, keys_t, cache_values, tree_keys.T, tree_values, tree_mask, n_lo
    )
    got_acc = got_acc.reshape(n_lo, rows_owned, heads_local, HD)
    got_top = got_stats[:, 0, :, :heads_local]
    got_den = got_stats[:, 1, :, :heads_local]
    highest = jnp.max(got_top, axis=0)
    scale = jnp.exp(got_top - highest)
    num = jnp.sum(scale[..., None] * got_acc, axis=0)
    total = jnp.sum(scale * got_den, axis=0)
    merged = (num / total[..., None]).reshape(rows_owned, heads_local * HD)

    row_nodes = quarter * rows_owned + jnp.arange(rows_owned, dtype=jnp.int32)
    live_rows = row_nodes < live_size
    return jnp.where(live_rows[:, None], merged, 0.0).astype(jnp.bfloat16)


def solution(mesh):
    def run(queries, cache_keys, cache_values, tree_keys, tree_values, parents, tree_sizes, cache_lens):
        n_hi = cache_keys.shape[0]
        n_lo = mesh.shape["req"] // n_hi
        split = Mesh(mesh.devices.reshape(n_hi, n_lo, mesh.shape["head"]), ("rh", "rl", "head"))
        rows = ("rh", "rl")
        placed = (
            P(("rh", "rl", "head"), None),
            P(None, rows, "head"),
            P(None, rows, "head"),
            P(rows, "head"),
            P(rows, "head"),
            P(),
            P(),
            P(),
        )
        return jax.shard_map(
            body, mesh=split, in_specs=placed, out_specs=P(rows, "head"), check_vma=False
        )(queries, cache_keys, cache_values, tree_keys, tree_values, parents, tree_sizes, cache_lens)

    return run
```

```python
import functools
import math

import jax
import jax.numpy as jnp
from jax import lax
from jax.experimental import pallas as pl
from jax.experimental.pallas import tpu as pltpu
from jax.sharding import Mesh
from jax.sharding import PartitionSpec as P

NH = 128
KVH = 8
HD = 128


negative_fill = -1e30


def ancestry(parents):
    node_count = parents.shape[1]
    node_ids = jnp.arange(node_count, dtype=jnp.int32)
    linked = jnp.logical_or(
        parents[:, :, None] == node_ids[None, None, :], node_ids[:, None] == node_ids[None, :]
    )
    reached = linked.astype(jnp.bfloat16)
    for doubling in range((node_count - 1).bit_length()):
        squared = jnp.einsum("aij,ajk->aik", reached, reached, preferred_element_type=jnp.float32)
        reached = jnp.minimum(squared, 1.0).astype(jnp.bfloat16)
    return reached


def attend_kernel(
    info_ref, q_ref, kt_hbm, v_hbm, tkt_ref, tv_ref, tmask_ref, acc_out, stat_out,
    kslots, vslots, send_sem, recv_sem, own_sem, acc_ref, top_ref, den_ref, stats,
    acc_slots, stat_slots, fsend, frecv, fown, *, scale, n_hi, n_quarters,
):
    request = lax.axis_index("rh")
    quarter = lax.axis_index("rl")
    head_axis = lax.axis_index("head")
    mesh = pl.DeviceIdType.MESH
    length = info_ref[0]
    n_lo = info_ref[1]
    rows = q_ref.shape[0]
    heads = q_ref.shape[1] // HD
    block_len = kt_hbm.shape[2]

    barrier = pltpu.get_barrier_semaphore()
    for t in range(n_hi):

        @pl.when(t != request)
        def _():
            pl.semaphore_signal(
                barrier, inc=1, device_id=(t, quarter, head_axis), device_id_type=mesh
            )

    for r in range(n_quarters):

        @pl.when(r != quarter)
        def _():
            pl.semaphore_signal(
                barrier, inc=1, device_id=(request, r, head_axis), device_id_type=mesh
            )

    pl.semaphore_wait(barrier, n_hi - 1 + n_quarters - 1)

    def pushes(t):
        dest = (t, quarter, head_axis)
        return (
            pltpu.make_async_remote_copy(
                kt_hbm.at[t], kslots.at[request], send_sem.at[t, 0], recv_sem.at[request, 0],
                device_id=dest, device_id_type=mesh,
            ),
            pltpu.make_async_remote_copy(
                v_hbm.at[t], vslots.at[request], send_sem.at[t, 1], recv_sem.at[request, 1],
                device_id=dest, device_id_type=mesh,
            ),
        )

    ahead = 2
    for shift in range(1, min(ahead, n_hi - 1) + 1):
        t = lax.rem(request + shift, n_hi)
        for copy in pushes(t):
            copy.start()
    own_k = pltpu.make_async_copy(kt_hbm.at[request], kslots.at[request], own_sem.at[0])
    own_v = pltpu.make_async_copy(v_hbm.at[request], vslots.at[request], own_sem.at[1])
    own_k.start()
    own_v.start()

    acc_ref[...] = jnp.zeros_like(acc_ref)
    top_ref[...] = jnp.full_like(top_ref, negative_fill)
    den_ref[...] = jnp.zeros_like(den_ref)

    def group(s, with_tree):
        start = (s * n_lo + quarter) * block_len
        kt_ref = kslots.at[s]
        v_ref = vslots.at[s]
        pos = start + lax.broadcasted_iota(jnp.int32, (1, block_len), 1)
        bias = jnp.where(pos < length, 0.0, negative_fill)

        def head(h, carry):
            col = pl.multiple_of(h * HD, HD)
            qh = q_ref[:, pl.ds(col, HD)]
            sc = jnp.dot(qh, kt_ref[...], preferred_element_type=jnp.float32) * scale + bias
            peak = jnp.max(sc, axis=1, keepdims=True)
            if with_tree:
                st = jnp.dot(qh, tkt_ref[...], preferred_element_type=jnp.float32) * scale
                tlive = tmask_ref[...] > 0.5
                st = jnp.where(tlive, st, negative_fill)
                peak = jnp.maximum(peak, jnp.max(st, axis=1, keepdims=True))
            w = jnp.exp(sc - jnp.maximum(peak, 0.1 * negative_fill))
            tot = jnp.sum(w, axis=1, keepdims=True)
            gs = jnp.dot(w.astype(jnp.bfloat16), v_ref[...], preferred_element_type=jnp.float32)
            if with_tree:
                wt = jnp.where(tlive, jnp.exp(st - peak), 0.0)
                tot = tot + jnp.sum(wt, axis=1, keepdims=True)
                gs = gs + jnp.dot(
                    wt.astype(jnp.bfloat16), tv_ref[...], preferred_element_type=jnp.float32
                )
            floored = jnp.maximum(tot, 1.0)
            part = gs / floored
            lt = peak + jnp.log(floored)
            old = top_ref[h][:, :1]
            new = jnp.maximum(old, lt)
            keep = jnp.exp(old - new)
            add = jnp.exp(lt - new)
            acc_ref[:, pl.ds(col, HD)] = keep * acc_ref[:, pl.ds(col, HD)] + add * part
            den_ref[h] = jnp.broadcast_to(keep * den_ref[h][:, :1] + add, (rows, HD))
            top_ref[h] = jnp.broadcast_to(new, (rows, HD))
            return carry

        lax.fori_loop(0, heads, head, 0, unroll=4)

    own_k.wait()
    own_v.wait()
    group(request, True)

    def landed(s):
        source = (s, quarter, head_axis)
        return (
            pltpu.make_async_remote_copy(
                kt_hbm.at[s], kslots.at[s], send_sem.at[s, 0], recv_sem.at[s, 0],
                device_id=source, device_id_type=mesh,
            ),
            pltpu.make_async_remote_copy(
                v_hbm.at[s], vslots.at[s], send_sem.at[s, 1], recv_sem.at[s, 1],
                device_id=source, device_id_type=mesh,
            ),
        )

    def arrival(step, carry):
        @pl.when(step + ahead + 1 < n_hi)
        def _():
            t = lax.rem(request + step + ahead + 1, n_hi)
            for copy in pushes(t):
                copy.start()

        s = lax.rem(request - step - 1 + n_hi, n_hi)
        for copy in landed(s):
            copy.wait_recv()
        group(s, False)
        return carry

    lax.fori_loop(0, n_hi - 1, arrival, 0)
    for shift in range(1, n_hi):
        t = lax.rem(request + shift, n_hi)
        for copy in pushes(t):
            copy.wait_send()

    lane = lax.broadcasted_iota(jnp.int32, (rows, HD), 1)
    tops = jnp.full((rows, HD), negative_fill, jnp.float32)
    dens = jnp.zeros((rows, HD), jnp.float32)
    for h in range(heads):
        tops = jnp.where(lane == h, top_ref[h], tops)
        dens = jnp.where(lane == h, den_ref[h], dens)
    stats[0] = tops
    stats[1] = dens

    quarter_rows = rows // n_quarters

    def quarter_copies(r, slot, device):
        piece = pl.ds(r * quarter_rows, quarter_rows)
        return (
            pltpu.make_async_remote_copy(
                acc_ref.at[piece, :], acc_slots.at[slot], fsend.at[r, 0], frecv.at[slot, 0],
                device_id=device, device_id_type=mesh,
            ),
            pltpu.make_async_remote_copy(
                stats.at[:, piece, :], stat_slots.at[slot], fsend.at[r, 1], frecv.at[slot, 1],
                device_id=device, device_id_type=mesh,
            ),
        )

    for r in range(n_quarters):
        for copy in quarter_copies(r, quarter, (request, r, head_axis)):
            pl.when(r != quarter)(copy.start)
    mine = pl.ds(pl.multiple_of(quarter * quarter_rows, quarter_rows), quarter_rows)
    keep_acc = pltpu.make_async_copy(acc_ref.at[mine, :], acc_slots.at[quarter], fown.at[0])
    keep_stat = pltpu.make_async_copy(stats.at[:, mine, :], stat_slots.at[quarter], fown.at[1])
    keep_acc.start()
    keep_stat.start()
    keep_acc.wait()
    keep_stat.wait()
    for r in range(n_quarters):
        for copy in quarter_copies(r, r, (request, r, head_axis)):
            pl.when(r != quarter)(copy.wait_recv)
    for r in range(n_quarters):
        for copy in quarter_copies(r, quarter, (request, r, head_axis)):
            pl.when(r != quarter)(copy.wait_send)
    acc_out[...] = acc_slots[...]
    stat_out[...] = stat_slots[...]


def attend(info, query_block, keys_t, values, tree_keys_t, tree_values, tree_mask, n_quarters):
    rows, width = query_block.shape
    heads = width // HD
    n_hi = keys_t.shape[0]
    quarter_rows = rows // n_quarters
    vmem = pl.BlockSpec(memory_space=pltpu.VMEM)
    hbm = pl.BlockSpec(memory_space=pl.ANY)
    acc_shape = (n_quarters, quarter_rows, width)
    stat_shape = (n_quarters, 2, quarter_rows, HD)
    return pl.pallas_call(
        functools.partial(
            attend_kernel, scale=1.0 / math.sqrt(HD), n_hi=n_hi, n_quarters=n_quarters
        ),
        out_shape=(
            jax.ShapeDtypeStruct(acc_shape, jnp.float32),
            jax.ShapeDtypeStruct(stat_shape, jnp.float32),
        ),
        in_specs=[pl.BlockSpec(memory_space=pltpu.SMEM), vmem, hbm, hbm, vmem, vmem, vmem],
        out_specs=(vmem, vmem),
        scratch_shapes=[
            pltpu.VMEM(keys_t.shape, keys_t.dtype),
            pltpu.VMEM(values.shape, values.dtype),
            pltpu.SemaphoreType.DMA((n_hi, 2)),
            pltpu.SemaphoreType.DMA((n_hi, 2)),
            pltpu.SemaphoreType.DMA((2,)),
            pltpu.VMEM((rows, width), jnp.float32),
            pltpu.VMEM((heads, rows, HD), jnp.float32),
            pltpu.VMEM((heads, rows, HD), jnp.float32),
            pltpu.VMEM((2, rows, HD), jnp.float32),
            pltpu.VMEM(acc_shape, jnp.float32),
            pltpu.VMEM(stat_shape, jnp.float32),
            pltpu.SemaphoreType.DMA((n_quarters, 2)),
            pltpu.SemaphoreType.DMA((n_quarters, 2)),
            pltpu.SemaphoreType.DMA((2,)),
        ],
        compiler_params=pltpu.CompilerParams(
            collective_id=1, has_side_effects=True, vmem_limit_bytes=48 * 1024 * 1024
        ),
    )(info, query_block, keys_t, values, tree_keys_t, tree_values, tree_mask)


def exchange_kernel(src_ref, out_ref, slots, send_sem, recv_sem, own_sem, *, n_lo, n_head):
    request = lax.axis_index("rh")
    quarter = lax.axis_index("rl")
    head = lax.axis_index("head")
    me = quarter * n_head + head
    peers = n_lo * n_head
    mesh = pl.DeviceIdType.MESH

    barrier = pltpu.get_barrier_semaphore()
    for d in range(peers):
        dest = (request, d // n_head, d % n_head)

        @pl.when(d != me)
        def _():
            pl.semaphore_signal(barrier, inc=1, device_id=dest, device_id_type=mesh)

    pl.semaphore_wait(barrier, peers - 1)

    def push(d):
        return pltpu.make_async_remote_copy(
            src_ref.at[d % n_head],
            slots.at[me],
            send_sem.at[d],
            recv_sem.at[me],
            device_id=(request, d // n_head, d % n_head),
            device_id_type=mesh,
        )

    for d in range(peers):
        pl.when(d != me)(push(d).start)
    own = pltpu.make_async_copy(src_ref.at[head], slots.at[me], own_sem)
    own.start()
    own.wait()
    for d in range(peers):
        pl.when(d != me)(push(d).wait_send)
    for s in range(peers):
        arrival = pltpu.make_async_remote_copy(
            src_ref.at[0],
            slots.at[s],
            send_sem.at[s],
            recv_sem.at[s],
            device_id=(request, s // n_head, s % n_head),
            device_id_type=mesh,
        )
        pl.when(s != me)(arrival.wait_recv)
    out_ref[...] = slots[...]


def exchange_queries(pieces, n_lo, n_head):
    peers = n_lo * n_head
    shape = (peers,) + pieces.shape[1:]
    vmem = pl.BlockSpec(memory_space=pltpu.VMEM)
    return pl.pallas_call(
        functools.partial(exchange_kernel, n_lo=n_lo, n_head=n_head),
        out_shape=jax.ShapeDtypeStruct(shape, pieces.dtype),
        in_specs=[vmem],
        out_specs=vmem,
        scratch_shapes=[
            pltpu.VMEM(shape, pieces.dtype),
            pltpu.SemaphoreType.DMA((peers,)),
            pltpu.SemaphoreType.DMA((peers,)),
            pltpu.SemaphoreType.DMA(()),
        ],
        compiler_params=pltpu.CompilerParams(collective_id=0, has_side_effects=True),
    )(pieces)


def body(
    queries, cache_keys, cache_values, tree_keys, tree_values, parents, tree_sizes, cache_lens
):
    group_size = NH // KVH
    softmax_scale = 1.0 / math.sqrt(HD)
    request = lax.axis_index("rh")
    quarter = lax.axis_index("rl")
    n_lo = lax.axis_size("rl")
    n_hi = lax.axis_size("rh")
    cache_block = cache_keys.shape[1]
    kv_local = cache_keys.shape[2] // HD
    heads_local = kv_local * group_size
    node_count = parents.shape[1]
    rows_owned = tree_keys.shape[0]

    n_head = lax.axis_size("head")
    width = queries.shape[1] // n_head
    pieces = queries.reshape(queries.shape[0], n_head, width // HD, HD).transpose(1, 0, 2, 3)
    pieces = pieces.reshape(n_head, queries.shape[0] * width // HD, HD)
    query_block = exchange_queries(pieces, n_lo, n_head)
    query_block = query_block.reshape(node_count, width)

    reached = ancestry(parents)
    ancestors = lax.dynamic_index_in_dim(reached, request, 0, keepdims=False)
    ancestors = lax.dynamic_slice_in_dim(ancestors, quarter * rows_owned, rows_owned, 1)
    tree_mask = ancestors.astype(jnp.float32)
    length = lax.dynamic_index_in_dim(cache_lens, request, 0, keepdims=False)
    live_size = lax.dynamic_index_in_dim(tree_sizes, request, 0, keepdims=False)
    info = jnp.stack([length, jnp.int32(n_lo)]).astype(jnp.int32)
    keys_t = cache_keys.transpose(0, 2, 1)
    got_acc, got_stats = attend(
        info, query_block, keys_t, cache_values, tree_keys.T, tree_values, tree_mask, n_lo
    )
    got_acc = got_acc.reshape(n_lo, rows_owned, heads_local, HD)
    got_top = got_stats[:, 0, :, :heads_local]
    got_den = got_stats[:, 1, :, :heads_local]
    highest = jnp.max(got_top, axis=0)
    scale = jnp.exp(got_top - highest)
    num = jnp.sum(scale[..., None] * got_acc, axis=0)
    total = jnp.sum(scale * got_den, axis=0)
    merged = (num / total[..., None]).reshape(rows_owned, heads_local * HD)

    row_nodes = quarter * rows_owned + jnp.arange(rows_owned, dtype=jnp.int32)
    live_rows = row_nodes < live_size
    return jnp.where(live_rows[:, None], merged, 0.0).astype(jnp.bfloat16)


def solution(mesh):
    def run(queries, cache_keys, cache_values, tree_keys, tree_values, parents, tree_sizes, cache_lens):
        n_hi = cache_keys.shape[0]
        n_lo = mesh.shape["req"] // n_hi
        split = Mesh(mesh.devices.reshape(n_hi, n_lo, mesh.shape["head"]), ("rh", "rl", "head"))
        rows = ("rh", "rl")
        placed = (
            P(("rh", "rl", "head"), None),
            P(None, rows, "head"),
            P(None, rows, "head"),
            P(rows, "head"),
            P(rows, "head"),
            P(),
            P(),
            P(),
        )
        return jax.shard_map(
            body, mesh=split, in_specs=placed, out_specs=P(rows, "head"), check_vma=False
        )(queries, cache_keys, cache_values, tree_keys, tree_values, parents, tree_sizes, cache_lens)

    return run
```

```python
import functools
import math

import jax
import jax.numpy as jnp
from jax import lax
from jax.experimental import pallas as pl
from jax.experimental.pallas import tpu as pltpu
from jax.sharding import Mesh
from jax.sharding import PartitionSpec as P

NH = 128
KVH = 8
HD = 128


negative_fill = -1e30


def ancestry(parents):
    node_count = parents.shape[1]
    node_ids = jnp.arange(node_count, dtype=jnp.int32)
    linked = jnp.logical_or(
        parents[:, :, None] == node_ids[None, None, :], node_ids[:, None] == node_ids[None, :]
    )
    reached = linked.astype(jnp.bfloat16)
    for doubling in range((node_count - 1).bit_length()):
        squared = jnp.einsum("aij,ajk->aik", reached, reached, preferred_element_type=jnp.float32)
        reached = jnp.minimum(squared, 1.0).astype(jnp.bfloat16)
    return reached


def attend_kernel(
    info_ref, q_ref, kt_hbm, v_hbm, tkt_ref, tv_ref, tmask_ref, acc_out, stat_out,
    kslots, vslots, send_sem, recv_sem, own_sem, acc_ref, top_ref, den_ref, stats,
    acc_slots, stat_slots, fsend, frecv, fown, *, scale, n_hi, n_quarters,
):
    request = lax.axis_index("rh")
    quarter = lax.axis_index("rl")
    head_axis = lax.axis_index("head")
    mesh = pl.DeviceIdType.MESH
    length = info_ref[0]
    n_lo = info_ref[1]
    rows = q_ref.shape[0]
    heads = q_ref.shape[1] // HD
    block_len = kt_hbm.shape[2]

    barrier = pltpu.get_barrier_semaphore()
    for t in range(n_hi):

        @pl.when(t != request)
        def _():
            pl.semaphore_signal(
                barrier, inc=1, device_id=(t, quarter, head_axis), device_id_type=mesh
            )

    for r in range(n_quarters):

        @pl.when(r != quarter)
        def _():
            pl.semaphore_signal(
                barrier, inc=1, device_id=(request, r, head_axis), device_id_type=mesh
            )

    pl.semaphore_wait(barrier, n_hi - 1 + n_quarters - 1)

    def pushes(t):
        dest = (t, quarter, head_axis)
        return (
            pltpu.make_async_remote_copy(
                kt_hbm.at[t], kslots.at[request], send_sem.at[t, 0], recv_sem.at[request, 0],
                device_id=dest, device_id_type=mesh,
            ),
            pltpu.make_async_remote_copy(
                v_hbm.at[t], vslots.at[request], send_sem.at[t, 1], recv_sem.at[request, 1],
                device_id=dest, device_id_type=mesh,
            ),
        )

    ahead = 2
    for shift in range(1, min(ahead, n_hi - 1) + 1):
        t = lax.rem(request + shift, n_hi)
        for copy in pushes(t):
            copy.start()
    own_k = pltpu.make_async_copy(kt_hbm.at[request], kslots.at[request], own_sem.at[0])
    own_v = pltpu.make_async_copy(v_hbm.at[request], vslots.at[request], own_sem.at[1])
    own_k.start()
    own_v.start()

    acc_ref[...] = jnp.zeros_like(acc_ref)
    top_ref[...] = jnp.full_like(top_ref, negative_fill)
    den_ref[...] = jnp.zeros_like(den_ref)

    def group(s, with_tree):
        start = (s * n_lo + quarter) * block_len
        kt_ref = kslots.at[s]
        v_ref = vslots.at[s]
        pos = start + lax.broadcasted_iota(jnp.int32, (1, block_len), 1)
        bias = jnp.where(pos < length, 0.0, negative_fill)

        def head(h, carry):
            col = pl.multiple_of(h * HD, HD)
            qh = q_ref[:, pl.ds(col, HD)]
            sc = jnp.dot(qh, kt_ref[...], preferred_element_type=jnp.float32) * scale + bias
            peak = jnp.max(sc, axis=1, keepdims=True)
            if with_tree:
                st = jnp.dot(qh, tkt_ref[...], preferred_element_type=jnp.float32) * scale
                tlive = tmask_ref[...] > 0.5
                st = jnp.where(tlive, st, negative_fill)
                peak = jnp.maximum(peak, jnp.max(st, axis=1, keepdims=True))
            w = jnp.exp(sc - jnp.maximum(peak, 0.1 * negative_fill))
            tot = jnp.sum(w, axis=1, keepdims=True)
            gs = jnp.dot(w.astype(jnp.bfloat16), v_ref[...], preferred_element_type=jnp.float32)
            if with_tree:
                wt = jnp.where(tlive, jnp.exp(st - peak), 0.0)
                tot = tot + jnp.sum(wt, axis=1, keepdims=True)
                gs = gs + jnp.dot(
                    wt.astype(jnp.bfloat16), tv_ref[...], preferred_element_type=jnp.float32
                )
            floored = jnp.maximum(tot, 1.0)
            part = gs / floored
            lt = peak + jnp.log(floored)
            old = top_ref[h][:, :1]
            new = jnp.maximum(old, lt)
            keep = jnp.exp(old - new)
            add = jnp.exp(lt - new)
            acc_ref[:, pl.ds(col, HD)] = keep * acc_ref[:, pl.ds(col, HD)] + add * part
            den_ref[h] = jnp.broadcast_to(keep * den_ref[h][:, :1] + add, (rows, HD))
            top_ref[h] = jnp.broadcast_to(new, (rows, HD))
            return carry

        lax.fori_loop(0, heads, head, 0, unroll=8)

    own_k.wait()
    own_v.wait()
    group(request, True)

    def landed(s):
        source = (s, quarter, head_axis)
        return (
            pltpu.make_async_remote_copy(
                kt_hbm.at[s], kslots.at[s], send_sem.at[s, 0], recv_sem.at[s, 0],
                device_id=source, device_id_type=mesh,
            ),
            pltpu.make_async_remote_copy(
                v_hbm.at[s], vslots.at[s], send_sem.at[s, 1], recv_sem.at[s, 1],
                device_id=source, device_id_type=mesh,
            ),
        )

    def arrival(step, carry):
        @pl.when(step + ahead + 1 < n_hi)
        def _():
            t = lax.rem(request + step + ahead + 1, n_hi)
            for copy in pushes(t):
                copy.start()

        s = lax.rem(request - step - 1 + n_hi, n_hi)
        for copy in landed(s):
            copy.wait_recv()
        group(s, False)
        return carry

    lax.fori_loop(0, n_hi - 1, arrival, 0)
    for shift in range(1, n_hi):
        t = lax.rem(request + shift, n_hi)
        for copy in pushes(t):
            copy.wait_send()

    lane = lax.broadcasted_iota(jnp.int32, (rows, HD), 1)
    tops = jnp.full((rows, HD), negative_fill, jnp.float32)
    dens = jnp.zeros((rows, HD), jnp.float32)
    for h in range(heads):
        tops = jnp.where(lane == h, top_ref[h], tops)
        dens = jnp.where(lane == h, den_ref[h], dens)
    stats[0] = tops
    stats[1] = dens

    quarter_rows = rows // n_quarters

    def quarter_copies(r, slot, device):
        piece = pl.ds(r * quarter_rows, quarter_rows)
        return (
            pltpu.make_async_remote_copy(
                acc_ref.at[piece, :], acc_slots.at[slot], fsend.at[r, 0], frecv.at[slot, 0],
                device_id=device, device_id_type=mesh,
            ),
            pltpu.make_async_remote_copy(
                stats.at[:, piece, :], stat_slots.at[slot], fsend.at[r, 1], frecv.at[slot, 1],
                device_id=device, device_id_type=mesh,
            ),
        )

    for r in range(n_quarters):
        for copy in quarter_copies(r, quarter, (request, r, head_axis)):
            pl.when(r != quarter)(copy.start)
    mine = pl.ds(pl.multiple_of(quarter * quarter_rows, quarter_rows), quarter_rows)
    keep_acc = pltpu.make_async_copy(acc_ref.at[mine, :], acc_slots.at[quarter], fown.at[0])
    keep_stat = pltpu.make_async_copy(stats.at[:, mine, :], stat_slots.at[quarter], fown.at[1])
    keep_acc.start()
    keep_stat.start()
    keep_acc.wait()
    keep_stat.wait()
    for r in range(n_quarters):
        for copy in quarter_copies(r, r, (request, r, head_axis)):
            pl.when(r != quarter)(copy.wait_recv)
    for r in range(n_quarters):
        for copy in quarter_copies(r, quarter, (request, r, head_axis)):
            pl.when(r != quarter)(copy.wait_send)
    acc_out[...] = acc_slots[...]
    stat_out[...] = stat_slots[...]


def attend(info, query_block, keys_t, values, tree_keys_t, tree_values, tree_mask, n_quarters):
    rows, width = query_block.shape
    heads = width // HD
    n_hi = keys_t.shape[0]
    quarter_rows = rows // n_quarters
    vmem = pl.BlockSpec(memory_space=pltpu.VMEM)
    hbm = pl.BlockSpec(memory_space=pl.ANY)
    acc_shape = (n_quarters, quarter_rows, width)
    stat_shape = (n_quarters, 2, quarter_rows, HD)
    return pl.pallas_call(
        functools.partial(
            attend_kernel, scale=1.0 / math.sqrt(HD), n_hi=n_hi, n_quarters=n_quarters
        ),
        out_shape=(
            jax.ShapeDtypeStruct(acc_shape, jnp.float32),
            jax.ShapeDtypeStruct(stat_shape, jnp.float32),
        ),
        in_specs=[pl.BlockSpec(memory_space=pltpu.SMEM), vmem, hbm, hbm, vmem, vmem, vmem],
        out_specs=(vmem, vmem),
        scratch_shapes=[
            pltpu.VMEM(keys_t.shape, keys_t.dtype),
            pltpu.VMEM(values.shape, values.dtype),
            pltpu.SemaphoreType.DMA((n_hi, 2)),
            pltpu.SemaphoreType.DMA((n_hi, 2)),
            pltpu.SemaphoreType.DMA((2,)),
            pltpu.VMEM((rows, width), jnp.float32),
            pltpu.VMEM((heads, rows, HD), jnp.float32),
            pltpu.VMEM((heads, rows, HD), jnp.float32),
            pltpu.VMEM((2, rows, HD), jnp.float32),
            pltpu.VMEM(acc_shape, jnp.float32),
            pltpu.VMEM(stat_shape, jnp.float32),
            pltpu.SemaphoreType.DMA((n_quarters, 2)),
            pltpu.SemaphoreType.DMA((n_quarters, 2)),
            pltpu.SemaphoreType.DMA((2,)),
        ],
        compiler_params=pltpu.CompilerParams(
            collective_id=1, has_side_effects=True, vmem_limit_bytes=48 * 1024 * 1024
        ),
    )(info, query_block, keys_t, values, tree_keys_t, tree_values, tree_mask)


def exchange_kernel(src_ref, out_ref, slots, send_sem, recv_sem, own_sem, *, n_lo, n_head):
    request = lax.axis_index("rh")
    quarter = lax.axis_index("rl")
    head = lax.axis_index("head")
    me = quarter * n_head + head
    peers = n_lo * n_head
    mesh = pl.DeviceIdType.MESH

    barrier = pltpu.get_barrier_semaphore()
    for d in range(peers):
        dest = (request, d // n_head, d % n_head)

        @pl.when(d != me)
        def _():
            pl.semaphore_signal(barrier, inc=1, device_id=dest, device_id_type=mesh)

    pl.semaphore_wait(barrier, peers - 1)

    def push(d):
        return pltpu.make_async_remote_copy(
            src_ref.at[d % n_head],
            slots.at[me],
            send_sem.at[d],
            recv_sem.at[me],
            device_id=(request, d // n_head, d % n_head),
            device_id_type=mesh,
        )

    for d in range(peers):
        pl.when(d != me)(push(d).start)
    own = pltpu.make_async_copy(src_ref.at[head], slots.at[me], own_sem)
    own.start()
    own.wait()
    for d in range(peers):
        pl.when(d != me)(push(d).wait_send)
    for s in range(peers):
        arrival = pltpu.make_async_remote_copy(
            src_ref.at[0],
            slots.at[s],
            send_sem.at[s],
            recv_sem.at[s],
            device_id=(request, s // n_head, s % n_head),
            device_id_type=mesh,
        )
        pl.when(s != me)(arrival.wait_recv)
    out_ref[...] = slots[...]


def exchange_queries(pieces, n_lo, n_head):
    peers = n_lo * n_head
    shape = (peers,) + pieces.shape[1:]
    vmem = pl.BlockSpec(memory_space=pltpu.VMEM)
    return pl.pallas_call(
        functools.partial(exchange_kernel, n_lo=n_lo, n_head=n_head),
        out_shape=jax.ShapeDtypeStruct(shape, pieces.dtype),
        in_specs=[vmem],
        out_specs=vmem,
        scratch_shapes=[
            pltpu.VMEM(shape, pieces.dtype),
            pltpu.SemaphoreType.DMA((peers,)),
            pltpu.SemaphoreType.DMA((peers,)),
            pltpu.SemaphoreType.DMA(()),
        ],
        compiler_params=pltpu.CompilerParams(collective_id=0, has_side_effects=True),
    )(pieces)


def body(
    queries, cache_keys, cache_values, tree_keys, tree_values, parents, tree_sizes, cache_lens
):
    group_size = NH // KVH
    softmax_scale = 1.0 / math.sqrt(HD)
    request = lax.axis_index("rh")
    quarter = lax.axis_index("rl")
    n_lo = lax.axis_size("rl")
    n_hi = lax.axis_size("rh")
    cache_block = cache_keys.shape[1]
    kv_local = cache_keys.shape[2] // HD
    heads_local = kv_local * group_size
    node_count = parents.shape[1]
    rows_owned = tree_keys.shape[0]

    n_head = lax.axis_size("head")
    width = queries.shape[1] // n_head
    pieces = queries.reshape(queries.shape[0], n_head, width // HD, HD).transpose(1, 0, 2, 3)
    pieces = pieces.reshape(n_head, queries.shape[0] * width // HD, HD)
    query_block = exchange_queries(pieces, n_lo, n_head)
    query_block = query_block.reshape(node_count, width)

    reached = ancestry(parents)
    ancestors = lax.dynamic_index_in_dim(reached, request, 0, keepdims=False)
    ancestors = lax.dynamic_slice_in_dim(ancestors, quarter * rows_owned, rows_owned, 1)
    tree_mask = ancestors.astype(jnp.float32)
    length = lax.dynamic_index_in_dim(cache_lens, request, 0, keepdims=False)
    live_size = lax.dynamic_index_in_dim(tree_sizes, request, 0, keepdims=False)
    info = jnp.stack([length, jnp.int32(n_lo)]).astype(jnp.int32)
    keys_t = cache_keys.transpose(0, 2, 1)
    got_acc, got_stats = attend(
        info, query_block, keys_t, cache_values, tree_keys.T, tree_values, tree_mask, n_lo
    )
    got_acc = got_acc.reshape(n_lo, rows_owned, heads_local, HD)
    got_top = got_stats[:, 0, :, :heads_local]
    got_den = got_stats[:, 1, :, :heads_local]
    highest = jnp.max(got_top, axis=0)
    scale = jnp.exp(got_top - highest)
    num = jnp.sum(scale[..., None] * got_acc, axis=0)
    total = jnp.sum(scale * got_den, axis=0)
    merged = (num / total[..., None]).reshape(rows_owned, heads_local * HD)

    row_nodes = quarter * rows_owned + jnp.arange(rows_owned, dtype=jnp.int32)
    live_rows = row_nodes < live_size
    return jnp.where(live_rows[:, None], merged, 0.0).astype(jnp.bfloat16)


def solution(mesh):
    def run(queries, cache_keys, cache_values, tree_keys, tree_values, parents, tree_sizes, cache_lens):
        n_hi = cache_keys.shape[0]
        n_lo = mesh.shape["req"] // n_hi
        split = Mesh(mesh.devices.reshape(n_hi, n_lo, mesh.shape["head"]), ("rh", "rl", "head"))
        rows = ("rh", "rl")
        placed = (
            P(("rh", "rl", "head"), None),
            P(None, rows, "head"),
            P(None, rows, "head"),
            P(rows, "head"),
            P(rows, "head"),
            P(),
            P(),
            P(),
        )
        return jax.shard_map(
            body, mesh=split, in_specs=placed, out_specs=P(rows, "head"), check_vma=False
        )(queries, cache_keys, cache_values, tree_keys, tree_values, parents, tree_sizes, cache_lens)

    return run
```

```python
import functools
import math

import jax
import jax.numpy as jnp
from jax import lax
from jax.experimental import pallas as pl
from jax.experimental.pallas import tpu as pltpu
from jax.sharding import Mesh
from jax.sharding import PartitionSpec as P

NH = 128
KVH = 8
HD = 128


negative_fill = -1e30


def ancestry(parents):
    node_count = parents.shape[1]
    node_ids = jnp.arange(node_count, dtype=jnp.int32)
    linked = jnp.logical_or(
        parents[:, :, None] == node_ids[None, None, :], node_ids[:, None] == node_ids[None, :]
    )
    reached = linked.astype(jnp.bfloat16)
    for doubling in range((node_count - 1).bit_length()):
        squared = jnp.einsum("aij,ajk->aik", reached, reached, preferred_element_type=jnp.float32)
        reached = jnp.minimum(squared, 1.0).astype(jnp.bfloat16)
    return reached


def attend_kernel(
    info_ref, q_ref, kt_hbm, v_hbm, tkt_ref, tv_ref, tmask_ref, acc_out, stat_out,
    kslots, vslots, send_sem, recv_sem, own_sem, acc_ref, top_ref, den_ref, stats,
    acc_slots, stat_slots, fsend, frecv, fown, *, scale, n_hi, n_quarters,
):
    request = lax.axis_index("rh")
    quarter = lax.axis_index("rl")
    head_axis = lax.axis_index("head")
    mesh = pl.DeviceIdType.MESH
    length = info_ref[0]
    n_lo = info_ref[1]
    rows = q_ref.shape[0]
    heads = q_ref.shape[1] // HD
    block_len = kt_hbm.shape[2]

    barrier = pltpu.get_barrier_semaphore()
    for t in range(n_hi):

        @pl.when(t != request)
        def _():
            pl.semaphore_signal(
                barrier, inc=1, device_id=(t, quarter, head_axis), device_id_type=mesh
            )

    for r in range(n_quarters):

        @pl.when(r != quarter)
        def _():
            pl.semaphore_signal(
                barrier, inc=1, device_id=(request, r, head_axis), device_id_type=mesh
            )

    pl.semaphore_wait(barrier, n_hi - 1 + n_quarters - 1)

    def pushes(t):
        dest = (t, quarter, head_axis)
        return (
            pltpu.make_async_remote_copy(
                kt_hbm.at[t], kslots.at[request], send_sem.at[t, 0], recv_sem.at[request, 0],
                device_id=dest, device_id_type=mesh,
            ),
            pltpu.make_async_remote_copy(
                v_hbm.at[t], vslots.at[request], send_sem.at[t, 1], recv_sem.at[request, 1],
                device_id=dest, device_id_type=mesh,
            ),
        )

    ahead = 2
    for shift in range(1, min(ahead, n_hi - 1) + 1):
        t = lax.rem(request + shift, n_hi)
        for copy in pushes(t):
            copy.start()
    own_k = pltpu.make_async_copy(kt_hbm.at[request], kslots.at[request], own_sem.at[0])
    own_v = pltpu.make_async_copy(v_hbm.at[request], vslots.at[request], own_sem.at[1])
    own_k.start()
    own_v.start()

    acc_ref[...] = jnp.zeros_like(acc_ref)
    top_ref[...] = jnp.full_like(top_ref, negative_fill)
    den_ref[...] = jnp.zeros_like(den_ref)

    def group(s, with_tree):
        start = (s * n_lo + quarter) * block_len
        kt_ref = kslots.at[s]
        v_ref = vslots.at[s]
        pos = start + lax.broadcasted_iota(jnp.int32, (1, block_len), 1)
        bias = jnp.where(pos < length, 0.0, negative_fill)

        def pair(p, carry):
            col = pl.multiple_of(p * 2 * HD, 2 * HD)
            both = q_ref[:, pl.ds(col, 2 * HD)]
            qh = jnp.concatenate([both[:, :HD], both[:, HD:]], axis=0)
            sc = jnp.dot(qh, kt_ref[...], preferred_element_type=jnp.float32) * scale + bias
            peak = jnp.max(sc, axis=1, keepdims=True)
            if with_tree:
                st = jnp.dot(qh, tkt_ref[...], preferred_element_type=jnp.float32) * scale
                tlive = jnp.concatenate([tmask_ref[...], tmask_ref[...]], axis=0) > 0.5
                st = jnp.where(tlive, st, negative_fill)
                peak = jnp.maximum(peak, jnp.max(st, axis=1, keepdims=True))
            w = jnp.exp(sc - jnp.maximum(peak, 0.1 * negative_fill))
            tot = jnp.sum(w, axis=1, keepdims=True)
            gs = jnp.dot(w.astype(jnp.bfloat16), v_ref[...], preferred_element_type=jnp.float32)
            if with_tree:
                wt = jnp.where(tlive, jnp.exp(st - peak), 0.0)
                tot = tot + jnp.sum(wt, axis=1, keepdims=True)
                gs = gs + jnp.dot(
                    wt.astype(jnp.bfloat16), tv_ref[...], preferred_element_type=jnp.float32
                )
            floored = jnp.maximum(tot, 1.0)
            part = gs / floored
            lt = peak + jnp.log(floored)
            for half in range(2):
                h = 2 * p + half
                hcol = pl.multiple_of(h * HD, HD)
                lt_h = lt[half * rows : (half + 1) * rows]
                part_h = part[half * rows : (half + 1) * rows]
                old = top_ref[h][:, :1]
                new = jnp.maximum(old, lt_h)
                keep = jnp.exp(old - new)
                add = jnp.exp(lt_h - new)
                acc_ref[:, pl.ds(hcol, HD)] = keep * acc_ref[:, pl.ds(hcol, HD)] + add * part_h
                den_ref[h] = jnp.broadcast_to(keep * den_ref[h][:, :1] + add, (rows, HD))
                top_ref[h] = jnp.broadcast_to(new, (rows, HD))
            return carry

        lax.fori_loop(0, heads // 2, pair, 0, unroll=2)

    own_k.wait()
    own_v.wait()
    group(request, True)

    def landed(s):
        source = (s, quarter, head_axis)
        return (
            pltpu.make_async_remote_copy(
                kt_hbm.at[s], kslots.at[s], send_sem.at[s, 0], recv_sem.at[s, 0],
                device_id=source, device_id_type=mesh,
            ),
            pltpu.make_async_remote_copy(
                v_hbm.at[s], vslots.at[s], send_sem.at[s, 1], recv_sem.at[s, 1],
                device_id=source, device_id_type=mesh,
            ),
        )

    def arrival(step, carry):
        @pl.when(step + ahead + 1 < n_hi)
        def _():
            t = lax.rem(request + step + ahead + 1, n_hi)
            for copy in pushes(t):
                copy.start()

        s = lax.rem(request - step - 1 + n_hi, n_hi)
        for copy in landed(s):
            copy.wait_recv()
        group(s, False)
        return carry

    lax.fori_loop(0, n_hi - 1, arrival, 0)
    for shift in range(1, n_hi):
        t = lax.rem(request + shift, n_hi)
        for copy in pushes(t):
            copy.wait_send()

    lane = lax.broadcasted_iota(jnp.int32, (rows, HD), 1)
    tops = jnp.full((rows, HD), negative_fill, jnp.float32)
    dens = jnp.zeros((rows, HD), jnp.float32)
    for h in range(heads):
        tops = jnp.where(lane == h, top_ref[h], tops)
        dens = jnp.where(lane == h, den_ref[h], dens)
    stats[0] = tops
    stats[1] = dens

    quarter_rows = rows // n_quarters

    def quarter_copies(r, slot, device):
        piece = pl.ds(r * quarter_rows, quarter_rows)
        return (
            pltpu.make_async_remote_copy(
                acc_ref.at[piece, :], acc_slots.at[slot], fsend.at[r, 0], frecv.at[slot, 0],
                device_id=device, device_id_type=mesh,
            ),
            pltpu.make_async_remote_copy(
                stats.at[:, piece, :], stat_slots.at[slot], fsend.at[r, 1], frecv.at[slot, 1],
                device_id=device, device_id_type=mesh,
            ),
        )

    for r in range(n_quarters):
        for copy in quarter_copies(r, quarter, (request, r, head_axis)):
            pl.when(r != quarter)(copy.start)
    mine = pl.ds(pl.multiple_of(quarter * quarter_rows, quarter_rows), quarter_rows)
    keep_acc = pltpu.make_async_copy(acc_ref.at[mine, :], acc_slots.at[quarter], fown.at[0])
    keep_stat = pltpu.make_async_copy(stats.at[:, mine, :], stat_slots.at[quarter], fown.at[1])
    keep_acc.start()
    keep_stat.start()
    keep_acc.wait()
    keep_stat.wait()
    for r in range(n_quarters):
        for copy in quarter_copies(r, r, (request, r, head_axis)):
            pl.when(r != quarter)(copy.wait_recv)
    for r in range(n_quarters):
        for copy in quarter_copies(r, quarter, (request, r, head_axis)):
            pl.when(r != quarter)(copy.wait_send)
    acc_out[...] = acc_slots[...]
    stat_out[...] = stat_slots[...]


def attend(info, query_block, keys_t, values, tree_keys_t, tree_values, tree_mask, n_quarters):
    rows, width = query_block.shape
    heads = width // HD
    n_hi = keys_t.shape[0]
    quarter_rows = rows // n_quarters
    vmem = pl.BlockSpec(memory_space=pltpu.VMEM)
    hbm = pl.BlockSpec(memory_space=pl.ANY)
    acc_shape = (n_quarters, quarter_rows, width)
    stat_shape = (n_quarters, 2, quarter_rows, HD)
    return pl.pallas_call(
        functools.partial(
            attend_kernel, scale=1.0 / math.sqrt(HD), n_hi=n_hi, n_quarters=n_quarters
        ),
        out_shape=(
            jax.ShapeDtypeStruct(acc_shape, jnp.float32),
            jax.ShapeDtypeStruct(stat_shape, jnp.float32),
        ),
        in_specs=[pl.BlockSpec(memory_space=pltpu.SMEM), vmem, hbm, hbm, vmem, vmem, vmem],
        out_specs=(vmem, vmem),
        scratch_shapes=[
            pltpu.VMEM(keys_t.shape, keys_t.dtype),
            pltpu.VMEM(values.shape, values.dtype),
            pltpu.SemaphoreType.DMA((n_hi, 2)),
            pltpu.SemaphoreType.DMA((n_hi, 2)),
            pltpu.SemaphoreType.DMA((2,)),
            pltpu.VMEM((rows, width), jnp.float32),
            pltpu.VMEM((heads, rows, HD), jnp.float32),
            pltpu.VMEM((heads, rows, HD), jnp.float32),
            pltpu.VMEM((2, rows, HD), jnp.float32),
            pltpu.VMEM(acc_shape, jnp.float32),
            pltpu.VMEM(stat_shape, jnp.float32),
            pltpu.SemaphoreType.DMA((n_quarters, 2)),
            pltpu.SemaphoreType.DMA((n_quarters, 2)),
            pltpu.SemaphoreType.DMA((2,)),
        ],
        compiler_params=pltpu.CompilerParams(
            collective_id=1, has_side_effects=True, vmem_limit_bytes=48 * 1024 * 1024
        ),
    )(info, query_block, keys_t, values, tree_keys_t, tree_values, tree_mask)


def exchange_kernel(src_ref, out_ref, slots, send_sem, recv_sem, own_sem, *, n_lo, n_head):
    request = lax.axis_index("rh")
    quarter = lax.axis_index("rl")
    head = lax.axis_index("head")
    me = quarter * n_head + head
    peers = n_lo * n_head
    mesh = pl.DeviceIdType.MESH

    barrier = pltpu.get_barrier_semaphore()
    for d in range(peers):
        dest = (request, d // n_head, d % n_head)

        @pl.when(d != me)
        def _():
            pl.semaphore_signal(barrier, inc=1, device_id=dest, device_id_type=mesh)

    pl.semaphore_wait(barrier, peers - 1)

    def push(d):
        return pltpu.make_async_remote_copy(
            src_ref.at[d % n_head],
            slots.at[me],
            send_sem.at[d],
            recv_sem.at[me],
            device_id=(request, d // n_head, d % n_head),
            device_id_type=mesh,
        )

    for d in range(peers):
        pl.when(d != me)(push(d).start)
    own = pltpu.make_async_copy(src_ref.at[head], slots.at[me], own_sem)
    own.start()
    own.wait()
    for d in range(peers):
        pl.when(d != me)(push(d).wait_send)
    for s in range(peers):
        arrival = pltpu.make_async_remote_copy(
            src_ref.at[0],
            slots.at[s],
            send_sem.at[s],
            recv_sem.at[s],
            device_id=(request, s // n_head, s % n_head),
            device_id_type=mesh,
        )
        pl.when(s != me)(arrival.wait_recv)
    out_ref[...] = slots[...]


def exchange_queries(pieces, n_lo, n_head):
    peers = n_lo * n_head
    shape = (peers,) + pieces.shape[1:]
    vmem = pl.BlockSpec(memory_space=pltpu.VMEM)
    return pl.pallas_call(
        functools.partial(exchange_kernel, n_lo=n_lo, n_head=n_head),
        out_shape=jax.ShapeDtypeStruct(shape, pieces.dtype),
        in_specs=[vmem],
        out_specs=vmem,
        scratch_shapes=[
            pltpu.VMEM(shape, pieces.dtype),
            pltpu.SemaphoreType.DMA((peers,)),
            pltpu.SemaphoreType.DMA((peers,)),
            pltpu.SemaphoreType.DMA(()),
        ],
        compiler_params=pltpu.CompilerParams(collective_id=0, has_side_effects=True),
    )(pieces)


def body(
    queries, cache_keys, cache_values, tree_keys, tree_values, parents, tree_sizes, cache_lens
):
    group_size = NH // KVH
    softmax_scale = 1.0 / math.sqrt(HD)
    request = lax.axis_index("rh")
    quarter = lax.axis_index("rl")
    n_lo = lax.axis_size("rl")
    n_hi = lax.axis_size("rh")
    cache_block = cache_keys.shape[1]
    kv_local = cache_keys.shape[2] // HD
    heads_local = kv_local * group_size
    node_count = parents.shape[1]
    rows_owned = tree_keys.shape[0]

    n_head = lax.axis_size("head")
    width = queries.shape[1] // n_head
    pieces = queries.reshape(queries.shape[0], n_head, width // HD, HD).transpose(1, 0, 2, 3)
    pieces = pieces.reshape(n_head, queries.shape[0] * width // HD, HD)
    query_block = exchange_queries(pieces, n_lo, n_head)
    query_block = query_block.reshape(node_count, width)

    reached = ancestry(parents)
    ancestors = lax.dynamic_index_in_dim(reached, request, 0, keepdims=False)
    ancestors = lax.dynamic_slice_in_dim(ancestors, quarter * rows_owned, rows_owned, 1)
    tree_mask = ancestors.astype(jnp.float32)
    length = lax.dynamic_index_in_dim(cache_lens, request, 0, keepdims=False)
    live_size = lax.dynamic_index_in_dim(tree_sizes, request, 0, keepdims=False)
    info = jnp.stack([length, jnp.int32(n_lo)]).astype(jnp.int32)
    keys_t = cache_keys.transpose(0, 2, 1)
    got_acc, got_stats = attend(
        info, query_block, keys_t, cache_values, tree_keys.T, tree_values, tree_mask, n_lo
    )
    got_acc = got_acc.reshape(n_lo, rows_owned, heads_local, HD)
    got_top = got_stats[:, 0, :, :heads_local]
    got_den = got_stats[:, 1, :, :heads_local]
    highest = jnp.max(got_top, axis=0)
    scale = jnp.exp(got_top - highest)
    num = jnp.sum(scale[..., None] * got_acc, axis=0)
    total = jnp.sum(scale * got_den, axis=0)
    merged = (num / total[..., None]).reshape(rows_owned, heads_local * HD)

    row_nodes = quarter * rows_owned + jnp.arange(rows_owned, dtype=jnp.int32)
    live_rows = row_nodes < live_size
    return jnp.where(live_rows[:, None], merged, 0.0).astype(jnp.bfloat16)


def solution(mesh):
    def run(queries, cache_keys, cache_values, tree_keys, tree_values, parents, tree_sizes, cache_lens):
        n_hi = cache_keys.shape[0]
        n_lo = mesh.shape["req"] // n_hi
        split = Mesh(mesh.devices.reshape(n_hi, n_lo, mesh.shape["head"]), ("rh", "rl", "head"))
        rows = ("rh", "rl")
        placed = (
            P(("rh", "rl", "head"), None),
            P(None, rows, "head"),
            P(None, rows, "head"),
            P(rows, "head"),
            P(rows, "head"),
            P(),
            P(),
            P(),
        )
        return jax.shard_map(
            body, mesh=split, in_specs=placed, out_specs=P(rows, "head"), check_vma=False
        )(queries, cache_keys, cache_values, tree_keys, tree_values, parents, tree_sizes, cache_lens)

    return run
```

```python
import functools
import math

import jax
import jax.numpy as jnp
from jax import lax
from jax.experimental import pallas as pl
from jax.experimental.pallas import tpu as pltpu
from jax.sharding import Mesh
from jax.sharding import PartitionSpec as P

NH = 128
KVH = 8
HD = 128


negative_fill = -1e30


def ancestry(parents):
    node_count = parents.shape[1]
    node_ids = jnp.arange(node_count, dtype=jnp.int32)
    linked = jnp.logical_or(
        parents[:, :, None] == node_ids[None, None, :], node_ids[:, None] == node_ids[None, :]
    )
    reached = linked.astype(jnp.bfloat16)
    for doubling in range((node_count - 1).bit_length()):
        squared = jnp.einsum("aij,ajk->aik", reached, reached, preferred_element_type=jnp.float32)
        reached = jnp.minimum(squared, 1.0).astype(jnp.bfloat16)
    return reached


def attend_kernel(
    info_ref, q_ref, kt_hbm, v_hbm, tkt_ref, tv_ref, tmask_ref, acc_out, stat_out,
    kslots, vslots, send_sem, recv_sem, own_sem, acc_ref, top_ref, den_ref, stats,
    acc_slots, stat_slots, fsend, frecv, fown, *, scale, n_hi, n_quarters,
):
    request = lax.axis_index("rh")
    quarter = lax.axis_index("rl")
    head_axis = lax.axis_index("head")
    mesh = pl.DeviceIdType.MESH
    length = info_ref[0]
    n_lo = info_ref[1]
    rows = q_ref.shape[0]
    heads = q_ref.shape[1] // HD
    block_len = kt_hbm.shape[2]

    barrier = pltpu.get_barrier_semaphore()
    for t in range(n_hi):

        @pl.when(t != request)
        def _():
            pl.semaphore_signal(
                barrier, inc=1, device_id=(t, quarter, head_axis), device_id_type=mesh
            )

    for r in range(n_quarters):

        @pl.when(r != quarter)
        def _():
            pl.semaphore_signal(
                barrier, inc=1, device_id=(request, r, head_axis), device_id_type=mesh
            )

    pl.semaphore_wait(barrier, n_hi - 1 + n_quarters - 1)

    def pushes(t):
        dest = (t, quarter, head_axis)
        return (
            pltpu.make_async_remote_copy(
                kt_hbm.at[t], kslots.at[request], send_sem.at[t, 0], recv_sem.at[request, 0],
                device_id=dest, device_id_type=mesh,
            ),
            pltpu.make_async_remote_copy(
                v_hbm.at[t], vslots.at[request], send_sem.at[t, 1], recv_sem.at[request, 1],
                device_id=dest, device_id_type=mesh,
            ),
        )

    ahead = 2
    for shift in range(1, min(ahead, n_hi - 1) + 1):
        t = lax.rem(request + shift, n_hi)
        for copy in pushes(t):
            copy.start()
    own_k = pltpu.make_async_copy(kt_hbm.at[request], kslots.at[request], own_sem.at[0])
    own_v = pltpu.make_async_copy(v_hbm.at[request], vslots.at[request], own_sem.at[1])
    own_k.start()
    own_v.start()

    acc_ref[...] = jnp.zeros_like(acc_ref)
    top_ref[...] = jnp.full_like(top_ref, negative_fill)
    den_ref[...] = jnp.zeros_like(den_ref)

    def group(s, with_tree):
        start = (s * n_lo + quarter) * block_len
        kt_ref = kslots.at[s]
        v_ref = vslots.at[s]
        pos = start + lax.broadcasted_iota(jnp.int32, (1, block_len), 1)
        bias = jnp.where(pos < length, 0.0, negative_fill)

        stack = 4

        def pair(p, carry):
            col = pl.multiple_of(p * stack * HD, stack * HD)
            both = q_ref[:, pl.ds(col, stack * HD)]
            qh = jnp.concatenate([both[:, i * HD : (i + 1) * HD] for i in range(stack)], axis=0)
            sc = jnp.dot(qh, kt_ref[...], preferred_element_type=jnp.float32) * scale + bias
            peak = jnp.max(sc, axis=1, keepdims=True)
            if with_tree:
                st = jnp.dot(qh, tkt_ref[...], preferred_element_type=jnp.float32) * scale
                tlive = jnp.concatenate([tmask_ref[...]] * stack, axis=0) > 0.5
                st = jnp.where(tlive, st, negative_fill)
                peak = jnp.maximum(peak, jnp.max(st, axis=1, keepdims=True))
            w = jnp.exp(sc - jnp.maximum(peak, 0.1 * negative_fill))
            tot = jnp.sum(w, axis=1, keepdims=True)
            gs = jnp.dot(w.astype(jnp.bfloat16), v_ref[...], preferred_element_type=jnp.float32)
            if with_tree:
                wt = jnp.where(tlive, jnp.exp(st - peak), 0.0)
                tot = tot + jnp.sum(wt, axis=1, keepdims=True)
                gs = gs + jnp.dot(
                    wt.astype(jnp.bfloat16), tv_ref[...], preferred_element_type=jnp.float32
                )
            floored = jnp.maximum(tot, 1.0)
            part = gs / floored
            lt = peak + jnp.log(floored)
            for half in range(stack):
                h = stack * p + half
                hcol = pl.multiple_of(h * HD, HD)
                lt_h = lt[half * rows : (half + 1) * rows]
                part_h = part[half * rows : (half + 1) * rows]
                old = top_ref[h][:, :1]
                new = jnp.maximum(old, lt_h)
                keep = jnp.exp(old - new)
                add = jnp.exp(lt_h - new)
                acc_ref[:, pl.ds(hcol, HD)] = keep * acc_ref[:, pl.ds(hcol, HD)] + add * part_h
                den_ref[h] = jnp.broadcast_to(keep * den_ref[h][:, :1] + add, (rows, HD))
                top_ref[h] = jnp.broadcast_to(new, (rows, HD))
            return carry

        lax.fori_loop(0, heads // stack, pair, 0)

    own_k.wait()
    own_v.wait()
    group(request, True)

    def landed(s):
        source = (s, quarter, head_axis)
        return (
            pltpu.make_async_remote_copy(
                kt_hbm.at[s], kslots.at[s], send_sem.at[s, 0], recv_sem.at[s, 0],
                device_id=source, device_id_type=mesh,
            ),
            pltpu.make_async_remote_copy(
                v_hbm.at[s], vslots.at[s], send_sem.at[s, 1], recv_sem.at[s, 1],
                device_id=source, device_id_type=mesh,
            ),
        )

    def arrival(step, carry):
        @pl.when(step + ahead + 1 < n_hi)
        def _():
            t = lax.rem(request + step + ahead + 1, n_hi)
            for copy in pushes(t):
                copy.start()

        s = lax.rem(request - step - 1 + n_hi, n_hi)
        for copy in landed(s):
            copy.wait_recv()
        group(s, False)
        return carry

    lax.fori_loop(0, n_hi - 1, arrival, 0)
    for shift in range(1, n_hi):
        t = lax.rem(request + shift, n_hi)
        for copy in pushes(t):
            copy.wait_send()

    lane = lax.broadcasted_iota(jnp.int32, (rows, HD), 1)
    tops = jnp.full((rows, HD), negative_fill, jnp.float32)
    dens = jnp.zeros((rows, HD), jnp.float32)
    for h in range(heads):
        tops = jnp.where(lane == h, top_ref[h], tops)
        dens = jnp.where(lane == h, den_ref[h], dens)
    stats[0] = tops
    stats[1] = dens

    quarter_rows = rows // n_quarters

    def quarter_copies(r, slot, device):
        piece = pl.ds(r * quarter_rows, quarter_rows)
        return (
            pltpu.make_async_remote_copy(
                acc_ref.at[piece, :], acc_slots.at[slot], fsend.at[r, 0], frecv.at[slot, 0],
                device_id=device, device_id_type=mesh,
            ),
            pltpu.make_async_remote_copy(
                stats.at[:, piece, :], stat_slots.at[slot], fsend.at[r, 1], frecv.at[slot, 1],
                device_id=device, device_id_type=mesh,
            ),
        )

    for r in range(n_quarters):
        for copy in quarter_copies(r, quarter, (request, r, head_axis)):
            pl.when(r != quarter)(copy.start)
    mine = pl.ds(pl.multiple_of(quarter * quarter_rows, quarter_rows), quarter_rows)
    keep_acc = pltpu.make_async_copy(acc_ref.at[mine, :], acc_slots.at[quarter], fown.at[0])
    keep_stat = pltpu.make_async_copy(stats.at[:, mine, :], stat_slots.at[quarter], fown.at[1])
    keep_acc.start()
    keep_stat.start()
    keep_acc.wait()
    keep_stat.wait()
    for r in range(n_quarters):
        for copy in quarter_copies(r, r, (request, r, head_axis)):
            pl.when(r != quarter)(copy.wait_recv)
    for r in range(n_quarters):
        for copy in quarter_copies(r, quarter, (request, r, head_axis)):
            pl.when(r != quarter)(copy.wait_send)
    acc_out[...] = acc_slots[...]
    stat_out[...] = stat_slots[...]


def attend(info, query_block, keys_t, values, tree_keys_t, tree_values, tree_mask, n_quarters):
    rows, width = query_block.shape
    heads = width // HD
    n_hi = keys_t.shape[0]
    quarter_rows = rows // n_quarters
    vmem = pl.BlockSpec(memory_space=pltpu.VMEM)
    hbm = pl.BlockSpec(memory_space=pl.ANY)
    acc_shape = (n_quarters, quarter_rows, width)
    stat_shape = (n_quarters, 2, quarter_rows, HD)
    return pl.pallas_call(
        functools.partial(
            attend_kernel, scale=1.0 / math.sqrt(HD), n_hi=n_hi, n_quarters=n_quarters
        ),
        out_shape=(
            jax.ShapeDtypeStruct(acc_shape, jnp.float32),
            jax.ShapeDtypeStruct(stat_shape, jnp.float32),
        ),
        in_specs=[pl.BlockSpec(memory_space=pltpu.SMEM), vmem, hbm, hbm, vmem, vmem, vmem],
        out_specs=(vmem, vmem),
        scratch_shapes=[
            pltpu.VMEM(keys_t.shape, keys_t.dtype),
            pltpu.VMEM(values.shape, values.dtype),
            pltpu.SemaphoreType.DMA((n_hi, 2)),
            pltpu.SemaphoreType.DMA((n_hi, 2)),
            pltpu.SemaphoreType.DMA((2,)),
            pltpu.VMEM((rows, width), jnp.float32),
            pltpu.VMEM((heads, rows, HD), jnp.float32),
            pltpu.VMEM((heads, rows, HD), jnp.float32),
            pltpu.VMEM((2, rows, HD), jnp.float32),
            pltpu.VMEM(acc_shape, jnp.float32),
            pltpu.VMEM(stat_shape, jnp.float32),
            pltpu.SemaphoreType.DMA((n_quarters, 2)),
            pltpu.SemaphoreType.DMA((n_quarters, 2)),
            pltpu.SemaphoreType.DMA((2,)),
        ],
        compiler_params=pltpu.CompilerParams(
            collective_id=1, has_side_effects=True, vmem_limit_bytes=48 * 1024 * 1024
        ),
    )(info, query_block, keys_t, values, tree_keys_t, tree_values, tree_mask)


def exchange_kernel(src_ref, out_ref, slots, send_sem, recv_sem, own_sem, *, n_lo, n_head):
    request = lax.axis_index("rh")
    quarter = lax.axis_index("rl")
    head = lax.axis_index("head")
    me = quarter * n_head + head
    peers = n_lo * n_head
    mesh = pl.DeviceIdType.MESH

    barrier = pltpu.get_barrier_semaphore()
    for d in range(peers):
        dest = (request, d // n_head, d % n_head)

        @pl.when(d != me)
        def _():
            pl.semaphore_signal(barrier, inc=1, device_id=dest, device_id_type=mesh)

    pl.semaphore_wait(barrier, peers - 1)

    def push(d):
        return pltpu.make_async_remote_copy(
            src_ref.at[d % n_head],
            slots.at[me],
            send_sem.at[d],
            recv_sem.at[me],
            device_id=(request, d // n_head, d % n_head),
            device_id_type=mesh,
        )

    for d in range(peers):
        pl.when(d != me)(push(d).start)
    own = pltpu.make_async_copy(src_ref.at[head], slots.at[me], own_sem)
    own.start()
    own.wait()
    for d in range(peers):
        pl.when(d != me)(push(d).wait_send)
    for s in range(peers):
        arrival = pltpu.make_async_remote_copy(
            src_ref.at[0],
            slots.at[s],
            send_sem.at[s],
            recv_sem.at[s],
            device_id=(request, s // n_head, s % n_head),
            device_id_type=mesh,
        )
        pl.when(s != me)(arrival.wait_recv)
    out_ref[...] = slots[...]


def exchange_queries(pieces, n_lo, n_head):
    peers = n_lo * n_head
    shape = (peers,) + pieces.shape[1:]
    vmem = pl.BlockSpec(memory_space=pltpu.VMEM)
    return pl.pallas_call(
        functools.partial(exchange_kernel, n_lo=n_lo, n_head=n_head),
        out_shape=jax.ShapeDtypeStruct(shape, pieces.dtype),
        in_specs=[vmem],
        out_specs=vmem,
        scratch_shapes=[
            pltpu.VMEM(shape, pieces.dtype),
            pltpu.SemaphoreType.DMA((peers,)),
            pltpu.SemaphoreType.DMA((peers,)),
            pltpu.SemaphoreType.DMA(()),
        ],
        compiler_params=pltpu.CompilerParams(collective_id=0, has_side_effects=True),
    )(pieces)


def body(
    queries, cache_keys, cache_values, tree_keys, tree_values, parents, tree_sizes, cache_lens
):
    group_size = NH // KVH
    softmax_scale = 1.0 / math.sqrt(HD)
    request = lax.axis_index("rh")
    quarter = lax.axis_index("rl")
    n_lo = lax.axis_size("rl")
    n_hi = lax.axis_size("rh")
    cache_block = cache_keys.shape[1]
    kv_local = cache_keys.shape[2] // HD
    heads_local = kv_local * group_size
    node_count = parents.shape[1]
    rows_owned = tree_keys.shape[0]

    n_head = lax.axis_size("head")
    width = queries.shape[1] // n_head
    pieces = queries.reshape(queries.shape[0], n_head, width // HD, HD).transpose(1, 0, 2, 3)
    pieces = pieces.reshape(n_head, queries.shape[0] * width // HD, HD)
    query_block = exchange_queries(pieces, n_lo, n_head)
    query_block = query_block.reshape(node_count, width)

    reached = ancestry(parents)
    ancestors = lax.dynamic_index_in_dim(reached, request, 0, keepdims=False)
    ancestors = lax.dynamic_slice_in_dim(ancestors, quarter * rows_owned, rows_owned, 1)
    tree_mask = ancestors.astype(jnp.float32)
    length = lax.dynamic_index_in_dim(cache_lens, request, 0, keepdims=False)
    live_size = lax.dynamic_index_in_dim(tree_sizes, request, 0, keepdims=False)
    info = jnp.stack([length, jnp.int32(n_lo)]).astype(jnp.int32)
    keys_t = cache_keys.transpose(0, 2, 1)
    got_acc, got_stats = attend(
        info, query_block, keys_t, cache_values, tree_keys.T, tree_values, tree_mask, n_lo
    )
    got_acc = got_acc.reshape(n_lo, rows_owned, heads_local, HD)
    got_top = got_stats[:, 0, :, :heads_local]
    got_den = got_stats[:, 1, :, :heads_local]
    highest = jnp.max(got_top, axis=0)
    scale = jnp.exp(got_top - highest)
    num = jnp.sum(scale[..., None] * got_acc, axis=0)
    total = jnp.sum(scale * got_den, axis=0)
    merged = (num / total[..., None]).reshape(rows_owned, heads_local * HD)

    row_nodes = quarter * rows_owned + jnp.arange(rows_owned, dtype=jnp.int32)
    live_rows = row_nodes < live_size
    return jnp.where(live_rows[:, None], merged, 0.0).astype(jnp.bfloat16)


def solution(mesh):
    def run(queries, cache_keys, cache_values, tree_keys, tree_values, parents, tree_sizes, cache_lens):
        n_hi = cache_keys.shape[0]
        n_lo = mesh.shape["req"] // n_hi
        split = Mesh(mesh.devices.reshape(n_hi, n_lo, mesh.shape["head"]), ("rh", "rl", "head"))
        rows = ("rh", "rl")
        placed = (
            P(("rh", "rl", "head"), None),
            P(None, rows, "head"),
            P(None, rows, "head"),
            P(rows, "head"),
            P(rows, "head"),
            P(),
            P(),
            P(),
        )
        return jax.shard_map(
            body, mesh=split, in_specs=placed, out_specs=P(rows, "head"), check_vma=False
        )(queries, cache_keys, cache_values, tree_keys, tree_values, parents, tree_sizes, cache_lens)

    return run
```

```python
import functools
import math

import jax
import jax.numpy as jnp
from jax import lax
from jax.experimental import pallas as pl
from jax.experimental.pallas import tpu as pltpu
from jax.sharding import Mesh
from jax.sharding import PartitionSpec as P

NH = 128
KVH = 8
HD = 128


negative_fill = -1e30


def ancestry(parents):
    node_count = parents.shape[1]
    node_ids = jnp.arange(node_count, dtype=jnp.int32)
    linked = jnp.logical_or(
        parents[:, :, None] == node_ids[None, None, :], node_ids[:, None] == node_ids[None, :]
    )
    reached = linked.astype(jnp.bfloat16)
    for doubling in range((node_count - 1).bit_length()):
        squared = jnp.einsum("aij,ajk->aik", reached, reached, preferred_element_type=jnp.float32)
        reached = jnp.minimum(squared, 1.0).astype(jnp.bfloat16)
    return reached


def attend_kernel(
    info_ref, q_ref, kt_hbm, v_hbm, tkt_ref, tv_ref, tmask_ref, acc_out, stat_out,
    kslots, vslots, send_sem, recv_sem, own_sem, acc_ref, top_ref, den_ref, stats,
    acc_slots, stat_slots, fsend, frecv, fown, *, scale, n_hi, n_quarters,
):
    request = lax.axis_index("rh")
    quarter = lax.axis_index("rl")
    head_axis = lax.axis_index("head")
    mesh = pl.DeviceIdType.MESH
    length = info_ref[0]
    n_lo = info_ref[1]
    rows = q_ref.shape[0]
    heads = q_ref.shape[1] // HD
    block_len = kt_hbm.shape[2]

    barrier = pltpu.get_barrier_semaphore()
    for t in range(n_hi):

        @pl.when(t != request)
        def _():
            pl.semaphore_signal(
                barrier, inc=1, device_id=(t, quarter, head_axis), device_id_type=mesh
            )

    for r in range(n_quarters):

        @pl.when(r != quarter)
        def _():
            pl.semaphore_signal(
                barrier, inc=1, device_id=(request, r, head_axis), device_id_type=mesh
            )

    pl.semaphore_wait(barrier, n_hi - 1 + n_quarters - 1)

    def pushes(t):
        dest = (t, quarter, head_axis)
        return (
            pltpu.make_async_remote_copy(
                kt_hbm.at[t], kslots.at[request], send_sem.at[t, 0], recv_sem.at[request, 0],
                device_id=dest, device_id_type=mesh,
            ),
            pltpu.make_async_remote_copy(
                v_hbm.at[t], vslots.at[request], send_sem.at[t, 1], recv_sem.at[request, 1],
                device_id=dest, device_id_type=mesh,
            ),
        )

    ahead = 2
    for shift in range(1, min(ahead, n_hi - 1) + 1):
        t = lax.rem(request + shift, n_hi)
        for copy in pushes(t):
            copy.start()
    own_k = pltpu.make_async_copy(kt_hbm.at[request], kslots.at[request], own_sem.at[0])
    own_v = pltpu.make_async_copy(v_hbm.at[request], vslots.at[request], own_sem.at[1])
    own_k.start()
    own_v.start()

    acc_ref[...] = jnp.zeros_like(acc_ref)
    top_ref[...] = jnp.full_like(top_ref, negative_fill)
    den_ref[...] = jnp.zeros_like(den_ref)

    def group(s, with_tree):
        start = (s * n_lo + quarter) * block_len
        kt_ref = kslots.at[s]
        v_ref = vslots.at[s]
        pos = start + lax.broadcasted_iota(jnp.int32, (1, block_len), 1)
        bias = jnp.where(pos < length, 0.0, negative_fill)

        def pair(p, carry):
            col = pl.multiple_of(p * 2 * HD, 2 * HD)
            both = q_ref[:, pl.ds(col, 2 * HD)]
            qh = jnp.concatenate([both[:, :HD], both[:, HD:]], axis=0)
            sc = jnp.dot(qh, kt_ref[...], preferred_element_type=jnp.float32) * scale + bias
            peak = jnp.max(sc, axis=1, keepdims=True)
            if with_tree:
                st = jnp.dot(qh, tkt_ref[...], preferred_element_type=jnp.float32) * scale
                tlive = jnp.concatenate([tmask_ref[...], tmask_ref[...]], axis=0) > 0.5
                st = jnp.where(tlive, st, negative_fill)
                peak = jnp.maximum(peak, jnp.max(st, axis=1, keepdims=True))
            w = jnp.exp(sc - jnp.maximum(peak, 0.1 * negative_fill))
            tot = jnp.sum(w, axis=1, keepdims=True)
            gs = jnp.dot(w.astype(jnp.bfloat16), v_ref[...], preferred_element_type=jnp.float32)
            if with_tree:
                wt = jnp.where(tlive, jnp.exp(st - peak), 0.0)
                tot = tot + jnp.sum(wt, axis=1, keepdims=True)
                gs = gs + jnp.dot(
                    wt.astype(jnp.bfloat16), tv_ref[...], preferred_element_type=jnp.float32
                )
            floored = jnp.maximum(tot, 1.0)
            part = gs / floored
            lt = peak + jnp.log(floored)
            for half in range(2):
                h = 2 * p + half
                hcol = pl.multiple_of(h * HD, HD)
                lt_h = lt[half * rows : (half + 1) * rows]
                part_h = part[half * rows : (half + 1) * rows]
                old = top_ref[h][:, :1]
                new = jnp.maximum(old, lt_h)
                keep = jnp.exp(old - new)
                add = jnp.exp(lt_h - new)
                acc_ref[:, pl.ds(hcol, HD)] = keep * acc_ref[:, pl.ds(hcol, HD)] + add * part_h
                den_ref[h] = jnp.broadcast_to(keep * den_ref[h][:, :1] + add, (rows, HD))
                top_ref[h] = jnp.broadcast_to(new, (rows, HD))
            return carry

        lax.fori_loop(0, heads // 2, pair, 0, unroll=4)

    own_k.wait()
    own_v.wait()
    group(request, True)

    def landed(s):
        source = (s, quarter, head_axis)
        return (
            pltpu.make_async_remote_copy(
                kt_hbm.at[s], kslots.at[s], send_sem.at[s, 0], recv_sem.at[s, 0],
                device_id=source, device_id_type=mesh,
            ),
            pltpu.make_async_remote_copy(
                v_hbm.at[s], vslots.at[s], send_sem.at[s, 1], recv_sem.at[s, 1],
                device_id=source, device_id_type=mesh,
            ),
        )

    def arrival(step, carry):
        @pl.when(step + ahead + 1 < n_hi)
        def _():
            t = lax.rem(request + step + ahead + 1, n_hi)
            for copy in pushes(t):
                copy.start()

        s = lax.rem(request - step - 1 + n_hi, n_hi)
        for copy in landed(s):
            copy.wait_recv()
        group(s, False)
        return carry

    lax.fori_loop(0, n_hi - 1, arrival, 0)
    for shift in range(1, n_hi):
        t = lax.rem(request + shift, n_hi)
        for copy in pushes(t):
            copy.wait_send()

    lane = lax.broadcasted_iota(jnp.int32, (rows, HD), 1)
    tops = jnp.full((rows, HD), negative_fill, jnp.float32)
    dens = jnp.zeros((rows, HD), jnp.float32)
    for h in range(heads):
        tops = jnp.where(lane == h, top_ref[h], tops)
        dens = jnp.where(lane == h, den_ref[h], dens)
    stats[0] = tops
    stats[1] = dens

    quarter_rows = rows // n_quarters

    def quarter_copies(r, slot, device):
        piece = pl.ds(r * quarter_rows, quarter_rows)
        return (
            pltpu.make_async_remote_copy(
                acc_ref.at[piece, :], acc_slots.at[slot], fsend.at[r, 0], frecv.at[slot, 0],
                device_id=device, device_id_type=mesh,
            ),
            pltpu.make_async_remote_copy(
                stats.at[:, piece, :], stat_slots.at[slot], fsend.at[r, 1], frecv.at[slot, 1],
                device_id=device, device_id_type=mesh,
            ),
        )

    for r in range(n_quarters):
        for copy in quarter_copies(r, quarter, (request, r, head_axis)):
            pl.when(r != quarter)(copy.start)
    mine = pl.ds(pl.multiple_of(quarter * quarter_rows, quarter_rows), quarter_rows)
    keep_acc = pltpu.make_async_copy(acc_ref.at[mine, :], acc_slots.at[quarter], fown.at[0])
    keep_stat = pltpu.make_async_copy(stats.at[:, mine, :], stat_slots.at[quarter], fown.at[1])
    keep_acc.start()
    keep_stat.start()
    keep_acc.wait()
    keep_stat.wait()
    for r in range(n_quarters):
        for copy in quarter_copies(r, r, (request, r, head_axis)):
            pl.when(r != quarter)(copy.wait_recv)
    for r in range(n_quarters):
        for copy in quarter_copies(r, quarter, (request, r, head_axis)):
            pl.when(r != quarter)(copy.wait_send)
    acc_out[...] = acc_slots[...]
    stat_out[...] = stat_slots[...]


def attend(info, query_block, keys_t, values, tree_keys_t, tree_values, tree_mask, n_quarters):
    rows, width = query_block.shape
    heads = width // HD
    n_hi = keys_t.shape[0]
    quarter_rows = rows // n_quarters
    vmem = pl.BlockSpec(memory_space=pltpu.VMEM)
    hbm = pl.BlockSpec(memory_space=pl.ANY)
    acc_shape = (n_quarters, quarter_rows, width)
    stat_shape = (n_quarters, 2, quarter_rows, HD)
    return pl.pallas_call(
        functools.partial(
            attend_kernel, scale=1.0 / math.sqrt(HD), n_hi=n_hi, n_quarters=n_quarters
        ),
        out_shape=(
            jax.ShapeDtypeStruct(acc_shape, jnp.float32),
            jax.ShapeDtypeStruct(stat_shape, jnp.float32),
        ),
        in_specs=[pl.BlockSpec(memory_space=pltpu.SMEM), vmem, hbm, hbm, vmem, vmem, vmem],
        out_specs=(vmem, vmem),
        scratch_shapes=[
            pltpu.VMEM(keys_t.shape, keys_t.dtype),
            pltpu.VMEM(values.shape, values.dtype),
            pltpu.SemaphoreType.DMA((n_hi, 2)),
            pltpu.SemaphoreType.DMA((n_hi, 2)),
            pltpu.SemaphoreType.DMA((2,)),
            pltpu.VMEM((rows, width), jnp.float32),
            pltpu.VMEM((heads, rows, HD), jnp.float32),
            pltpu.VMEM((heads, rows, HD), jnp.float32),
            pltpu.VMEM((2, rows, HD), jnp.float32),
            pltpu.VMEM(acc_shape, jnp.float32),
            pltpu.VMEM(stat_shape, jnp.float32),
            pltpu.SemaphoreType.DMA((n_quarters, 2)),
            pltpu.SemaphoreType.DMA((n_quarters, 2)),
            pltpu.SemaphoreType.DMA((2,)),
        ],
        compiler_params=pltpu.CompilerParams(
            collective_id=1, has_side_effects=True, vmem_limit_bytes=48 * 1024 * 1024
        ),
    )(info, query_block, keys_t, values, tree_keys_t, tree_values, tree_mask)


def exchange_kernel(src_ref, out_ref, slots, send_sem, recv_sem, own_sem, *, n_lo, n_head):
    request = lax.axis_index("rh")
    quarter = lax.axis_index("rl")
    head = lax.axis_index("head")
    me = quarter * n_head + head
    peers = n_lo * n_head
    mesh = pl.DeviceIdType.MESH

    barrier = pltpu.get_barrier_semaphore()
    for d in range(peers):
        dest = (request, d // n_head, d % n_head)

        @pl.when(d != me)
        def _():
            pl.semaphore_signal(barrier, inc=1, device_id=dest, device_id_type=mesh)

    pl.semaphore_wait(barrier, peers - 1)

    def push(d):
        return pltpu.make_async_remote_copy(
            src_ref.at[d % n_head],
            slots.at[me],
            send_sem.at[d],
            recv_sem.at[me],
            device_id=(request, d // n_head, d % n_head),
            device_id_type=mesh,
        )

    for d in range(peers):
        pl.when(d != me)(push(d).start)
    own = pltpu.make_async_copy(src_ref.at[head], slots.at[me], own_sem)
    own.start()
    own.wait()
    for d in range(peers):
        pl.when(d != me)(push(d).wait_send)
    for s in range(peers):
        arrival = pltpu.make_async_remote_copy(
            src_ref.at[0],
            slots.at[s],
            send_sem.at[s],
            recv_sem.at[s],
            device_id=(request, s // n_head, s % n_head),
            device_id_type=mesh,
        )
        pl.when(s != me)(arrival.wait_recv)
    out_ref[...] = slots[...]


def exchange_queries(pieces, n_lo, n_head):
    peers = n_lo * n_head
    shape = (peers,) + pieces.shape[1:]
    vmem = pl.BlockSpec(memory_space=pltpu.VMEM)
    return pl.pallas_call(
        functools.partial(exchange_kernel, n_lo=n_lo, n_head=n_head),
        out_shape=jax.ShapeDtypeStruct(shape, pieces.dtype),
        in_specs=[vmem],
        out_specs=vmem,
        scratch_shapes=[
            pltpu.VMEM(shape, pieces.dtype),
            pltpu.SemaphoreType.DMA((peers,)),
            pltpu.SemaphoreType.DMA((peers,)),
            pltpu.SemaphoreType.DMA(()),
        ],
        compiler_params=pltpu.CompilerParams(collective_id=0, has_side_effects=True),
    )(pieces)


def body(
    queries, cache_keys, cache_values, tree_keys, tree_values, parents, tree_sizes, cache_lens
):
    group_size = NH // KVH
    softmax_scale = 1.0 / math.sqrt(HD)
    request = lax.axis_index("rh")
    quarter = lax.axis_index("rl")
    n_lo = lax.axis_size("rl")
    n_hi = lax.axis_size("rh")
    cache_block = cache_keys.shape[1]
    kv_local = cache_keys.shape[2] // HD
    heads_local = kv_local * group_size
    node_count = parents.shape[1]
    rows_owned = tree_keys.shape[0]

    n_head = lax.axis_size("head")
    width = queries.shape[1] // n_head
    pieces = queries.reshape(queries.shape[0], n_head, width // HD, HD).transpose(1, 0, 2, 3)
    pieces = pieces.reshape(n_head, queries.shape[0] * width // HD, HD)
    query_block = exchange_queries(pieces, n_lo, n_head)
    query_block = query_block.reshape(node_count, width)

    reached = ancestry(parents)
    ancestors = lax.dynamic_index_in_dim(reached, request, 0, keepdims=False)
    ancestors = lax.dynamic_slice_in_dim(ancestors, quarter * rows_owned, rows_owned, 1)
    tree_mask = ancestors.astype(jnp.float32)
    length = lax.dynamic_index_in_dim(cache_lens, request, 0, keepdims=False)
    live_size = lax.dynamic_index_in_dim(tree_sizes, request, 0, keepdims=False)
    info = jnp.stack([length, jnp.int32(n_lo)]).astype(jnp.int32)
    keys_t = cache_keys.transpose(0, 2, 1)
    got_acc, got_stats = attend(
        info, query_block, keys_t, cache_values, tree_keys.T, tree_values, tree_mask, n_lo
    )
    got_acc = got_acc.reshape(n_lo, rows_owned, heads_local, HD)
    got_top = got_stats[:, 0, :, :heads_local]
    got_den = got_stats[:, 1, :, :heads_local]
    highest = jnp.max(got_top, axis=0)
    scale = jnp.exp(got_top - highest)
    num = jnp.sum(scale[..., None] * got_acc, axis=0)
    total = jnp.sum(scale * got_den, axis=0)
    merged = (num / total[..., None]).reshape(rows_owned, heads_local * HD)

    row_nodes = quarter * rows_owned + jnp.arange(rows_owned, dtype=jnp.int32)
    live_rows = row_nodes < live_size
    return jnp.where(live_rows[:, None], merged, 0.0).astype(jnp.bfloat16)


def solution(mesh):
    def run(queries, cache_keys, cache_values, tree_keys, tree_values, parents, tree_sizes, cache_lens):
        n_hi = cache_keys.shape[0]
        n_lo = mesh.shape["req"] // n_hi
        split = Mesh(mesh.devices.reshape(n_hi, n_lo, mesh.shape["head"]), ("rh", "rl", "head"))
        rows = ("rh", "rl")
        placed = (
            P(("rh", "rl", "head"), None),
            P(None, rows, "head"),
            P(None, rows, "head"),
            P(rows, "head"),
            P(rows, "head"),
            P(),
            P(),
            P(),
        )
        return jax.shard_map(
            body, mesh=split, in_specs=placed, out_specs=P(rows, "head"), check_vma=False
        )(queries, cache_keys, cache_values, tree_keys, tree_values, parents, tree_sizes, cache_lens)

    return run
```

```python
import functools
import math

import jax
import jax.numpy as jnp
from jax import lax
from jax.experimental import pallas as pl
from jax.experimental.pallas import tpu as pltpu
from jax.sharding import Mesh
from jax.sharding import PartitionSpec as P

NH = 128
KVH = 8
HD = 128


negative_fill = -1e30


def ancestry(parents):
    node_count = parents.shape[1]
    node_ids = jnp.arange(node_count, dtype=jnp.int32)
    linked = jnp.logical_or(
        parents[:, :, None] == node_ids[None, None, :], node_ids[:, None] == node_ids[None, :]
    )
    reached = linked.astype(jnp.bfloat16)
    for doubling in range((node_count - 1).bit_length()):
        squared = jnp.einsum("aij,ajk->aik", reached, reached, preferred_element_type=jnp.float32)
        reached = jnp.minimum(squared, 1.0).astype(jnp.bfloat16)
    return reached


def attend_kernel(
    info_ref, q_ref, kt_hbm, v_hbm, tkt_ref, tv_ref, tmask_ref, acc_out, stat_out,
    kslots, vslots, send_sem, recv_sem, own_sem, acc_ref, top_ref, den_ref, stats,
    acc_slots, stat_slots, fsend, frecv, fown, *, scale, n_hi, n_quarters,
):
    request = lax.axis_index("rh")
    quarter = lax.axis_index("rl")
    head_axis = lax.axis_index("head")
    mesh = pl.DeviceIdType.MESH
    length = info_ref[0]
    n_lo = info_ref[1]
    rows = q_ref.shape[0]
    heads = q_ref.shape[1] // HD
    block_len = kt_hbm.shape[2]

    barrier = pltpu.get_barrier_semaphore()
    for t in range(n_hi):

        @pl.when(t != request)
        def _():
            pl.semaphore_signal(
                barrier, inc=1, device_id=(t, quarter, head_axis), device_id_type=mesh
            )

    for r in range(n_quarters):

        @pl.when(r != quarter)
        def _():
            pl.semaphore_signal(
                barrier, inc=1, device_id=(request, r, head_axis), device_id_type=mesh
            )

    pl.semaphore_wait(barrier, n_hi - 1 + n_quarters - 1)

    def pushes(t):
        dest = (t, quarter, head_axis)
        return (
            pltpu.make_async_remote_copy(
                kt_hbm.at[t], kslots.at[request], send_sem.at[t, 0], recv_sem.at[request, 0],
                device_id=dest, device_id_type=mesh,
            ),
            pltpu.make_async_remote_copy(
                v_hbm.at[t], vslots.at[request], send_sem.at[t, 1], recv_sem.at[request, 1],
                device_id=dest, device_id_type=mesh,
            ),
        )

    ahead = 2
    for shift in range(1, min(ahead, n_hi - 1) + 1):
        t = lax.rem(request + shift, n_hi)
        for copy in pushes(t):
            copy.start()
    own_k = pltpu.make_async_copy(kt_hbm.at[request], kslots.at[request], own_sem.at[0])
    own_v = pltpu.make_async_copy(v_hbm.at[request], vslots.at[request], own_sem.at[1])
    own_k.start()
    own_v.start()

    acc_ref[...] = jnp.zeros_like(acc_ref)
    top_ref[...] = jnp.full_like(top_ref, negative_fill)
    den_ref[...] = jnp.zeros_like(den_ref)

    def group(s, with_tree):
        start = (s * n_lo + quarter) * block_len
        kt_ref = kslots.at[s]
        v_ref = vslots.at[s]
        pos = start + lax.broadcasted_iota(jnp.int32, (1, block_len), 1)
        bias = jnp.where(pos < length, 0.0, negative_fill)

        def pair(p, carry):
            col = pl.multiple_of(p * 2 * HD, 2 * HD)
            both = q_ref[:, pl.ds(col, 2 * HD)]
            qh = jnp.concatenate([both[:, :HD], both[:, HD:]], axis=0)
            sc = jnp.dot(qh, kt_ref[...], preferred_element_type=jnp.float32) * scale + bias
            peak = jnp.max(sc, axis=1, keepdims=True)
            if with_tree:
                st = jnp.dot(qh, tkt_ref[...], preferred_element_type=jnp.float32) * scale
                tlive = jnp.concatenate([tmask_ref[...], tmask_ref[...]], axis=0) > 0.5
                st = jnp.where(tlive, st, negative_fill)
                peak = jnp.maximum(peak, jnp.max(st, axis=1, keepdims=True))
            w = jnp.exp(sc - jnp.maximum(peak, 0.1 * negative_fill))
            tot = jnp.sum(w, axis=1, keepdims=True)
            gs = jnp.dot(w.astype(jnp.bfloat16), v_ref[...], preferred_element_type=jnp.float32)
            if with_tree:
                wt = jnp.where(tlive, jnp.exp(st - peak), 0.0)
                tot = tot + jnp.sum(wt, axis=1, keepdims=True)
                gs = gs + jnp.dot(
                    wt.astype(jnp.bfloat16), tv_ref[...], preferred_element_type=jnp.float32
                )
            floored = jnp.maximum(tot, 1.0)
            part = gs / floored
            lt = peak + jnp.log(floored)
            for half in range(2):
                h = 2 * p + half
                hcol = pl.multiple_of(h * HD, HD)
                lt_h = lt[half * rows : (half + 1) * rows]
                part_h = part[half * rows : (half + 1) * rows]
                old = top_ref[h][:, :1]
                new = jnp.maximum(old, lt_h)
                keep = jnp.exp(old - new)
                add = jnp.exp(lt_h - new)
                acc_ref[:, pl.ds(hcol, HD)] = keep * acc_ref[:, pl.ds(hcol, HD)] + add * part_h
                den_ref[h] = jnp.broadcast_to(keep * den_ref[h][:, :1] + add, (rows, HD))
                top_ref[h] = jnp.broadcast_to(new, (rows, HD))
            return carry

        lax.fori_loop(0, heads // 2, pair, 0, unroll=4)

    own_k.wait()
    own_v.wait()
    group(request, True)

    def landed(s):
        source = (s, quarter, head_axis)
        return (
            pltpu.make_async_remote_copy(
                kt_hbm.at[s], kslots.at[s], send_sem.at[s, 0], recv_sem.at[s, 0],
                device_id=source, device_id_type=mesh,
            ),
            pltpu.make_async_remote_copy(
                v_hbm.at[s], vslots.at[s], send_sem.at[s, 1], recv_sem.at[s, 1],
                device_id=source, device_id_type=mesh,
            ),
        )

    def arrival(step, carry):
        @pl.when(step + ahead + 1 < n_hi)
        def _():
            t = lax.rem(request + step + ahead + 1, n_hi)
            for copy in pushes(t):
                copy.start()

        s = lax.rem(request - step - 1 + n_hi, n_hi)
        for copy in landed(s):
            copy.wait_recv()
        group(s, False)
        return carry

    lax.fori_loop(0, n_hi - 1, arrival, 0)
    for shift in range(1, n_hi):
        t = lax.rem(request + shift, n_hi)
        for copy in pushes(t):
            copy.wait_send()

    lane = lax.broadcasted_iota(jnp.int32, (rows, HD), 1)
    tops = jnp.full((rows, HD), negative_fill, jnp.float32)
    dens = jnp.zeros((rows, HD), jnp.float32)
    for h in range(heads):
        tops = jnp.where(lane == h, top_ref[h], tops)
        dens = jnp.where(lane == h, den_ref[h], dens)
    stats[0] = tops
    stats[1] = dens

    quarter_rows = rows // n_quarters

    def quarter_copies(r, slot, device):
        piece = pl.ds(r * quarter_rows, quarter_rows)
        return (
            pltpu.make_async_remote_copy(
                acc_ref.at[piece, :], acc_slots.at[slot], fsend.at[r, 0], frecv.at[slot, 0],
                device_id=device, device_id_type=mesh,
            ),
            pltpu.make_async_remote_copy(
                stats.at[:, piece, :], stat_slots.at[slot], fsend.at[r, 1], frecv.at[slot, 1],
                device_id=device, device_id_type=mesh,
            ),
        )

    for r in range(n_quarters):
        for copy in quarter_copies(r, quarter, (request, r, head_axis)):
            pl.when(r != quarter)(copy.start)
    mine = pl.ds(pl.multiple_of(quarter * quarter_rows, quarter_rows), quarter_rows)
    keep_acc = pltpu.make_async_copy(acc_ref.at[mine, :], acc_slots.at[quarter], fown.at[0])
    keep_stat = pltpu.make_async_copy(stats.at[:, mine, :], stat_slots.at[quarter], fown.at[1])
    keep_acc.start()
    keep_stat.start()
    keep_acc.wait()
    keep_stat.wait()
    for r in range(n_quarters):
        for copy in quarter_copies(r, r, (request, r, head_axis)):
            pl.when(r != quarter)(copy.wait_recv)
    for r in range(n_quarters):
        for copy in quarter_copies(r, quarter, (request, r, head_axis)):
            pl.when(r != quarter)(copy.wait_send)
    acc_out[...] = acc_slots[...]
    stat_out[...] = stat_slots[...]


def attend(info, query_block, keys_t, values, tree_keys_t, tree_values, tree_mask, n_quarters):
    rows, width = query_block.shape
    heads = width // HD
    n_hi = keys_t.shape[0]
    quarter_rows = rows // n_quarters
    vmem = pl.BlockSpec(memory_space=pltpu.VMEM)
    hbm = pl.BlockSpec(memory_space=pl.ANY)
    acc_shape = (n_quarters, quarter_rows, width)
    stat_shape = (n_quarters, 2, quarter_rows, HD)
    return pl.pallas_call(
        functools.partial(
            attend_kernel, scale=1.0 / math.sqrt(HD), n_hi=n_hi, n_quarters=n_quarters
        ),
        out_shape=(
            jax.ShapeDtypeStruct(acc_shape, jnp.float32),
            jax.ShapeDtypeStruct(stat_shape, jnp.float32),
        ),
        in_specs=[pl.BlockSpec(memory_space=pltpu.SMEM), vmem, hbm, hbm, vmem, vmem, vmem],
        out_specs=(vmem, vmem),
        scratch_shapes=[
            pltpu.VMEM(keys_t.shape, keys_t.dtype),
            pltpu.VMEM(values.shape, values.dtype),
            pltpu.SemaphoreType.DMA((n_hi, 2)),
            pltpu.SemaphoreType.DMA((n_hi, 2)),
            pltpu.SemaphoreType.DMA((2,)),
            pltpu.VMEM((rows, width), jnp.float32),
            pltpu.VMEM((heads, rows, HD), jnp.float32),
            pltpu.VMEM((heads, rows, HD), jnp.float32),
            pltpu.VMEM((2, rows, HD), jnp.float32),
            pltpu.VMEM(acc_shape, jnp.float32),
            pltpu.VMEM(stat_shape, jnp.float32),
            pltpu.SemaphoreType.DMA((n_quarters, 2)),
            pltpu.SemaphoreType.DMA((n_quarters, 2)),
            pltpu.SemaphoreType.DMA((2,)),
        ],
        compiler_params=pltpu.CompilerParams(
            collective_id=1, has_side_effects=True, vmem_limit_bytes=48 * 1024 * 1024
        ),
    )(info, query_block, keys_t, values, tree_keys_t, tree_values, tree_mask)


def exchange_kernel(src_ref, out_ref, slots, send_sem, recv_sem, own_sem, *, n_lo, n_head):
    request = lax.axis_index("rh")
    quarter = lax.axis_index("rl")
    head = lax.axis_index("head")
    me = quarter * n_head + head
    peers = n_lo * n_head
    mesh = pl.DeviceIdType.MESH

    barrier = pltpu.get_barrier_semaphore()
    for d in range(peers):
        dest = (request, d // n_head, d % n_head)

        @pl.when(d != me)
        def _():
            pl.semaphore_signal(barrier, inc=1, device_id=dest, device_id_type=mesh)

    pl.semaphore_wait(barrier, peers - 1)

    def push(d):
        return pltpu.make_async_remote_copy(
            src_ref.at[d % n_head],
            slots.at[me],
            send_sem.at[d],
            recv_sem.at[me],
            device_id=(request, d // n_head, d % n_head),
            device_id_type=mesh,
        )

    for d in range(peers):
        pl.when(d != me)(push(d).start)
    own = pltpu.make_async_copy(src_ref.at[head], slots.at[me], own_sem)
    own.start()
    own.wait()
    for d in range(peers):
        pl.when(d != me)(push(d).wait_send)
    for s in range(peers):
        arrival = pltpu.make_async_remote_copy(
            src_ref.at[0],
            slots.at[s],
            send_sem.at[s],
            recv_sem.at[s],
            device_id=(request, s // n_head, s % n_head),
            device_id_type=mesh,
        )
        pl.when(s != me)(arrival.wait_recv)
    out_ref[...] = slots[...]


def exchange_queries(pieces, n_lo, n_head):
    peers = n_lo * n_head
    shape = (peers,) + pieces.shape[1:]
    vmem = pl.BlockSpec(memory_space=pltpu.VMEM)
    return pl.pallas_call(
        functools.partial(exchange_kernel, n_lo=n_lo, n_head=n_head),
        out_shape=jax.ShapeDtypeStruct(shape, pieces.dtype),
        in_specs=[vmem],
        out_specs=vmem,
        scratch_shapes=[
            pltpu.VMEM(shape, pieces.dtype),
            pltpu.SemaphoreType.DMA((peers,)),
            pltpu.SemaphoreType.DMA((peers,)),
            pltpu.SemaphoreType.DMA(()),
        ],
        compiler_params=pltpu.CompilerParams(collective_id=0, has_side_effects=True),
    )(pieces)


def body(
    queries, cache_keys, cache_values, tree_keys, tree_values, parents, tree_sizes, cache_lens
):
    group_size = NH // KVH
    softmax_scale = 1.0 / math.sqrt(HD)
    request = lax.axis_index("rh")
    quarter = lax.axis_index("rl")
    n_lo = lax.axis_size("rl")
    n_hi = lax.axis_size("rh")
    cache_block = cache_keys.shape[1]
    kv_local = cache_keys.shape[2] // HD
    heads_local = kv_local * group_size
    node_count = parents.shape[1]
    rows_owned = tree_keys.shape[0]

    n_head = lax.axis_size("head")
    width = queries.shape[1] // n_head
    pieces = queries.reshape(queries.shape[0], n_head, width // HD, HD).transpose(1, 0, 2, 3)
    pieces = pieces.reshape(n_head, queries.shape[0] * width // HD, HD)
    query_block = exchange_queries(pieces, n_lo, n_head)
    query_block = query_block.reshape(node_count, width)

    own_parents = lax.dynamic_slice_in_dim(parents, request, 1, 0)
    ancestors = ancestry(own_parents)[0]
    ancestors = lax.dynamic_slice_in_dim(ancestors, quarter * rows_owned, rows_owned, 1)
    tree_mask = ancestors.astype(jnp.float32)
    length = lax.dynamic_index_in_dim(cache_lens, request, 0, keepdims=False)
    live_size = lax.dynamic_index_in_dim(tree_sizes, request, 0, keepdims=False)
    info = jnp.stack([length, jnp.int32(n_lo)]).astype(jnp.int32)
    keys_t = cache_keys.transpose(0, 2, 1)
    got_acc, got_stats = attend(
        info, query_block, keys_t, cache_values, tree_keys.T, tree_values, tree_mask, n_lo
    )
    got_acc = got_acc.reshape(n_lo, rows_owned, heads_local, HD)
    got_top = got_stats[:, 0, :, :heads_local]
    got_den = got_stats[:, 1, :, :heads_local]
    highest = jnp.max(got_top, axis=0)
    scale = jnp.exp(got_top - highest)
    num = jnp.sum(scale[..., None] * got_acc, axis=0)
    total = jnp.sum(scale * got_den, axis=0)
    merged = (num / total[..., None]).reshape(rows_owned, heads_local * HD)

    row_nodes = quarter * rows_owned + jnp.arange(rows_owned, dtype=jnp.int32)
    live_rows = row_nodes < live_size
    return jnp.where(live_rows[:, None], merged, 0.0).astype(jnp.bfloat16)


def solution(mesh):
    def run(queries, cache_keys, cache_values, tree_keys, tree_values, parents, tree_sizes, cache_lens):
        n_hi = cache_keys.shape[0]
        n_lo = mesh.shape["req"] // n_hi
        split = Mesh(mesh.devices.reshape(n_hi, n_lo, mesh.shape["head"]), ("rh", "rl", "head"))
        rows = ("rh", "rl")
        placed = (
            P(("rh", "rl", "head"), None),
            P(None, rows, "head"),
            P(None, rows, "head"),
            P(rows, "head"),
            P(rows, "head"),
            P(),
            P(),
            P(),
        )
        return jax.shard_map(
            body, mesh=split, in_specs=placed, out_specs=P(rows, "head"), check_vma=False
        )(queries, cache_keys, cache_values, tree_keys, tree_values, parents, tree_sizes, cache_lens)

    return run
```

```python
import functools
import math

import jax
import jax.numpy as jnp
from jax import lax
from jax.experimental import pallas as pl
from jax.experimental.pallas import tpu as pltpu
from jax.sharding import Mesh
from jax.sharding import PartitionSpec as P

NH = 128
KVH = 8
HD = 128


negative_fill = -1e30


def ancestry(parents):
    node_count = parents.shape[1]
    node_ids = jnp.arange(node_count, dtype=jnp.int32)
    linked = jnp.logical_or(
        parents[:, :, None] == node_ids[None, None, :], node_ids[:, None] == node_ids[None, :]
    )
    reached = linked.astype(jnp.bfloat16)
    for doubling in range((node_count - 1).bit_length()):
        squared = jnp.einsum("aij,ajk->aik", reached, reached, preferred_element_type=jnp.float32)
        reached = jnp.minimum(squared, 1.0).astype(jnp.bfloat16)
    return reached


def attend_kernel(
    info_ref, q_ref, kt_hbm, v_hbm, tkt_ref, tv_ref, tmask_ref, acc_out, stat_out,
    kslots, vslots, send_sem, recv_sem, own_sem, acc_ref, top_ref, den_ref, stats,
    acc_slots, stat_slots, fsend, frecv, fown, *, scale, n_hi, n_quarters,
):
    request = lax.axis_index("rh")
    quarter = lax.axis_index("rl")
    head_axis = lax.axis_index("head")
    mesh = pl.DeviceIdType.MESH
    length = info_ref[0]
    n_lo = info_ref[1]
    rows = q_ref.shape[0]
    heads = q_ref.shape[1] // HD
    block_len = kt_hbm.shape[2]

    barrier = pltpu.get_barrier_semaphore()
    for t in range(n_hi):

        @pl.when(t != request)
        def _():
            pl.semaphore_signal(
                barrier, inc=1, device_id=(t, quarter, head_axis), device_id_type=mesh
            )

    for r in range(n_quarters):

        @pl.when(r != quarter)
        def _():
            pl.semaphore_signal(
                barrier, inc=1, device_id=(request, r, head_axis), device_id_type=mesh
            )

    pl.semaphore_wait(barrier, n_hi - 1 + n_quarters - 1)

    def pushes(t):
        dest = (t, quarter, head_axis)
        return (
            pltpu.make_async_remote_copy(
                kt_hbm.at[t], kslots.at[request], send_sem.at[t, 0], recv_sem.at[request, 0],
                device_id=dest, device_id_type=mesh,
            ),
            pltpu.make_async_remote_copy(
                v_hbm.at[t], vslots.at[request], send_sem.at[t, 1], recv_sem.at[request, 1],
                device_id=dest, device_id_type=mesh,
            ),
        )

    ahead = 2
    for shift in range(1, min(ahead, n_hi - 1) + 1):
        t = lax.rem(request + shift, n_hi)
        for copy in pushes(t):
            copy.start()
    own_k = pltpu.make_async_copy(kt_hbm.at[request], kslots.at[request], own_sem.at[0])
    own_v = pltpu.make_async_copy(v_hbm.at[request], vslots.at[request], own_sem.at[1])
    own_k.start()
    own_v.start()

    acc_ref[...] = jnp.zeros_like(acc_ref)
    top_ref[...] = jnp.full_like(top_ref, negative_fill)
    den_ref[...] = jnp.zeros_like(den_ref)

    def group(s, with_tree):
        start = (s * n_lo + quarter) * block_len
        kt_ref = kslots.at[s]
        v_ref = vslots.at[s]
        pos = start + lax.broadcasted_iota(jnp.int32, (1, block_len), 1)
        bias = jnp.where(pos < length, 0.0, negative_fill)

        def pair(p, carry):
            col = pl.multiple_of(p * 2 * HD, 2 * HD)
            both = q_ref[:, pl.ds(col, 2 * HD)]
            qh = jnp.concatenate([both[:, :HD], both[:, HD:]], axis=0)
            sc = jnp.dot(qh, kt_ref[...], preferred_element_type=jnp.float32) * scale + bias
            peak = jnp.max(sc, axis=1, keepdims=True)
            if with_tree:
                st = jnp.dot(qh, tkt_ref[...], preferred_element_type=jnp.float32) * scale
                tlive = jnp.concatenate([tmask_ref[...], tmask_ref[...]], axis=0) > 0.5
                st = jnp.where(tlive, st, negative_fill)
                peak = jnp.maximum(peak, jnp.max(st, axis=1, keepdims=True))
            w = jnp.exp(sc - jnp.maximum(peak, 0.1 * negative_fill))
            tot = jnp.sum(w, axis=1, keepdims=True)
            gs = jnp.dot(w.astype(jnp.bfloat16), v_ref[...], preferred_element_type=jnp.float32)
            if with_tree:
                wt = jnp.where(tlive, jnp.exp(st - peak), 0.0)
                tot = tot + jnp.sum(wt, axis=1, keepdims=True)
                gs = gs + jnp.dot(
                    wt.astype(jnp.bfloat16), tv_ref[...], preferred_element_type=jnp.float32
                )
            floored = jnp.maximum(tot, 1.0)
            part = gs / floored
            lt = peak + jnp.log(floored)
            for half in range(2):
                h = 2 * p + half
                hcol = pl.multiple_of(h * HD, HD)
                lt_h = lt[half * rows : (half + 1) * rows]
                part_h = part[half * rows : (half + 1) * rows]
                old = top_ref[h][:, :1]
                new = jnp.maximum(old, lt_h)
                keep = jnp.exp(old - new)
                add = jnp.exp(lt_h - new)
                acc_ref[:, pl.ds(hcol, HD)] = keep * acc_ref[:, pl.ds(hcol, HD)] + add * part_h
                den_ref[h] = jnp.broadcast_to(keep * den_ref[h][:, :1] + add, (rows, HD))
                top_ref[h] = jnp.broadcast_to(new, (rows, HD))
            return carry

        lax.fori_loop(0, heads // 2, pair, 0, unroll=4)

    own_k.wait()
    own_v.wait()
    group(request, True)

    def landed(s):
        source = (s, quarter, head_axis)
        return (
            pltpu.make_async_remote_copy(
                kt_hbm.at[s], kslots.at[s], send_sem.at[s, 0], recv_sem.at[s, 0],
                device_id=source, device_id_type=mesh,
            ),
            pltpu.make_async_remote_copy(
                v_hbm.at[s], vslots.at[s], send_sem.at[s, 1], recv_sem.at[s, 1],
                device_id=source, device_id_type=mesh,
            ),
        )

    def arrival(step, carry):
        @pl.when(step + ahead + 1 < n_hi)
        def _():
            t = lax.rem(request + step + ahead + 1, n_hi)
            for copy in pushes(t):
                copy.start()

        s = lax.rem(request - step - 1 + n_hi, n_hi)
        for copy in landed(s):
            copy.wait_recv()
        group(s, False)
        return carry

    lax.fori_loop(0, n_hi - 1, arrival, 0)
    for shift in range(1, n_hi):
        t = lax.rem(request + shift, n_hi)
        for copy in pushes(t):
            copy.wait_send()

    lane = lax.broadcasted_iota(jnp.int32, (rows, HD), 1)
    tops = jnp.full((rows, HD), negative_fill, jnp.float32)
    dens = jnp.zeros((rows, HD), jnp.float32)
    for h in range(heads):
        tops = jnp.where(lane == h, top_ref[h], tops)
        dens = jnp.where(lane == h, den_ref[h], dens)
    stats[0] = tops
    stats[1] = dens

    quarter_rows = rows // n_quarters

    def quarter_copies(r, slot, device):
        piece = pl.ds(r * quarter_rows, quarter_rows)
        return (
            pltpu.make_async_remote_copy(
                acc_ref.at[piece, :], acc_slots.at[slot], fsend.at[r, 0], frecv.at[slot, 0],
                device_id=device, device_id_type=mesh,
            ),
            pltpu.make_async_remote_copy(
                stats.at[:, piece, :], stat_slots.at[slot], fsend.at[r, 1], frecv.at[slot, 1],
                device_id=device, device_id_type=mesh,
            ),
        )

    for r in range(n_quarters):
        for copy in quarter_copies(r, quarter, (request, r, head_axis)):
            pl.when(r != quarter)(copy.start)
    mine = pl.ds(pl.multiple_of(quarter * quarter_rows, quarter_rows), quarter_rows)
    keep_acc = pltpu.make_async_copy(acc_ref.at[mine, :], acc_slots.at[quarter], fown.at[0])
    keep_stat = pltpu.make_async_copy(stats.at[:, mine, :], stat_slots.at[quarter], fown.at[1])
    keep_acc.start()
    keep_stat.start()
    keep_acc.wait()
    keep_stat.wait()
    for r in range(n_quarters):
        for copy in quarter_copies(r, r, (request, r, head_axis)):
            pl.when(r != quarter)(copy.wait_recv)
    for r in range(n_quarters):
        for copy in quarter_copies(r, quarter, (request, r, head_axis)):
            pl.when(r != quarter)(copy.wait_send)
    acc_out[...] = acc_slots[...]
    stat_out[...] = stat_slots[...]


def attend(info, query_block, keys_t, values, tree_keys_t, tree_values, tree_mask, n_quarters):
    rows, width = query_block.shape
    heads = width // HD
    n_hi = keys_t.shape[0]
    quarter_rows = rows // n_quarters
    vmem = pl.BlockSpec(memory_space=pltpu.VMEM)
    hbm = pl.BlockSpec(memory_space=pl.ANY)
    acc_shape = (n_quarters, quarter_rows, width)
    stat_shape = (n_quarters, 2, quarter_rows, HD)
    return pl.pallas_call(
        functools.partial(
            attend_kernel, scale=1.0 / math.sqrt(HD), n_hi=n_hi, n_quarters=n_quarters
        ),
        out_shape=(
            jax.ShapeDtypeStruct(acc_shape, jnp.float32),
            jax.ShapeDtypeStruct(stat_shape, jnp.float32),
        ),
        in_specs=[pl.BlockSpec(memory_space=pltpu.SMEM), vmem, hbm, hbm, vmem, vmem, vmem],
        out_specs=(vmem, vmem),
        scratch_shapes=[
            pltpu.VMEM(keys_t.shape, keys_t.dtype),
            pltpu.VMEM(values.shape, values.dtype),
            pltpu.SemaphoreType.DMA((n_hi, 2)),
            pltpu.SemaphoreType.DMA((n_hi, 2)),
            pltpu.SemaphoreType.DMA((2,)),
            pltpu.VMEM((rows, width), jnp.float32),
            pltpu.VMEM((heads, rows, HD), jnp.float32),
            pltpu.VMEM((heads, rows, HD), jnp.float32),
            pltpu.VMEM((2, rows, HD), jnp.float32),
            pltpu.VMEM(acc_shape, jnp.float32),
            pltpu.VMEM(stat_shape, jnp.float32),
            pltpu.SemaphoreType.DMA((n_quarters, 2)),
            pltpu.SemaphoreType.DMA((n_quarters, 2)),
            pltpu.SemaphoreType.DMA((2,)),
        ],
        compiler_params=pltpu.CompilerParams(
            collective_id=1, has_side_effects=True, vmem_limit_bytes=48 * 1024 * 1024
        ),
    )(info, query_block, keys_t, values, tree_keys_t, tree_values, tree_mask)


def exchange_kernel(src_ref, out_ref, slots, send_sem, recv_sem, own_sem, *, n_lo, n_head):
    request = lax.axis_index("rh")
    quarter = lax.axis_index("rl")
    head = lax.axis_index("head")
    me = quarter * n_head + head
    peers = n_lo * n_head
    mesh = pl.DeviceIdType.MESH

    barrier = pltpu.get_barrier_semaphore()
    for d in range(peers):
        dest = (request, d // n_head, d % n_head)

        @pl.when(d != me)
        def _():
            pl.semaphore_signal(barrier, inc=1, device_id=dest, device_id_type=mesh)

    pl.semaphore_wait(barrier, peers - 1)

    def push(d):
        return pltpu.make_async_remote_copy(
            src_ref.at[d % n_head],
            slots.at[me],
            send_sem.at[d],
            recv_sem.at[me],
            device_id=(request, d // n_head, d % n_head),
            device_id_type=mesh,
        )

    for d in range(peers):
        pl.when(d != me)(push(d).start)
    own = pltpu.make_async_copy(src_ref.at[head], slots.at[me], own_sem)
    own.start()
    own.wait()
    for d in range(peers):
        pl.when(d != me)(push(d).wait_send)
    for s in range(peers):
        arrival = pltpu.make_async_remote_copy(
            src_ref.at[0],
            slots.at[s],
            send_sem.at[s],
            recv_sem.at[s],
            device_id=(request, s // n_head, s % n_head),
            device_id_type=mesh,
        )
        pl.when(s != me)(arrival.wait_recv)
    out_ref[...] = slots[...]


def exchange_queries(pieces, n_lo, n_head):
    peers = n_lo * n_head
    shape = (peers,) + pieces.shape[1:]
    vmem = pl.BlockSpec(memory_space=pltpu.VMEM)
    return pl.pallas_call(
        functools.partial(exchange_kernel, n_lo=n_lo, n_head=n_head),
        out_shape=jax.ShapeDtypeStruct(shape, pieces.dtype),
        in_specs=[vmem],
        out_specs=vmem,
        scratch_shapes=[
            pltpu.VMEM(shape, pieces.dtype),
            pltpu.SemaphoreType.DMA((peers,)),
            pltpu.SemaphoreType.DMA((peers,)),
            pltpu.SemaphoreType.DMA(()),
        ],
        compiler_params=pltpu.CompilerParams(collective_id=0, has_side_effects=True),
    )(pieces)


def body(
    queries, cache_keys, cache_values, tree_keys, tree_values, parents, tree_sizes, cache_lens
):
    group_size = NH // KVH
    softmax_scale = 1.0 / math.sqrt(HD)
    request = lax.axis_index("rh")
    quarter = lax.axis_index("rl")
    n_lo = lax.axis_size("rl")
    n_hi = lax.axis_size("rh")
    cache_block = cache_keys.shape[1]
    kv_local = cache_keys.shape[2] // HD
    heads_local = kv_local * group_size
    node_count = parents.shape[1]
    rows_owned = tree_keys.shape[0]

    n_head = lax.axis_size("head")
    width = queries.shape[1] // n_head
    pieces = queries.reshape(queries.shape[0], n_head, width // HD, HD).transpose(1, 0, 2, 3)
    pieces = pieces.reshape(n_head, queries.shape[0] * width // HD, HD)
    keys_t = cache_keys.transpose(0, 2, 1)
    pieces, keys_t = lax.optimization_barrier((pieces, keys_t))
    query_block = exchange_queries(pieces, n_lo, n_head)
    query_block = query_block.reshape(node_count, width)

    own_parents = lax.dynamic_slice_in_dim(parents, request, 1, 0)
    ancestors = ancestry(own_parents)[0]
    ancestors = lax.dynamic_slice_in_dim(ancestors, quarter * rows_owned, rows_owned, 1)
    tree_mask = ancestors.astype(jnp.float32)
    length = lax.dynamic_index_in_dim(cache_lens, request, 0, keepdims=False)
    live_size = lax.dynamic_index_in_dim(tree_sizes, request, 0, keepdims=False)
    info = jnp.stack([length, jnp.int32(n_lo)]).astype(jnp.int32)
    got_acc, got_stats = attend(
        info, query_block, keys_t, cache_values, tree_keys.T, tree_values, tree_mask, n_lo
    )
    got_acc = got_acc.reshape(n_lo, rows_owned, heads_local, HD)
    got_top = got_stats[:, 0, :, :heads_local]
    got_den = got_stats[:, 1, :, :heads_local]
    highest = jnp.max(got_top, axis=0)
    scale = jnp.exp(got_top - highest)
    num = jnp.sum(scale[..., None] * got_acc, axis=0)
    total = jnp.sum(scale * got_den, axis=0)
    merged = (num / total[..., None]).reshape(rows_owned, heads_local * HD)

    row_nodes = quarter * rows_owned + jnp.arange(rows_owned, dtype=jnp.int32)
    live_rows = row_nodes < live_size
    return jnp.where(live_rows[:, None], merged, 0.0).astype(jnp.bfloat16)


def solution(mesh):
    def run(queries, cache_keys, cache_values, tree_keys, tree_values, parents, tree_sizes, cache_lens):
        n_hi = cache_keys.shape[0]
        n_lo = mesh.shape["req"] // n_hi
        split = Mesh(mesh.devices.reshape(n_hi, n_lo, mesh.shape["head"]), ("rh", "rl", "head"))
        rows = ("rh", "rl")
        placed = (
            P(("rh", "rl", "head"), None),
            P(None, rows, "head"),
            P(None, rows, "head"),
            P(rows, "head"),
            P(rows, "head"),
            P(),
            P(),
            P(),
        )
        return jax.shard_map(
            body, mesh=split, in_specs=placed, out_specs=P(rows, "head"), check_vma=False
        )(queries, cache_keys, cache_values, tree_keys, tree_values, parents, tree_sizes, cache_lens)

    return run
```

```python
import functools
import math

import jax
import jax.numpy as jnp
from jax import lax
from jax.experimental import pallas as pl
from jax.experimental.pallas import tpu as pltpu
from jax.sharding import Mesh
from jax.sharding import PartitionSpec as P

NH = 128
KVH = 8
HD = 128


negative_fill = -1e30


def ancestry(parents):
    node_count = parents.shape[1]
    node_ids = jnp.arange(node_count, dtype=jnp.int32)
    linked = jnp.logical_or(
        parents[:, :, None] == node_ids[None, None, :], node_ids[:, None] == node_ids[None, :]
    )
    reached = linked.astype(jnp.bfloat16)
    for doubling in range((node_count - 1).bit_length()):
        squared = jnp.einsum("aij,ajk->aik", reached, reached, preferred_element_type=jnp.float32)
        reached = jnp.minimum(squared, 1.0).astype(jnp.bfloat16)
    return reached


def attend_kernel(
    info_ref, q_ref, kt_hbm, v_hbm, tkt_ref, tv_ref, tmask_ref, acc_out, stat_out,
    kslots, vslots, send_sem, recv_sem, own_sem, acc_ref, top_ref, den_ref, stats,
    acc_slots, stat_slots, fsend, frecv, fown, *, scale, n_hi, n_quarters,
):
    request = lax.axis_index("rh")
    quarter = lax.axis_index("rl")
    head_axis = lax.axis_index("head")
    mesh = pl.DeviceIdType.MESH
    length = info_ref[0]
    n_lo = info_ref[1]
    rows = q_ref.shape[0]
    heads = q_ref.shape[1] // HD
    block_len = kt_hbm.shape[2]

    barrier = pltpu.get_barrier_semaphore()
    for t in range(n_hi):

        @pl.when(t != request)
        def _():
            pl.semaphore_signal(
                barrier, inc=1, device_id=(t, quarter, head_axis), device_id_type=mesh
            )

    for r in range(n_quarters):

        @pl.when(r != quarter)
        def _():
            pl.semaphore_signal(
                barrier, inc=1, device_id=(request, r, head_axis), device_id_type=mesh
            )

    pl.semaphore_wait(barrier, n_hi - 1 + n_quarters - 1)

    def pushes(t):
        dest = (t, quarter, head_axis)
        return (
            pltpu.make_async_remote_copy(
                kt_hbm.at[t], kslots.at[request], send_sem.at[t, 0], recv_sem.at[request, 0],
                device_id=dest, device_id_type=mesh,
            ),
            pltpu.make_async_remote_copy(
                v_hbm.at[t], vslots.at[request], send_sem.at[t, 1], recv_sem.at[request, 1],
                device_id=dest, device_id_type=mesh,
            ),
        )

    ahead = 3
    for shift in range(1, min(ahead, n_hi - 1) + 1):
        t = lax.rem(request + shift, n_hi)
        for copy in pushes(t):
            copy.start()
    own_k = pltpu.make_async_copy(kt_hbm.at[request], kslots.at[request], own_sem.at[0])
    own_v = pltpu.make_async_copy(v_hbm.at[request], vslots.at[request], own_sem.at[1])
    own_k.start()
    own_v.start()

    acc_ref[...] = jnp.zeros_like(acc_ref)
    top_ref[...] = jnp.full_like(top_ref, negative_fill)
    den_ref[...] = jnp.zeros_like(den_ref)

    def group(s, with_tree):
        start = (s * n_lo + quarter) * block_len
        kt_ref = kslots.at[s]
        v_ref = vslots.at[s]
        pos = start + lax.broadcasted_iota(jnp.int32, (1, block_len), 1)
        bias = jnp.where(pos < length, 0.0, negative_fill)

        def pair(p, carry):
            col = pl.multiple_of(p * 2 * HD, 2 * HD)
            both = q_ref[:, pl.ds(col, 2 * HD)]
            qh = jnp.concatenate([both[:, :HD], both[:, HD:]], axis=0)
            sc = jnp.dot(qh, kt_ref[...], preferred_element_type=jnp.float32) * scale + bias
            peak = jnp.max(sc, axis=1, keepdims=True)
            if with_tree:
                st = jnp.dot(qh, tkt_ref[...], preferred_element_type=jnp.float32) * scale
                tlive = jnp.concatenate([tmask_ref[...], tmask_ref[...]], axis=0) > 0.5
                st = jnp.where(tlive, st, negative_fill)
                peak = jnp.maximum(peak, jnp.max(st, axis=1, keepdims=True))
            w = jnp.exp(sc - jnp.maximum(peak, 0.1 * negative_fill))
            tot = jnp.sum(w, axis=1, keepdims=True)
            gs = jnp.dot(w.astype(jnp.bfloat16), v_ref[...], preferred_element_type=jnp.float32)
            if with_tree:
                wt = jnp.where(tlive, jnp.exp(st - peak), 0.0)
                tot = tot + jnp.sum(wt, axis=1, keepdims=True)
                gs = gs + jnp.dot(
                    wt.astype(jnp.bfloat16), tv_ref[...], preferred_element_type=jnp.float32
                )
            floored = jnp.maximum(tot, 1.0)
            part = gs / floored
            lt = peak + jnp.log(floored)
            for half in range(2):
                h = 2 * p + half
                hcol = pl.multiple_of(h * HD, HD)
                lt_h = lt[half * rows : (half + 1) * rows]
                part_h = part[half * rows : (half + 1) * rows]
                old = top_ref[h][:, :1]
                new = jnp.maximum(old, lt_h)
                keep = jnp.exp(old - new)
                add = jnp.exp(lt_h - new)
                acc_ref[:, pl.ds(hcol, HD)] = keep * acc_ref[:, pl.ds(hcol, HD)] + add * part_h
                den_ref[h] = jnp.broadcast_to(keep * den_ref[h][:, :1] + add, (rows, HD))
                top_ref[h] = jnp.broadcast_to(new, (rows, HD))
            return carry

        lax.fori_loop(0, heads // 2, pair, 0, unroll=4)

    own_k.wait()
    own_v.wait()
    group(request, True)

    def landed(s):
        source = (s, quarter, head_axis)
        return (
            pltpu.make_async_remote_copy(
                kt_hbm.at[s], kslots.at[s], send_sem.at[s, 0], recv_sem.at[s, 0],
                device_id=source, device_id_type=mesh,
            ),
            pltpu.make_async_remote_copy(
                v_hbm.at[s], vslots.at[s], send_sem.at[s, 1], recv_sem.at[s, 1],
                device_id=source, device_id_type=mesh,
            ),
        )

    def arrival(step, carry):
        @pl.when(step + ahead + 1 < n_hi)
        def _():
            t = lax.rem(request + step + ahead + 1, n_hi)
            for copy in pushes(t):
                copy.start()

        s = lax.rem(request - step - 1 + n_hi, n_hi)
        for copy in landed(s):
            copy.wait_recv()
        group(s, False)
        return carry

    lax.fori_loop(0, n_hi - 1, arrival, 0)
    for shift in range(1, n_hi):
        t = lax.rem(request + shift, n_hi)
        for copy in pushes(t):
            copy.wait_send()

    lane = lax.broadcasted_iota(jnp.int32, (rows, HD), 1)
    tops = jnp.full((rows, HD), negative_fill, jnp.float32)
    dens = jnp.zeros((rows, HD), jnp.float32)
    for h in range(heads):
        tops = jnp.where(lane == h, top_ref[h], tops)
        dens = jnp.where(lane == h, den_ref[h], dens)
    stats[0] = tops
    stats[1] = dens

    quarter_rows = rows // n_quarters

    def quarter_copies(r, slot, device):
        piece = pl.ds(r * quarter_rows, quarter_rows)
        return (
            pltpu.make_async_remote_copy(
                acc_ref.at[piece, :], acc_slots.at[slot], fsend.at[r, 0], frecv.at[slot, 0],
                device_id=device, device_id_type=mesh,
            ),
            pltpu.make_async_remote_copy(
                stats.at[:, piece, :], stat_slots.at[slot], fsend.at[r, 1], frecv.at[slot, 1],
                device_id=device, device_id_type=mesh,
            ),
        )

    for r in range(n_quarters):
        for copy in quarter_copies(r, quarter, (request, r, head_axis)):
            pl.when(r != quarter)(copy.start)
    mine = pl.ds(pl.multiple_of(quarter * quarter_rows, quarter_rows), quarter_rows)
    keep_acc = pltpu.make_async_copy(acc_ref.at[mine, :], acc_slots.at[quarter], fown.at[0])
    keep_stat = pltpu.make_async_copy(stats.at[:, mine, :], stat_slots.at[quarter], fown.at[1])
    keep_acc.start()
    keep_stat.start()
    keep_acc.wait()
    keep_stat.wait()
    for r in range(n_quarters):
        for copy in quarter_copies(r, r, (request, r, head_axis)):
            pl.when(r != quarter)(copy.wait_recv)
    for r in range(n_quarters):
        for copy in quarter_copies(r, quarter, (request, r, head_axis)):
            pl.when(r != quarter)(copy.wait_send)
    acc_out[...] = acc_slots[...]
    stat_out[...] = stat_slots[...]


def attend(info, query_block, keys_t, values, tree_keys_t, tree_values, tree_mask, n_quarters):
    rows, width = query_block.shape
    heads = width // HD
    n_hi = keys_t.shape[0]
    quarter_rows = rows // n_quarters
    vmem = pl.BlockSpec(memory_space=pltpu.VMEM)
    hbm = pl.BlockSpec(memory_space=pl.ANY)
    acc_shape = (n_quarters, quarter_rows, width)
    stat_shape = (n_quarters, 2, quarter_rows, HD)
    return pl.pallas_call(
        functools.partial(
            attend_kernel, scale=1.0 / math.sqrt(HD), n_hi=n_hi, n_quarters=n_quarters
        ),
        out_shape=(
            jax.ShapeDtypeStruct(acc_shape, jnp.float32),
            jax.ShapeDtypeStruct(stat_shape, jnp.float32),
        ),
        in_specs=[pl.BlockSpec(memory_space=pltpu.SMEM), vmem, hbm, hbm, vmem, vmem, vmem],
        out_specs=(vmem, vmem),
        scratch_shapes=[
            pltpu.VMEM(keys_t.shape, keys_t.dtype),
            pltpu.VMEM(values.shape, values.dtype),
            pltpu.SemaphoreType.DMA((n_hi, 2)),
            pltpu.SemaphoreType.DMA((n_hi, 2)),
            pltpu.SemaphoreType.DMA((2,)),
            pltpu.VMEM((rows, width), jnp.float32),
            pltpu.VMEM((heads, rows, HD), jnp.float32),
            pltpu.VMEM((heads, rows, HD), jnp.float32),
            pltpu.VMEM((2, rows, HD), jnp.float32),
            pltpu.VMEM(acc_shape, jnp.float32),
            pltpu.VMEM(stat_shape, jnp.float32),
            pltpu.SemaphoreType.DMA((n_quarters, 2)),
            pltpu.SemaphoreType.DMA((n_quarters, 2)),
            pltpu.SemaphoreType.DMA((2,)),
        ],
        compiler_params=pltpu.CompilerParams(
            collective_id=1, has_side_effects=True, vmem_limit_bytes=48 * 1024 * 1024
        ),
    )(info, query_block, keys_t, values, tree_keys_t, tree_values, tree_mask)


def exchange_kernel(src_ref, out_ref, slots, send_sem, recv_sem, own_sem, *, n_lo, n_head):
    request = lax.axis_index("rh")
    quarter = lax.axis_index("rl")
    head = lax.axis_index("head")
    me = quarter * n_head + head
    peers = n_lo * n_head
    mesh = pl.DeviceIdType.MESH

    barrier = pltpu.get_barrier_semaphore()
    for d in range(peers):
        dest = (request, d // n_head, d % n_head)

        @pl.when(d != me)
        def _():
            pl.semaphore_signal(barrier, inc=1, device_id=dest, device_id_type=mesh)

    pl.semaphore_wait(barrier, peers - 1)

    def push(d):
        return pltpu.make_async_remote_copy(
            src_ref.at[d % n_head],
            slots.at[me],
            send_sem.at[d],
            recv_sem.at[me],
            device_id=(request, d // n_head, d % n_head),
            device_id_type=mesh,
        )

    for d in range(peers):
        pl.when(d != me)(push(d).start)
    own = pltpu.make_async_copy(src_ref.at[head], slots.at[me], own_sem)
    own.start()
    own.wait()
    for d in range(peers):
        pl.when(d != me)(push(d).wait_send)
    for s in range(peers):
        arrival = pltpu.make_async_remote_copy(
            src_ref.at[0],
            slots.at[s],
            send_sem.at[s],
            recv_sem.at[s],
            device_id=(request, s // n_head, s % n_head),
            device_id_type=mesh,
        )
        pl.when(s != me)(arrival.wait_recv)
    out_ref[...] = slots[...]


def exchange_queries(pieces, n_lo, n_head):
    peers = n_lo * n_head
    shape = (peers,) + pieces.shape[1:]
    vmem = pl.BlockSpec(memory_space=pltpu.VMEM)
    return pl.pallas_call(
        functools.partial(exchange_kernel, n_lo=n_lo, n_head=n_head),
        out_shape=jax.ShapeDtypeStruct(shape, pieces.dtype),
        in_specs=[vmem],
        out_specs=vmem,
        scratch_shapes=[
            pltpu.VMEM(shape, pieces.dtype),
            pltpu.SemaphoreType.DMA((peers,)),
            pltpu.SemaphoreType.DMA((peers,)),
            pltpu.SemaphoreType.DMA(()),
        ],
        compiler_params=pltpu.CompilerParams(collective_id=0, has_side_effects=True),
    )(pieces)


def body(
    queries, cache_keys, cache_values, tree_keys, tree_values, parents, tree_sizes, cache_lens
):
    group_size = NH // KVH
    softmax_scale = 1.0 / math.sqrt(HD)
    request = lax.axis_index("rh")
    quarter = lax.axis_index("rl")
    n_lo = lax.axis_size("rl")
    n_hi = lax.axis_size("rh")
    cache_block = cache_keys.shape[1]
    kv_local = cache_keys.shape[2] // HD
    heads_local = kv_local * group_size
    node_count = parents.shape[1]
    rows_owned = tree_keys.shape[0]

    n_head = lax.axis_size("head")
    width = queries.shape[1] // n_head
    pieces = queries.reshape(queries.shape[0], n_head, width // HD, HD).transpose(1, 0, 2, 3)
    pieces = pieces.reshape(n_head, queries.shape[0] * width // HD, HD)
    query_block = exchange_queries(pieces, n_lo, n_head)
    query_block = query_block.reshape(node_count, width)

    own_parents = lax.dynamic_slice_in_dim(parents, request, 1, 0)
    ancestors = ancestry(own_parents)[0]
    ancestors = lax.dynamic_slice_in_dim(ancestors, quarter * rows_owned, rows_owned, 1)
    tree_mask = ancestors.astype(jnp.float32)
    length = lax.dynamic_index_in_dim(cache_lens, request, 0, keepdims=False)
    live_size = lax.dynamic_index_in_dim(tree_sizes, request, 0, keepdims=False)
    info = jnp.stack([length, jnp.int32(n_lo)]).astype(jnp.int32)
    keys_t = cache_keys.transpose(0, 2, 1)
    got_acc, got_stats = attend(
        info, query_block, keys_t, cache_values, tree_keys.T, tree_values, tree_mask, n_lo
    )
    got_acc = got_acc.reshape(n_lo, rows_owned, heads_local, HD)
    got_top = got_stats[:, 0, :, :heads_local]
    got_den = got_stats[:, 1, :, :heads_local]
    highest = jnp.max(got_top, axis=0)
    scale = jnp.exp(got_top - highest)
    num = jnp.sum(scale[..., None] * got_acc, axis=0)
    total = jnp.sum(scale * got_den, axis=0)
    merged = (num / total[..., None]).reshape(rows_owned, heads_local * HD)

    row_nodes = quarter * rows_owned + jnp.arange(rows_owned, dtype=jnp.int32)
    live_rows = row_nodes < live_size
    return jnp.where(live_rows[:, None], merged, 0.0).astype(jnp.bfloat16)


def solution(mesh):
    def run(queries, cache_keys, cache_values, tree_keys, tree_values, parents, tree_sizes, cache_lens):
        n_hi = cache_keys.shape[0]
        n_lo = mesh.shape["req"] // n_hi
        split = Mesh(mesh.devices.reshape(n_hi, n_lo, mesh.shape["head"]), ("rh", "rl", "head"))
        rows = ("rh", "rl")
        placed = (
            P(("rh", "rl", "head"), None),
            P(None, rows, "head"),
            P(None, rows, "head"),
            P(rows, "head"),
            P(rows, "head"),
            P(),
            P(),
            P(),
        )
        return jax.shard_map(
            body, mesh=split, in_specs=placed, out_specs=P(rows, "head"), check_vma=False
        )(queries, cache_keys, cache_values, tree_keys, tree_values, parents, tree_sizes, cache_lens)

    return run
```

```python
import functools
import math

import jax
import jax.numpy as jnp
from jax import lax
from jax.experimental import pallas as pl
from jax.experimental.pallas import tpu as pltpu
from jax.sharding import Mesh
from jax.sharding import PartitionSpec as P

NH = 128
KVH = 8
HD = 128


negative_fill = -1e30


def ancestry(parents):
    node_count = parents.shape[1]
    node_ids = jnp.arange(node_count, dtype=jnp.int32)
    linked = jnp.logical_or(
        parents[:, :, None] == node_ids[None, None, :], node_ids[:, None] == node_ids[None, :]
    )
    reached = linked.astype(jnp.bfloat16)
    for doubling in range((node_count - 1).bit_length()):
        squared = jnp.einsum("aij,ajk->aik", reached, reached, preferred_element_type=jnp.float32)
        reached = jnp.minimum(squared, 1.0).astype(jnp.bfloat16)
    return reached


def attend_kernel(
    info_ref, q_ref, kt_hbm, v_hbm, tkt_ref, tv_ref, tmask_ref, acc_out, stat_out,
    kslots, vslots, send_sem, recv_sem, own_sem, acc_ref, top_ref, den_ref, stats,
    acc_slots, stat_slots, fsend, frecv, fown, *, scale, n_hi, n_quarters,
):
    request = lax.axis_index("rh")
    quarter = lax.axis_index("rl")
    head_axis = lax.axis_index("head")
    mesh = pl.DeviceIdType.MESH
    length = info_ref[0]
    n_lo = info_ref[1]
    rows = q_ref.shape[0]
    heads = q_ref.shape[1] // HD
    block_len = kt_hbm.shape[2]

    barrier = pltpu.get_barrier_semaphore()
    for t in range(n_hi):

        @pl.when(t != request)
        def _():
            pl.semaphore_signal(
                barrier, inc=1, device_id=(t, quarter, head_axis), device_id_type=mesh
            )

    for r in range(n_quarters):

        @pl.when(r != quarter)
        def _():
            pl.semaphore_signal(
                barrier, inc=1, device_id=(request, r, head_axis), device_id_type=mesh
            )

    pl.semaphore_wait(barrier, n_hi - 1 + n_quarters - 1)

    def pushes(t):
        dest = (t, quarter, head_axis)
        return (
            pltpu.make_async_remote_copy(
                kt_hbm.at[t], kslots.at[request], send_sem.at[t, 0], recv_sem.at[request, 0],
                device_id=dest, device_id_type=mesh,
            ),
            pltpu.make_async_remote_copy(
                v_hbm.at[t], vslots.at[request], send_sem.at[t, 1], recv_sem.at[request, 1],
                device_id=dest, device_id_type=mesh,
            ),
        )

    ahead = 4
    for shift in range(1, min(ahead, n_hi - 1) + 1):
        t = lax.rem(request + shift, n_hi)
        for copy in pushes(t):
            copy.start()
    own_k = pltpu.make_async_copy(kt_hbm.at[request], kslots.at[request], own_sem.at[0])
    own_v = pltpu.make_async_copy(v_hbm.at[request], vslots.at[request], own_sem.at[1])
    own_k.start()
    own_v.start()

    acc_ref[...] = jnp.zeros_like(acc_ref)
    top_ref[...] = jnp.full_like(top_ref, negative_fill)
    den_ref[...] = jnp.zeros_like(den_ref)

    def group(s, with_tree):
        start = (s * n_lo + quarter) * block_len
        kt_ref = kslots.at[s]
        v_ref = vslots.at[s]
        pos = start + lax.broadcasted_iota(jnp.int32, (1, block_len), 1)
        bias = jnp.where(pos < length, 0.0, negative_fill)

        def pair(p, carry):
            col = pl.multiple_of(p * 2 * HD, 2 * HD)
            both = q_ref[:, pl.ds(col, 2 * HD)]
            qh = jnp.concatenate([both[:, :HD], both[:, HD:]], axis=0)
            sc = jnp.dot(qh, kt_ref[...], preferred_element_type=jnp.float32) * scale + bias
            peak = jnp.max(sc, axis=1, keepdims=True)
            if with_tree:
                st = jnp.dot(qh, tkt_ref[...], preferred_element_type=jnp.float32) * scale
                tlive = jnp.concatenate([tmask_ref[...], tmask_ref[...]], axis=0) > 0.5
                st = jnp.where(tlive, st, negative_fill)
                peak = jnp.maximum(peak, jnp.max(st, axis=1, keepdims=True))
            w = jnp.exp(sc - jnp.maximum(peak, 0.1 * negative_fill))
            tot = jnp.sum(w, axis=1, keepdims=True)
            gs = jnp.dot(w.astype(jnp.bfloat16), v_ref[...], preferred_element_type=jnp.float32)
            if with_tree:
                wt = jnp.where(tlive, jnp.exp(st - peak), 0.0)
                tot = tot + jnp.sum(wt, axis=1, keepdims=True)
                gs = gs + jnp.dot(
                    wt.astype(jnp.bfloat16), tv_ref[...], preferred_element_type=jnp.float32
                )
            floored = jnp.maximum(tot, 1.0)
            part = gs / floored
            lt = peak + jnp.log(floored)
            for half in range(2):
                h = 2 * p + half
                hcol = pl.multiple_of(h * HD, HD)
                lt_h = lt[half * rows : (half + 1) * rows]
                part_h = part[half * rows : (half + 1) * rows]
                old = top_ref[h][:, :1]
                new = jnp.maximum(old, lt_h)
                keep = jnp.exp(old - new)
                add = jnp.exp(lt_h - new)
                acc_ref[:, pl.ds(hcol, HD)] = keep * acc_ref[:, pl.ds(hcol, HD)] + add * part_h
                den_ref[h] = jnp.broadcast_to(keep * den_ref[h][:, :1] + add, (rows, HD))
                top_ref[h] = jnp.broadcast_to(new, (rows, HD))
            return carry

        lax.fori_loop(0, heads // 2, pair, 0, unroll=4)

    own_k.wait()
    own_v.wait()
    group(request, True)

    def landed(s):
        source = (s, quarter, head_axis)
        return (
            pltpu.make_async_remote_copy(
                kt_hbm.at[s], kslots.at[s], send_sem.at[s, 0], recv_sem.at[s, 0],
                device_id=source, device_id_type=mesh,
            ),
            pltpu.make_async_remote_copy(
                v_hbm.at[s], vslots.at[s], send_sem.at[s, 1], recv_sem.at[s, 1],
                device_id=source, device_id_type=mesh,
            ),
        )

    def arrival(step, carry):
        @pl.when(step + ahead + 1 < n_hi)
        def _():
            t = lax.rem(request + step + ahead + 1, n_hi)
            for copy in pushes(t):
                copy.start()

        s = lax.rem(request - step - 1 + n_hi, n_hi)
        for copy in landed(s):
            copy.wait_recv()
        group(s, False)
        return carry

    lax.fori_loop(0, n_hi - 1, arrival, 0)
    for shift in range(1, n_hi):
        t = lax.rem(request + shift, n_hi)
        for copy in pushes(t):
            copy.wait_send()

    lane = lax.broadcasted_iota(jnp.int32, (rows, HD), 1)
    tops = jnp.full((rows, HD), negative_fill, jnp.float32)
    dens = jnp.zeros((rows, HD), jnp.float32)
    for h in range(heads):
        tops = jnp.where(lane == h, top_ref[h], tops)
        dens = jnp.where(lane == h, den_ref[h], dens)
    stats[0] = tops
    stats[1] = dens

    quarter_rows = rows // n_quarters

    def quarter_copies(r, slot, device):
        piece = pl.ds(r * quarter_rows, quarter_rows)
        return (
            pltpu.make_async_remote_copy(
                acc_ref.at[piece, :], acc_slots.at[slot], fsend.at[r, 0], frecv.at[slot, 0],
                device_id=device, device_id_type=mesh,
            ),
            pltpu.make_async_remote_copy(
                stats.at[:, piece, :], stat_slots.at[slot], fsend.at[r, 1], frecv.at[slot, 1],
                device_id=device, device_id_type=mesh,
            ),
        )

    for r in range(n_quarters):
        for copy in quarter_copies(r, quarter, (request, r, head_axis)):
            pl.when(r != quarter)(copy.start)
    mine = pl.ds(pl.multiple_of(quarter * quarter_rows, quarter_rows), quarter_rows)
    keep_acc = pltpu.make_async_copy(acc_ref.at[mine, :], acc_slots.at[quarter], fown.at[0])
    keep_stat = pltpu.make_async_copy(stats.at[:, mine, :], stat_slots.at[quarter], fown.at[1])
    keep_acc.start()
    keep_stat.start()
    keep_acc.wait()
    keep_stat.wait()
    for r in range(n_quarters):
        for copy in quarter_copies(r, r, (request, r, head_axis)):
            pl.when(r != quarter)(copy.wait_recv)
    for r in range(n_quarters):
        for copy in quarter_copies(r, quarter, (request, r, head_axis)):
            pl.when(r != quarter)(copy.wait_send)
    acc_out[...] = acc_slots[...]
    stat_out[...] = stat_slots[...]


def attend(info, query_block, keys_t, values, tree_keys_t, tree_values, tree_mask, n_quarters):
    rows, width = query_block.shape
    heads = width // HD
    n_hi = keys_t.shape[0]
    quarter_rows = rows // n_quarters
    vmem = pl.BlockSpec(memory_space=pltpu.VMEM)
    hbm = pl.BlockSpec(memory_space=pl.ANY)
    acc_shape = (n_quarters, quarter_rows, width)
    stat_shape = (n_quarters, 2, quarter_rows, HD)
    return pl.pallas_call(
        functools.partial(
            attend_kernel, scale=1.0 / math.sqrt(HD), n_hi=n_hi, n_quarters=n_quarters
        ),
        out_shape=(
            jax.ShapeDtypeStruct(acc_shape, jnp.float32),
            jax.ShapeDtypeStruct(stat_shape, jnp.float32),
        ),
        in_specs=[pl.BlockSpec(memory_space=pltpu.SMEM), vmem, hbm, hbm, vmem, vmem, vmem],
        out_specs=(vmem, vmem),
        scratch_shapes=[
            pltpu.VMEM(keys_t.shape, keys_t.dtype),
            pltpu.VMEM(values.shape, values.dtype),
            pltpu.SemaphoreType.DMA((n_hi, 2)),
            pltpu.SemaphoreType.DMA((n_hi, 2)),
            pltpu.SemaphoreType.DMA((2,)),
            pltpu.VMEM((rows, width), jnp.float32),
            pltpu.VMEM((heads, rows, HD), jnp.float32),
            pltpu.VMEM((heads, rows, HD), jnp.float32),
            pltpu.VMEM((2, rows, HD), jnp.float32),
            pltpu.VMEM(acc_shape, jnp.float32),
            pltpu.VMEM(stat_shape, jnp.float32),
            pltpu.SemaphoreType.DMA((n_quarters, 2)),
            pltpu.SemaphoreType.DMA((n_quarters, 2)),
            pltpu.SemaphoreType.DMA((2,)),
        ],
        compiler_params=pltpu.CompilerParams(
            collective_id=1, has_side_effects=True, vmem_limit_bytes=48 * 1024 * 1024
        ),
    )(info, query_block, keys_t, values, tree_keys_t, tree_values, tree_mask)


def exchange_kernel(src_ref, out_ref, slots, send_sem, recv_sem, own_sem, *, n_lo, n_head):
    request = lax.axis_index("rh")
    quarter = lax.axis_index("rl")
    head = lax.axis_index("head")
    me = quarter * n_head + head
    peers = n_lo * n_head
    mesh = pl.DeviceIdType.MESH

    barrier = pltpu.get_barrier_semaphore()
    for d in range(peers):
        dest = (request, d // n_head, d % n_head)

        @pl.when(d != me)
        def _():
            pl.semaphore_signal(barrier, inc=1, device_id=dest, device_id_type=mesh)

    pl.semaphore_wait(barrier, peers - 1)

    def push(d):
        return pltpu.make_async_remote_copy(
            src_ref.at[d % n_head],
            slots.at[me],
            send_sem.at[d],
            recv_sem.at[me],
            device_id=(request, d // n_head, d % n_head),
            device_id_type=mesh,
        )

    for d in range(peers):
        pl.when(d != me)(push(d).start)
    own = pltpu.make_async_copy(src_ref.at[head], slots.at[me], own_sem)
    own.start()
    own.wait()
    for d in range(peers):
        pl.when(d != me)(push(d).wait_send)
    for s in range(peers):
        arrival = pltpu.make_async_remote_copy(
            src_ref.at[0],
            slots.at[s],
            send_sem.at[s],
            recv_sem.at[s],
            device_id=(request, s // n_head, s % n_head),
            device_id_type=mesh,
        )
        pl.when(s != me)(arrival.wait_recv)
    out_ref[...] = slots[...]


def exchange_queries(pieces, n_lo, n_head):
    peers = n_lo * n_head
    shape = (peers,) + pieces.shape[1:]
    vmem = pl.BlockSpec(memory_space=pltpu.VMEM)
    return pl.pallas_call(
        functools.partial(exchange_kernel, n_lo=n_lo, n_head=n_head),
        out_shape=jax.ShapeDtypeStruct(shape, pieces.dtype),
        in_specs=[vmem],
        out_specs=vmem,
        scratch_shapes=[
            pltpu.VMEM(shape, pieces.dtype),
            pltpu.SemaphoreType.DMA((peers,)),
            pltpu.SemaphoreType.DMA((peers,)),
            pltpu.SemaphoreType.DMA(()),
        ],
        compiler_params=pltpu.CompilerParams(collective_id=0, has_side_effects=True),
    )(pieces)


def body(
    queries, cache_keys, cache_values, tree_keys, tree_values, parents, tree_sizes, cache_lens
):
    group_size = NH // KVH
    softmax_scale = 1.0 / math.sqrt(HD)
    request = lax.axis_index("rh")
    quarter = lax.axis_index("rl")
    n_lo = lax.axis_size("rl")
    n_hi = lax.axis_size("rh")
    cache_block = cache_keys.shape[1]
    kv_local = cache_keys.shape[2] // HD
    heads_local = kv_local * group_size
    node_count = parents.shape[1]
    rows_owned = tree_keys.shape[0]

    n_head = lax.axis_size("head")
    width = queries.shape[1] // n_head
    pieces = queries.reshape(queries.shape[0], n_head, width // HD, HD).transpose(1, 0, 2, 3)
    pieces = pieces.reshape(n_head, queries.shape[0] * width // HD, HD)
    query_block = exchange_queries(pieces, n_lo, n_head)
    query_block = query_block.reshape(node_count, width)

    own_parents = lax.dynamic_slice_in_dim(parents, request, 1, 0)
    ancestors = ancestry(own_parents)[0]
    ancestors = lax.dynamic_slice_in_dim(ancestors, quarter * rows_owned, rows_owned, 1)
    tree_mask = ancestors.astype(jnp.float32)
    length = lax.dynamic_index_in_dim(cache_lens, request, 0, keepdims=False)
    live_size = lax.dynamic_index_in_dim(tree_sizes, request, 0, keepdims=False)
    info = jnp.stack([length, jnp.int32(n_lo)]).astype(jnp.int32)
    keys_t = cache_keys.transpose(0, 2, 1)
    got_acc, got_stats = attend(
        info, query_block, keys_t, cache_values, tree_keys.T, tree_values, tree_mask, n_lo
    )
    got_acc = got_acc.reshape(n_lo, rows_owned, heads_local, HD)
    got_top = got_stats[:, 0, :, :heads_local]
    got_den = got_stats[:, 1, :, :heads_local]
    highest = jnp.max(got_top, axis=0)
    scale = jnp.exp(got_top - highest)
    num = jnp.sum(scale[..., None] * got_acc, axis=0)
    total = jnp.sum(scale * got_den, axis=0)
    merged = (num / total[..., None]).reshape(rows_owned, heads_local * HD)

    row_nodes = quarter * rows_owned + jnp.arange(rows_owned, dtype=jnp.int32)
    live_rows = row_nodes < live_size
    return jnp.where(live_rows[:, None], merged, 0.0).astype(jnp.bfloat16)


def solution(mesh):
    def run(queries, cache_keys, cache_values, tree_keys, tree_values, parents, tree_sizes, cache_lens):
        n_hi = cache_keys.shape[0]
        n_lo = mesh.shape["req"] // n_hi
        split = Mesh(mesh.devices.reshape(n_hi, n_lo, mesh.shape["head"]), ("rh", "rl", "head"))
        rows = ("rh", "rl")
        placed = (
            P(("rh", "rl", "head"), None),
            P(None, rows, "head"),
            P(None, rows, "head"),
            P(rows, "head"),
            P(rows, "head"),
            P(),
            P(),
            P(),
        )
        return jax.shard_map(
            body, mesh=split, in_specs=placed, out_specs=P(rows, "head"), check_vma=False
        )(queries, cache_keys, cache_values, tree_keys, tree_values, parents, tree_sizes, cache_lens)

    return run
```
